128 devices in a mesh: sess: 2 (over core), elem: 64 (over x, y, z).
Axes of the slice: x: 4, y: 4, z: 4, core: 2. Of those that a mesh axis runs over, the one named last changes fastest.
Arguments:
- pressure: float32 [2, 8, 8, 8, 8192], P('sess', None, None, None, 'elem'), may hold values from -6 to 6
- load: float32 [2, 8, 8, 8, 8192], P('sess', None, None, None, 'elem'), may hold values from -6 to 6
- stiffness: float32 [2, 3, 8, 8, 8, 8192], P('sess', None, None, None, None, 'elem'), may hold values from 0.02 to 0.2
- helm_mass: float32 [2, 8, 8, 8, 8192], P('sess', None, None, None, 'elem'), may hold values from 0.05 to 0.5
- order_slots: int32 [2, 64, 128], P('sess', 'elem'), may hold values from 0 to 127, each once within a row
- recv_ids: int32 [2, 65536], P('sess', 'elem'), may hold values from 0 to 65535, as said below
- donor_owner: int32 [2, 65536, 1], P('sess', 'elem'), may hold values from 0 to 63; in each aligned block of 1024 rows (0 to 1023, 1024 to 2047, ..., all dimensions but the last counted through in order) at most 24 rows name the same one
- donor_slot: int32 [2, 65536], P('sess', 'elem'), may hold values from 0 to 127
- interp_weights: float32 [2, 24, 65536], P('sess', None, 'elem'), may hold values from -5 to 5
- live_count: int32 [2, 64], P('sess', 'elem'), may hold values from 1 to 1024, 49152 in all within a row
- coarse_basis: float32 [2, 8192, 512], P('sess', 'elem'), may hold values from -0.0625 to 0.0625
- coarse_inverse: float32 [2, 512, 512], P('sess'), may hold values from -0.25 to 0.25
Outputs:
- smoothed: float32 [2, 8, 8, 8, 8192], P('sess', None, None, None, 'elem')
The draws below stay inside these ranges and needn't reach their ends.
Inputs may be any that keep to these rules, and one draw needn't show every extreme that they name: `recv_ids`: the receiver points of one device are distinct nodes of its block. `donor_owner`: at most 24 receivers of one device name the same owner. `order_slots`: each slab's entries are a permutation of its grid positions.
All inputs are finite; a program needn't handle non-finite values. No bound on the sum of `live_count` on one device may be relied on, other than what follows from the above.
Results may differ from the reference program's by a relative error of at most 0.0002.
Values sent between devices are 32-bit elements; how exact they have to be, the bound alone decides.
No kernel may reach another device: no remote copies, remote signals or barrier semaphores. Data moves between devices by JAX's collectives and lax.ppermute only.
A program may use at most 256 MiB of HBM per device.

```python
import math
import jax
import jax.numpy as jnp
import numpy as np
from jax import lax

NP = 8
EX = 8
EY = 8
R_DEV = 1024
NC = 512
CHEB = 4
SESSIONS = 2
E_DEV = 128
EBLOCKS = 64
ELEM_SESS = 8192
R_TOT = 65536
CAP = 24


def permute_block(block_key):
    return jax.random.permutation(block_key, R_DEV)


def draw_recv_ids(key, part):
    stride = NP ** 3 * E_DEV // R_DEV
    key_order = jax.random.fold_in(key, 11)
    key_offset = jax.random.fold_in(key, 12)
    block_keys = jax.random.split(key_order, SESSIONS * EBLOCKS)
    orders = jax.vmap(permute_block)(block_keys).astype(jnp.int32)
    offsets = jax.random.randint(key_offset, (SESSIONS * EBLOCKS, R_DEV), 0, stride).astype(jnp.int32)
    offsets = jnp.where(orders == R_DEV - 1, stride - 1, offsets)
    node_ids = orders * stride + offsets
    return node_ids.reshape(SESSIONS, R_TOT).astype(jnp.int32)


def place_ends(values, own_key, low, largest):
    shape = values.shape
    spot = [jax.random.randint(jax.random.fold_in(own_key, axis), (), 0, shape[axis]) for axis in range(len(shape))]
    values = values.at[tuple(spot)].set(low)
    longest = shape.index(max(shape))
    spot[longest] = (spot[longest] + 1) % shape[longest]
    return values.at[tuple(spot)].set(largest)


def block_levels(stream_key, dims, cuts, least, high):
    gain = 1.0
    for dim, shards_of in cuts:
        draws = jax.random.uniform(jax.random.fold_in(jax.random.fold_in(stream_key, 6), dim), (shards_of,), jnp.float32, least / len(cuts), high / len(cuts))
        gain = gain * jnp.repeat(jnp.exp(draws), dims[dim] // shards_of).reshape((-1,) + (1,) * (len(dims) - 1 - dim))
    return gain


def profile(amount, total, limit, skew):
    weights = [(1 << 20) // math.isqrt(rank ** skew) + 1 for rank in range(2, amount + 1)]
    surplus, given = total - limit - (amount - 1), [1] * (amount - 1)
    while surplus > 0:
        candidates = [i for i in range(amount - 1) if given[i] < limit]
        whole, remaining = sum([weights[i] for i in candidates]), surplus
        for i in candidates:
            more = min(limit - given[i], max(1, remaining * weights[i] // whole), surplus)
            given[i] = given[i] + more
            surplus = surplus - more
    return np.array([limit] + given)


def uneven(key, number_of, total, reach, slope):
    if number_of == 2:
        one = jax.random.randint(key, (), max(1, total - reach), min(reach, total - 1) + 1)
        return jnp.stack([one, total - one])
    lengths = jnp.asarray(profile(number_of, total, reach, slope), jnp.int32)
    pairs = (number_of - 1) // 2
    source_of, receiver = lengths[1:1 + 2 * pairs:2], lengths[2:2 + 2 * pairs:2]
    room = jnp.minimum(source_of - 1, reach - receiver)
    shifted = jax.random.randint(jax.random.fold_in(key, 1), (pairs,), 0, 1 << 20) % (room + 1)
    lengths = lengths.at[1:1 + 2 * pairs:2].set(source_of - shifted).at[2:2 + 2 * pairs:2].set(receiver + shifted)
    return lengths[jax.random.permutation(jax.random.fold_in(key, 2), number_of)]


def routed_block(key, own, number, rows, amount, top, limit, slope):
    sequence = jax.random.permutation(key, amount)
    crowded, common = portions_of(amount, rows * top, limit, slope, True), portions_of(amount, rows * top, limit, slope, False)
    places = jnp.arange(amount)

    def named(lengths, offset_by):
        used = int((lengths > 0).sum())
        fixed = max(1, used // 4)
        passed = fixed + (places - fixed + offset_by * (used - fixed)) % max(1, amount - fixed)
        return jnp.zeros((amount,), jnp.int32).at[sequence[jnp.where(places < fixed, places, passed)]].set(jnp.asarray(lengths, jnp.int32))

    lengths = jnp.where(number % 4 == 0, named(crowded, number // 4), named(common, number - number // 4 - 1))
    mixed = jax.random.permutation(jax.random.fold_in(own, 3), amount)
    source_of, taker = mixed[0:amount // 2 * 2:2], mixed[1:amount // 2 * 2:2]
    slack = jnp.minimum(lengths[source_of] - 1, limit - lengths[taker]) // 2
    slack = jnp.where((source_of == sequence[0]) | (taker == sequence[0]) | (lengths[taker] == 0), 0, jnp.maximum(slack, 0))
    passed = jax.random.randint(jax.random.fold_in(own, 4), (amount // 2,), 0, 1 << 20) % (slack + 1)
    lengths = lengths.at[source_of].add(-passed).at[taker].add(passed)
    members = jnp.searchsorted(jnp.cumsum(lengths), jnp.arange(rows * top), side="right").astype(jnp.int32)
    table = members.reshape(top, rows).T
    table = table[jax.random.permutation(jax.random.fold_in(own, 1), rows)]
    offset_by = jax.random.randint(jax.random.fold_in(own, 2), (rows, 1), 0, top)
    return jnp.take_along_axis(table, (jnp.arange(top)[None, :] + offset_by) % top, axis=1)


def portions_of(number_of, total, limit, skew, full):
    weights = [(1 << 20) // math.isqrt(grade ** skew) + 1 for grade in range(1, number_of + 1)]
    largest = limit if full else min(limit, max(-(-total // number_of), total * weights[0] // sum(weights)))
    least = 1 if total - largest >= number_of - 1 else 0
    given, rest = [largest] + [least] * (number_of - 1), total - largest - least * (number_of - 1)
    while rest > 0:
        free = [i for i in range(1, number_of) if given[i] < largest] or [i for i in range(1, number_of) if given[i] < limit]
        mass, remaining = sum([weights[i] for i in free]), rest
        for i in free:
            addition = min(limit - given[i], max(1, remaining * weights[i] // mass), rest)
            given[i] = given[i] + addition
            rest = rest - addition
    return np.array(given)


def noise(stream_key, extent, width, bound, cuts=(), kind=jnp.bfloat16):
    factor_of = block_levels(stream_key, extent, cuts, -0.22, 0.18) if cuts else 1.0
    entries = jax.random.normal(stream_key, extent, jnp.float32) * width * factor_of
    return jnp.minimum(jnp.maximum(entries, -bound), bound).astype(kind)


def setup_inputs(seed: int = 0) -> dict:
    splits = jax.random.split(jax.random.key(seed), 13)
    pressure = noise(splits[0], (SESSIONS, NP, NP, NP, ELEM_SESS), 1.0, 6.0, ((0, 2), (4, 64)), jnp.float32)
    load = noise(splits[1], (SESSIONS, NP, NP, NP, ELEM_SESS), 1.0, 6.0, ((0, 2), (4, 64)), jnp.float32)
    stiffness = jnp.clip(jnp.exp(math.log(0.2) - 2.3025851 * jax.random.uniform(splits[2], (SESSIONS, 3, NP, NP, NP, ELEM_SESS), jnp.float32) ** block_levels(splits[2], (SESSIONS, 3, NP, NP, NP, ELEM_SESS), ((0, 2), (5, 64)), -0.2, 0.2)), 0.02, 0.2)
    helm_mass = jnp.clip(jnp.exp(math.log(0.5) - 2.3025851 * jax.random.uniform(splits[3], (SESSIONS, NP, NP, NP, ELEM_SESS), jnp.float32) ** block_levels(splits[3], (SESSIONS, NP, NP, NP, ELEM_SESS), ((0, 2), (4, 64)), -0.2, 0.2)), 0.05, 0.5)
    order_slots = jax.vmap(lambda own: jax.random.permutation(own, E_DEV))(jax.random.split(splits[4], SESSIONS * EBLOCKS)).reshape((SESSIONS, EBLOCKS, E_DEV)).astype(jnp.int32)
    recv_ids = draw_recv_ids(jax.random.fold_in(splits[12], 71), 0)
    donor_owner_keys = jax.random.split(jax.random.fold_in(splits[6], 1), SESSIONS * R_TOT // R_DEV)
    donor_owner_turns = jax.random.permutation(jax.random.fold_in(splits[6], 3), SESSIONS * R_TOT // R_DEV)
    donor_owner = jax.vmap(lambda own, number: routed_block(jax.random.fold_in(splits[6], 2), own, number, R_DEV, EBLOCKS, 1, CAP, 2))(donor_owner_keys, donor_owner_turns).reshape((SESSIONS, R_TOT, 1))
    donor_slot = place_ends(jax.random.randint(splits[7], (SESSIONS, R_TOT), 0, E_DEV), jax.random.fold_in(splits[7], 1), 0, E_DEV - 1).astype(jnp.int32)
    interp_weights = noise(splits[8], (SESSIONS, 3 * NP, R_TOT), 0.35, 5.0, ((0, 2), (2, 64)), jnp.float32)
    live_count = jax.vmap(lambda own: uneven(own, EBLOCKS, EBLOCKS * R_DEV * 3 // 4, R_DEV, 2))(jax.random.split(splits[9], SESSIONS)).reshape((SESSIONS, EBLOCKS)).astype(jnp.int32)
    coarse_basis = noise(splits[10], (SESSIONS, ELEM_SESS, NC), ELEM_SESS ** -0.5, 0.0625, ((0, 2), (1, 64)), jnp.float32)
    coarse_inverse = noise(splits[11], (SESSIONS, NC, NC), NC ** -0.5, 0.25, ((0, 2),), jnp.float32)
    return {"pressure": pressure, "load": load, "stiffness": stiffness, "helm_mass": helm_mass, "order_slots": order_slots, "recv_ids": recv_ids, "donor_owner": donor_owner, "donor_slot": donor_slot, "interp_weights": interp_weights, "live_count": live_count, "coarse_basis": coarse_basis, "coarse_inverse": coarse_inverse}


exact_mode = lax.Precision.HIGHEST
spectrum_high = 8.0
spectrum_low = 0.8

def gll_derivative():
    gll_points = np.array([-1.0, -0.8717401485096066, -0.5917001814331423, -0.2092992179024789, 0.2092992179024789, 0.5917001814331423, 0.8717401485096066, 1.0])
    legendre = (429.0 * gll_points ** 7 - 693.0 * gll_points ** 5 + 315.0 * gll_points ** 3 - 35.0 * gll_points) / 16.0
    distance = gll_points[:, None] - gll_points[None, :]
    same_point = np.eye(8, dtype=bool)
    distance = np.where(same_point, 1.0, distance)
    deriv_table = legendre[:, None] / (legendre[None, :] * distance)
    corner_values = np.zeros((8, 8))
    corner_values[0, 0] = -14.0
    corner_values[7, 7] = 14.0
    deriv_table = np.where(same_point, corner_values, deriv_table)
    return jnp.asarray(deriv_table, jnp.float32)

def couple(high_face, low_face, stride, below_high, above_low, valid_next, valid_prev):
    next_low = jnp.concatenate([low_face[..., stride:], above_low], axis=-1)
    prev_high = jnp.concatenate([below_high, high_face[..., :-stride]], axis=-1)
    new_high = high_face + jnp.where(valid_next, next_low, 0.0)
    new_low = low_face + jnp.where(valid_prev, prev_high, 0.0)
    return (new_high, new_low)

def in_plane(field):
    last = NP - 1
    count = field.shape[-1]
    position = jnp.arange(count, dtype=jnp.int32)
    column_pos = position % EX
    row_pos = position // EX % EY
    high_face = field[:, :, last, :]
    low_face = field[:, :, 0, :]
    zero_one = jnp.zeros(high_face.shape[:-1] + (1,), field.dtype)
    new_high, new_low = couple(high_face, low_face, 1, zero_one, zero_one, column_pos < EX - 1, column_pos > 0)
    field = field.at[:, :, last, :].set(new_high).at[:, :, 0, :].set(new_low)
    high_face = field[:, last, :, :]
    low_face = field[:, 0, :, :]
    zero_row = jnp.zeros(high_face.shape[:-1] + (EX,), field.dtype)
    new_high, new_low = couple(high_face, low_face, EX, zero_row, zero_row, row_pos < EY - 1, row_pos > 0)
    return field.at[:, last, :, :].set(new_high).at[:, 0, :, :].set(new_low)

def through_layers(field, below_high, above_low):
    last = NP - 1
    new_high, new_low = couple(field[last], field[0], EX * EY, below_high, above_low, True, True)
    return field.at[last].set(new_high).at[0].set(new_low)

def assemble(field):
    field = in_plane(field)
    zero_plane = jnp.zeros((NP, NP, EX * EY), field.dtype)
    return through_layers(field, zero_plane, zero_plane)

def local_stiffness(field, stiffness, helm_mass, deriv_table):
    grad_x = jnp.einsum('ai,kjie->kjae', deriv_table, field, precision=exact_mode)
    grad_y = jnp.einsum('bj,kjie->kbie', deriv_table, field, precision=exact_mode)
    grad_z = jnp.einsum('ck,kjie->cjie', deriv_table, field, precision=exact_mode)
    result = jnp.einsum('ai,kjae->kjie', deriv_table, stiffness[0] * grad_x, precision=exact_mode)
    result = result + jnp.einsum('bj,kbie->kjie', deriv_table, stiffness[1] * grad_y, precision=exact_mode)
    result = result + jnp.einsum('ck,cjie->kjie', deriv_table, stiffness[2] * grad_z, precision=exact_mode)
    return result + helm_mass * field

def local_diagonal(stiffness, helm_mass, deriv_table):
    squared = deriv_table * deriv_table
    result = jnp.einsum('ai,kjae->kjie', squared, stiffness[0], precision=exact_mode)
    result = result + jnp.einsum('bj,kbie->kjie', squared, stiffness[1], precision=exact_mode)
    result = result + jnp.einsum('ck,cjie->kjie', squared, stiffness[2], precision=exact_mode)
    return result + helm_mass

def contract(gathered, weights):
    partial_x = jnp.einsum('kjir,ir->kjr', gathered, weights[0:NP], precision=exact_mode)
    partial_y = jnp.einsum('kjr,jr->kr', partial_x, weights[NP:2 * NP], precision=exact_mode)
    return lax.optimization_barrier(jnp.sum(partial_y * weights[2 * NP:3 * NP], axis=0))

def smooth(start, rhs, inv_diag, operator):
    center = 0.5 * (spectrum_high + spectrum_low)
    half_width = 0.5 * (spectrum_high - spectrum_low)
    sigma_ratio = center / half_width
    rho_now = 1.0 / sigma_ratio
    residual = rhs - operator(start)
    update = inv_diag * residual / center
    current = start
    for turn in range(CHEB):
        current = current + update
        if turn < CHEB - 1:
            residual = residual - operator(update)
            rho_next = 1.0 / (2.0 * sigma_ratio - rho_now)
            update = rho_next * rho_now * update + 2.0 * rho_next / half_width * inv_diag * residual
            rho_now = rho_next
    return current

def add_block(row_values, row_ids, row_terms):
    return row_values.at[row_ids].add(row_terms)

def reference(pressure, load, stiffness, helm_mass, order_slots, recv_ids, donor_owner, donor_slot, interp_weights, live_count, coarse_basis, coarse_inverse):
    deriv_table = gll_derivative()
    results = []
    for session in range(2):
        other_field = pressure[1 - session]
        grid_of = (jnp.arange(EBLOCKS, dtype=jnp.int32)[:, None] * E_DEV + order_slots[session]).reshape(-1).astype(jnp.int32)

        def to_grid(values):
            return jnp.zeros_like(values).at[..., grid_of].set(values)
        columns = (donor_owner[session, :, 0] * E_DEV + donor_slot[session]).reshape(EBLOCKS, R_DEV).astype(jnp.int32)
        weight_blocks = interp_weights[session].reshape(3 * NP, EBLOCKS, R_DEV).transpose(1, 0, 2)

        def one_block(pair):
            block_cols, block_weights = pair
            return contract(other_field[..., block_cols], block_weights)
        values = lax.map(one_block, (columns, weight_blocks))
        live_mask = (jnp.arange(R_DEV, dtype=jnp.int32)[None, :] < live_count[session][:, None]).astype(jnp.float32)
        blocks_flat = load[session].reshape(NP ** 3, EBLOCKS, E_DEV).transpose(1, 0, 2).reshape(EBLOCKS, NP ** 3 * E_DEV)
        blocks_flat = jax.vmap(add_block)(blocks_flat, recv_ids[session].reshape(EBLOCKS, R_DEV), values * live_mask)
        source = blocks_flat.reshape(EBLOCKS, NP ** 3, E_DEV).transpose(1, 0, 2).reshape(NP, NP, NP, ELEM_SESS)
        coef_grid = to_grid(stiffness[session])
        mass_grid = to_grid(helm_mass[session])

        def operator(field):
            return assemble(local_stiffness(field, coef_grid, mass_grid, deriv_table))
        rhs = assemble(to_grid(source))
        inv_diag = 1.0 / assemble(local_diagonal(coef_grid, mass_grid, deriv_table))
        first = smooth(to_grid(pressure[session]), rhs, inv_diag, operator)
        residual = rhs - operator(first)
        elem_sums = lax.optimization_barrier(jnp.sum(residual, axis=(0, 1, 2))) / math.sqrt(NP ** 3)
        coarse = jnp.dot(elem_sums[grid_of], coarse_basis[session], precision=exact_mode)
        solved = jnp.dot(coarse_inverse[session], coarse, precision=exact_mode)
        correction = jnp.dot(coarse_basis[session], solved, precision=exact_mode)
        corrected = first + to_grid(correction)[None, None, None, :]
        final = smooth(corrected, rhs, inv_diag, operator)
        results.append(final[..., grid_of])
    return jnp.stack(results)
```

```python
import functools
import math

import jax
import jax.numpy as jnp
import numpy as np
from jax import lax
from jax.experimental import pallas as pl
from jax.experimental.pallas import tpu as pltpu
from jax.sharding import PartitionSpec as P

NP = 8
EX = 8
EY = 8
LAYER = EX * EY
NODES = NP**3
R_DEV = 1024
NC = 512
CHEB = 4
OWNERS = 64
COMPS = 32
HALF = 12

exact_mode = lax.Precision.HIGHEST
spectrum_high = 8.0
spectrum_low = 0.8
f32 = jnp.float32
bf16 = jnp.bfloat16


def gll_derivative():
    x = np.array(
        [
            -1.0,
            -0.8717401485096066,
            -0.5917001814331423,
            -0.2092992179024789,
            0.2092992179024789,
            0.5917001814331423,
            0.8717401485096066,
            1.0,
        ]
    )
    legendre = (429.0 * x**7 - 693.0 * x**5 + 315.0 * x**3 - 35.0 * x) / 16.0
    distance = x[:, None] - x[None, :]
    same = np.eye(8, dtype=bool)
    table = legendre[:, None] / (legendre[None, :] * np.where(same, 1.0, distance))
    corner = np.zeros((8, 8))
    corner[0, 0] = -14.0
    corner[7, 7] = 14.0
    return np.where(same, corner, table).astype(np.float32).astype(np.float64)


DERIV = gll_derivative()


def chebyshev():
    center = 0.5 * (spectrum_high + spectrum_low)
    half_width = 0.5 * (spectrum_high - spectrum_low)
    sigma_ratio = center / half_width
    rho = 1.0 / sigma_ratio
    steps = [(0.0, 1.0 / center)]
    for _ in range(CHEB - 1):
        rho_next = 1.0 / (2.0 * sigma_ratio - rho)
        steps.append((rho_next * rho, 2.0 * rho_next / half_width))
        rho = rho_next
    return steps


STEPS = chebyshev()


def split3(x):
    hi = x.astype(bf16)
    rest = x - hi.astype(f32)
    mid = rest.astype(bf16)
    low = (rest - mid.astype(f32)).astype(bf16)
    return hi, mid, low


def dot_nn(a, b, precision=None):
    return lax.dot_general(
        a, b, (((1,), (0,)), ((), ())), precision=precision, preferred_element_type=f32
    )


def dot_nt(a, b, precision=None):
    return lax.dot_general(
        a, b, (((1,), (1,)), ((), ())), precision=precision, preferred_element_type=f32
    )


def iota(shape, axis):
    return lax.broadcasted_iota(jnp.int32, shape, axis)


def request_kernel(owner_ref, slot_ref, weight_ref, send_ref, rank_ref):
    owner = owner_ref[...]
    hits = iota((OWNERS, R_DEV), 0) == owner
    hits_f = hits.astype(f32)
    hits_b = hits_f.astype(bf16)
    upper = (iota((128, 128), 0) < iota((128, 128), 1)).astype(f32).astype(bf16)
    carry = jnp.zeros((OWNERS, 1), f32)
    ranks = []
    for b in range(R_DEV // 128):
        cols = slice(b * 128, b * 128 + 128)
        block = hits_f[:, cols]
        count = dot_nn(hits_b[:, cols], upper) + carry
        ranks.append(jnp.sum(block * count, axis=0, keepdims=True))
        carry = carry + jnp.sum(block, axis=1, keepdims=True)
    rank = jnp.concatenate(ranks, axis=1)
    rank_ref[...] = rank
    payload = jnp.concatenate(
        [
            weight_ref[...],
            jnp.broadcast_to(slot_ref[...].astype(f32), (COMPS - 3 * NP, R_DEV)),
        ],
        axis=0,
    )
    pieces = split3(payload)
    total = None
    for piece in pieces:
        rows = [
            piece * (rank == float(m)).astype(f32).astype(bf16) for m in range(2 * HALF)
        ]
        part = dot_nt(hits_b, jnp.concatenate(rows, axis=0))
        total = part if total is None else total + part
    send_ref[...] = total


def owner_kernel(recv_ref, field_ref, ret_ref):
    width = HALF * COMPS
    packed = jnp.concatenate([recv_ref[:, :width], recv_ref[:, width:]], axis=0)
    comps = packed.T
    pieces = jnp.concatenate(split3(field_ref[...]), axis=1)
    rows = []
    for pair in range(HALF // 2):
        a = comps[(2 * pair) * COMPS : (2 * pair + 1) * COMPS]
        b = comps[(2 * pair + 1) * COMPS : (2 * pair + 2) * COMPS]
        both = jnp.concatenate([a, b], axis=1)
        slot = both[3 * NP : 3 * NP + 1].astype(jnp.int32)
        pick = (iota((128, 256), 0) == slot).astype(f32).astype(bf16)
        gathered = dot_nn(pieces, jnp.concatenate([pick, pick, pick], axis=0))
        wx = both[0:NP]
        wy = both[NP : 2 * NP]
        wz = both[2 * NP : 3 * NP]
        acc = None
        for k in range(NP):
            line = None
            for j in range(NP):
                row = (k * NP + j) * NP
                term = gathered[row : row + NP] * wy[j : j + 1]
                line = term if line is None else line + term
            line = line * wz[k : k + 1]
            acc = line if acc is None else acc + line
        value = jnp.sum(acc * wx, axis=0, keepdims=True)
        rows.append(value[:, :128])
        rows.append(value[:, 128:])
    rows.append(jnp.zeros((128 - HALF, 128), f32))
    turned = jnp.concatenate(rows, axis=0).T
    ret_ref[...] = turned[:OWNERS] + pltpu.roll(turned[OWNERS:], 16, 1)


def deriv8(table, v):
    plus = [v[m] + v[7 - m] for m in range(4)]
    minus = [v[m] - v[7 - m] for m in range(4)]
    out = [None] * 8
    for a in range(4):
        even = odd = None
        for m in range(4):
            ce = 0.5 * (table[a, m] + table[a, 7 - m])
            co = 0.5 * (table[a, m] - table[a, 7 - m])
            te = plus[m] * float(ce)
            to = minus[m] * float(co)
            even = te if even is None else even + te
            odd = to if odd is None else odd + to
        out[a] = odd + even
        out[7 - a] = odd - even
    return out


def apply_line(v, coef):
    grad = deriv8(DERIV, v)
    return deriv8(DERIV.T, [grad[a] * coef(a) for a in range(8)])


def stiff_apply(v_ref, coef_ref, mass_ref, out_ref):
    def per_k(k, carry):
        base = pl.multiple_of(k * 64, 64)
        lines = [v_ref[pl.ds(base + i, 8, stride=8), :] for i in range(8)]
        res = apply_line(lines, lambda a: coef_ref[pl.ds(base + a * 8, 8), :])
        for i in range(8):
            out_ref[pl.ds(base + i, 8, stride=8), :] = res[i]
        rows = [v_ref[pl.ds(base + j * 8, 8), :] for j in range(8)]
        res = apply_line(rows, lambda b: coef_ref[pl.ds(512 + base + b * 8, 8), :])
        for j in range(8):
            at = pl.ds(base + j * 8, 8)
            out_ref[at, :] = out_ref[at, :] + res[j] + mass_ref[at, :] * rows[j]
        return carry

    lax.fori_loop(0, 8, per_k, 0)

    def per_j(j, carry):
        base = pl.multiple_of(j * 8, 8)
        cols = [v_ref[pl.ds(base + k * 64, 8), :] for k in range(8)]
        res = apply_line(cols, lambda c: coef_ref[pl.ds(1024 + base + c * 64, 8), :])
        for k in range(8):
            at = pl.ds(base + k * 64, 8)
            out_ref[at, :] = out_ref[at, :] + res[k]
        return carry

    lax.fori_loop(0, 8, per_j, 0)


def couple(high, low, shift, pos, count):
    lanes = high.shape[-1]
    next_low = pltpu.roll(low, lanes - shift, high.ndim - 1)
    prev_high = pltpu.roll(high, shift, high.ndim - 1)
    new_high = high + jnp.where(pos < count - 1, next_low, 0.0)
    new_low = low + jnp.where(pos > 0, prev_high, 0.0)
    return new_high, new_low


def in_plane(ref, count=NP):
    rows = count * NP
    col = iota((rows, 128), 1) % EX
    high, low = couple(
        ref[pl.ds(7, rows, stride=8), :], ref[pl.ds(0, rows, stride=8), :], 1, col, EX
    )
    ref[pl.ds(7, rows, stride=8), :] = high
    ref[pl.ds(0, rows, stride=8), :] = low
    line = (iota((8, 128), 1) // EX) % EY
    for k in range(count):
        high, low = couple(
            ref[k * 64 + 56 : k * 64 + 64], ref[k * 64 : k * 64 + 8], EX, line, EY
        )
        ref[k * 64 + 56 : k * 64 + 64] = high
        ref[k * 64 : k * 64 + 8] = low


def through(bottom, top, below, above):
    first = iota(bottom.shape, 1) < LAYER
    new_bottom = bottom + pltpu.roll(jnp.where(first, top, below), LAYER, 1)
    new_top = top + pltpu.roll(jnp.where(first, above, bottom), LAYER, 1)
    return new_bottom, new_top


def plain8(table, v):
    out = []
    for i in range(8):
        total = None
        for a in range(8):
            if table[a, i] == 0.0:
                continue
            term = v[a] * float(table[a, i])
            total = term if total is None else total + term
        out.append(total)
    return out


def take_lanes(x, index):
    return jnp.take_along_axis(
        x, jnp.broadcast_to(index, x.shape), axis=1, mode="promise_in_bounds"
    )


def setup_kernel(
    order_ref,
    stiff_ref,
    mass_ref,
    field_ref,
    basis_ref,
    inverse_ref,
    coef_ref,
    mass_out_ref,
    start_ref,
    diag_ref,
    inv_ref,
    basis_out_ref,
    solve_ref,
    pack_up_ref,
    pack_down_ref,
    tmp_ref,
):
    order = order_ref[...]
    match = (iota((128, 128), 0) == order).astype(f32)
    inv = jnp.sum(match.T * iota((128, 128), 0).astype(f32), axis=0, keepdims=True)
    inv = inv.astype(jnp.int32)
    inv_ref[...] = inv
    tmp_ref[...] = take_lanes(stiff_ref[0:512, :], inv)
    for k in range(8):
        for i in range(8):
            coef_ref[k * 64 + i * 8 : k * 64 + i * 8 + 8, :] = tmp_ref[
                pl.ds(k * 64 + i, 8, stride=8), :
            ]
    coef_ref[512:1536, :] = take_lanes(stiff_ref[512:1536, :], inv)
    mass_out_ref[...] = take_lanes(mass_ref[...], inv)
    start_ref[...] = take_lanes(field_ref[...], inv)
    basis = dot_nn(match, basis_ref[...], exact_mode)
    basis_out_ref[...] = basis
    solve = dot_nn(basis, inverse_ref[...], exact_mode)
    solve_ref[...] = solve
    squared = DERIV * DERIV

    def per_k(k, carry):
        base = pl.multiple_of(k * 64, 64)
        res = plain8(squared, [coef_ref[pl.ds(base + a * 8, 8), :] for a in range(8)])
        for i in range(8):
            diag_ref[pl.ds(base + i, 8, stride=8), :] = res[i]
        res = plain8(squared, [coef_ref[pl.ds(512 + base + b * 8, 8), :] for b in range(8)])
        for j in range(8):
            at = pl.ds(base + j * 8, 8)
            diag_ref[at, :] = diag_ref[at, :] + res[j] + mass_out_ref[at, :]
        return carry

    lax.fori_loop(0, 8, per_k, 0)

    def per_j(j, carry):
        base = pl.multiple_of(j * 8, 8)
        res = plain8(squared, [coef_ref[pl.ds(1024 + base + c * 64, 8), :] for c in range(8)])
        for k in range(8):
            at = pl.ds(base + k * 64, 8)
            diag_ref[at, :] = diag_ref[at, :] + res[k]
        return carry

    lax.fori_loop(0, 8, per_j, 0)
    in_plane(diag_ref)
    pack_up_ref[:, 0:512] = basis[LAYER:]
    pack_up_ref[:, 512:1024] = solve[LAYER:]
    pack_up_ref[:, 1024:1152] = mass_out_ref[448:512, :]
    pack_down_ref[:, 0:512] = basis[:LAYER]
    pack_down_ref[:, 512:1024] = solve[:LAYER]
    pack_down_ref[:, 1024:1152] = mass_out_ref[0:64, :]


def source_kernel(
    ret_ref,
    owner_ref,
    rank_ref,
    ids_ref,
    live_ref,
    load_ref,
    inv_ref,
    start_ref,
    coef_ref,
    mass_ref,
    diag_ref,
    out_ref,
    up_ref,
    down_ref,
):
    hits = (iota((OWNERS, R_DEV), 0) == owner_ref[...]).astype(f32)
    picked = dot_nn(ret_ref[...].T, hits, exact_mode)[0:32]
    rank = rank_ref[...].astype(jnp.int32)
    place = rank + jnp.where(rank >= HALF, 16 - HALF, 0)
    value = jnp.sum(
        jnp.where(iota((32, R_DEV), 0) == place, picked, 0.0), axis=0, keepdims=True
    )
    value = jnp.where(iota((1, R_DEV), 1) < live_ref[0, 0], value, 0.0)
    ids = ids_ref[...]
    node = lax.shift_right_logical(ids, 7)
    elem = jnp.bitwise_and(ids, 127)
    at_node = (iota((NODES, R_DEV), 0) == node).astype(f32).astype(bf16)
    at_elem = (iota((128, R_DEV), 0) == elem).astype(f32).astype(bf16)
    spread = jnp.concatenate([at_elem * piece for piece in split3(value)], axis=0)
    landed = dot_nt(at_node, spread)
    source = load_ref[...] + (landed[:, 0:128] + landed[:, 128:256] + landed[:, 256:384])
    source = take_lanes(source, inv_ref[...])
    stiff_apply(start_ref, coef_ref, mass_ref, out_ref)
    out_ref[...] = source - out_ref[...]
    in_plane(out_ref)
    up_ref[0:64] = out_ref[448:512]
    up_ref[64:128] = diag_ref[448:512]
    down_ref[0:64] = out_ref[0:64]
    down_ref[64:128] = diag_ref[0:64]


def finish_through(w_ref, below, above):
    bottom, top = through(w_ref[0:64], w_ref[448:512], below, above)
    return jnp.concatenate([bottom, w_ref[64:448], top], axis=0)


def emit(update_ref, coef_ref, mass_ref, w_ref, up_ref, down_ref):
    stiff_apply(update_ref, coef_ref, mass_ref, w_ref)
    in_plane(w_ref)
    up_ref[...] = w_ref[448:512]
    down_ref[...] = w_ref[0:64]


def first_step_kernel(
    w_ref,
    diag_ref,
    start_ref,
    below_ref,
    above_ref,
    coef_ref,
    mass_ref,
    res_ref,
    upd_ref,
    cur_ref,
    invd_ref,
    w_out_ref,
    up_ref,
    down_ref,
):
    residual = finish_through(w_ref, below_ref[0:64], above_ref[0:64])
    diag = finish_through(diag_ref, below_ref[64:128], above_ref[64:128])
    invd = 1.0 / diag
    invd_ref[...] = invd
    res_ref[...] = residual
    update = residual * invd * STEPS[0][1]
    upd_ref[...] = update
    cur_ref[...] = start_ref[...] + update
    emit(upd_ref, coef_ref, mass_ref, w_out_ref, up_ref, down_ref)


def step_kernel(
    turn,
    send,
    w_ref,
    res_in_ref,
    upd_in_ref,
    cur_in_ref,
    invd_ref,
    below_ref,
    above_ref,
    coef_ref,
    mass_ref,
    res_ref,
    upd_ref,
    cur_ref,
    *out_refs,
):
    alpha, beta = STEPS[turn]
    residual = res_in_ref[...] - finish_through(w_ref, below_ref[...], above_ref[...])
    res_ref[...] = residual
    update = alpha * upd_in_ref[...] + beta * invd_ref[...] * residual
    upd_ref[...] = update
    cur_ref[...] = cur_in_ref[...] + update
    if send:
        emit(upd_ref, coef_ref, mass_ref, *out_refs)


def coarse_kernel(res_ref, w_ref, basis_ref, from_below_ref, from_above_ref, out_ref):
    zeros = jnp.zeros((64, 128), f32)
    local = res_ref[...] - finish_through(w_ref, zeros, zeros)
    sums = jnp.sum(local, axis=0, keepdims=True)
    bottom = -jnp.sum(w_ref[0:64], axis=0, keepdims=True)
    top = -jnp.sum(w_ref[448:512], axis=0, keepdims=True)
    outer = jnp.where(iota((1, 128), 1) < LAYER, bottom, top)
    outer_basis = jnp.concatenate(
        [from_below_ref[:, 0:512], from_above_ref[:, 0:512]], axis=0
    )
    left = jnp.broadcast_to(jnp.concatenate([sums, outer], axis=1), (8, 256))
    right = jnp.concatenate([basis_ref[...], outer_basis], axis=0)
    part = dot_nn(left, right, exact_mode) * (1.0 / math.sqrt(NODES))
    out_ref[...] = jnp.broadcast_to(part[0:1], (OWNERS, NC))


def restart_kernel(
    parts_ref,
    solve_ref,
    from_below_ref,
    from_above_ref,
    mass_ref,
    w_ref,
    res_in_ref,
    cur_in_ref,
    invd_ref,
    below_ref,
    above_ref,
    coef_ref,
    res_ref,
    upd_ref,
    cur_ref,
    w_out_ref,
    up_ref,
    down_ref,
    near_ref,
):
    coarse = jnp.broadcast_to(jnp.sum(parts_ref[...], axis=0, keepdims=True), (8, NC))
    outer = jnp.concatenate(
        [from_above_ref[:, 512:1024], from_below_ref[:, 512:1024]], axis=0
    )
    both = dot_nt(coarse, jnp.concatenate([solve_ref[...], outer], axis=0), exact_mode)
    own = both[0:1, 0:128]
    beside = both[0:1, 128:256]
    near_ref[0:64] = from_below_ref[:, 1024:1152] * beside
    near_ref[64:128] = from_above_ref[:, 1024:1152] * beside
    in_plane(near_ref, 2)
    w_out_ref[...] = mass_ref[...] * own
    in_plane(w_out_ref)
    total = finish_through(
        w_ref, below_ref[...], above_ref[...]
    ) + finish_through(w_out_ref, near_ref[0:64], near_ref[64:128])
    residual = res_in_ref[...] - total
    res_ref[...] = residual
    update = residual * invd_ref[...] * STEPS[0][1]
    upd_ref[...] = update
    cur_ref[...] = cur_in_ref[...] + own + update
    emit(upd_ref, coef_ref, mass_ref, w_out_ref, up_ref, down_ref)


def last_kernel(
    w_ref,
    res_in_ref,
    upd_in_ref,
    cur_in_ref,
    invd_ref,
    below_ref,
    above_ref,
    order_ref,
    out_ref,
):
    alpha, beta = STEPS[CHEB - 1]
    residual = res_in_ref[...] - finish_through(w_ref, below_ref[...], above_ref[...])
    update = alpha * upd_in_ref[...] + beta * invd_ref[...] * residual
    out_ref[...] = take_lanes(cur_in_ref[...] + update, order_ref[...])


def call(kernel, name, outs, *args, scratch=(), smem=()):
    specs = [
        pl.BlockSpec(memory_space=pltpu.SMEM if n in smem else pltpu.VMEM)
        for n in range(len(args))
    ]
    return pl.pallas_call(
        kernel,
        name=name,
        out_shape=[jax.ShapeDtypeStruct(s, d) for s, d in outs],
        in_specs=specs,
        out_specs=[pl.BlockSpec(memory_space=pltpu.VMEM) for _ in outs],
        scratch_shapes=[pltpu.VMEM(s, f32) for s in scratch],
    )(*args)


FIELD = ((NODES, 128), f32)
PLANE = ((64, 128), f32)


def exchange(up, down):
    count = lax.axis_size("elem")
    forward = [(i, i + 1) for i in range(count - 1)]
    backward = [(b, a) for a, b in forward]
    below = lax.ppermute(up, "elem", forward)
    above = lax.ppermute(down, "elem", backward)
    return below, above


def per_device(
    pressure,
    load,
    stiffness,
    helm_mass,
    order_slots,
    recv_ids,
    donor_owner,
    donor_slot,
    interp_weights,
    live_count,
    coarse_basis,
    coarse_inverse,
):
    own_field = pressure.reshape(NODES, 128)
    order = order_slots.reshape(1, 128)
    owner = donor_owner.reshape(1, R_DEV)
    other_field = lax.ppermute(own_field, "sess", [(0, 1), (1, 0)])

    send, rank = call(
        request_kernel,
        "request",
        [((OWNERS, 2 * HALF * COMPS), f32), ((1, R_DEV), f32)],
        owner,
        donor_slot,
        interp_weights.reshape(3 * NP, R_DEV),
    )
    coef, mass, start, diag, inv, basis, solve, pack_up, pack_down = call(
        setup_kernel,
        "setup",
        [
            ((3 * NODES, 128), f32),
            FIELD,
            FIELD,
            FIELD,
            ((1, 128), jnp.int32),
            ((128, NC), f32),
            ((128, NC), f32),
            ((LAYER, 2 * NC + 128), f32),
            ((LAYER, 2 * NC + 128), f32),
        ],
        order,
        stiffness.reshape(3 * NODES, 128),
        helm_mass.reshape(NODES, 128),
        own_field,
        coarse_basis.reshape(128, NC),
        coarse_inverse.reshape(NC, NC),
        scratch=[(NODES, 128)],
    )
    from_below, from_above = exchange(pack_up, pack_down)
    received = lax.all_to_all(send, "elem", split_axis=0, concat_axis=0, tiled=True)
    (answer,) = call(
        owner_kernel, "owner", [((OWNERS, 128), f32)], received, other_field
    )
    answered = lax.all_to_all(answer, "elem", split_axis=0, concat_axis=0, tiled=True)
    w, up, down = call(
        source_kernel,
        "source",
        [FIELD, ((128, 128), f32), ((128, 128), f32)],
        answered,
        owner,
        rank,
        recv_ids,
        live_count,
        load.reshape(NODES, 128),
        inv,
        start,
        coef,
        mass,
        diag,
        smem=(4,),
    )
    below, above = exchange(up, down)
    stepped = [FIELD] * 3
    sent = [FIELD, PLANE, PLANE]
    res, upd, cur, invd, w, up, down = call(
        first_step_kernel,
        "first_step",
        stepped + [FIELD] + sent,
        w,
        diag,
        start,
        below,
        above,
        coef,
        mass,
    )
    for turn in range(1, CHEB):
        below, above = exchange(up, down)
        res, upd, cur, w, up, down = call(
            functools.partial(step_kernel, turn, True),
            f"step{turn}",
            stepped + sent,
            w,
            res,
            upd,
            cur,
            invd,
            below,
            above,
            coef,
            mass,
        )
    below, above = exchange(up, down)
    (part,) = call(
        coarse_kernel,
        "coarse",
        [((OWNERS, NC), f32)],
        res,
        w,
        basis,
        from_below,
        from_above,
    )
    parts = lax.all_to_all(part, "elem", split_axis=0, concat_axis=0, tiled=True)
    res, upd, cur, w, up, down = call(
        restart_kernel,
        "restart",
        stepped + sent,
        parts,
        solve,
        from_below,
        from_above,
        mass,
        w,
        res,
        cur,
        invd,
        below,
        above,
        coef,
        scratch=[(128, 128)],
    )
    for turn in range(1, CHEB - 1):
        below, above = exchange(up, down)
        res, upd, cur, w, up, down = call(
            functools.partial(step_kernel, turn, True),
            f"again{turn}",
            stepped + sent,
            w,
            res,
            upd,
            cur,
            invd,
            below,
            above,
            coef,
            mass,
        )
    below, above = exchange(up, down)
    (out,) = call(
        last_kernel, "last", [FIELD], w, res, upd, cur, invd, below, above, order
    )
    return out.reshape(1, NP, NP, NP, 128)


def solution(mesh):
    return jax.shard_map(
        per_device,
        mesh=mesh,
        in_specs=(
            P("sess", None, None, None, "elem"),
            P("sess", None, None, None, "elem"),
            P("sess", None, None, None, None, "elem"),
            P("sess", None, None, None, "elem"),
            P("sess", "elem", None),
            P("sess", "elem"),
            P("sess", "elem", None),
            P("sess", "elem"),
            P("sess", None, "elem"),
            P("sess", "elem"),
            P("sess", "elem", None),
            P("sess", None, None),
        ),
        out_specs=P("sess", None, None, None, "elem"),
        check_vma=False,
    )
```

```python
import math

import jax
import jax.numpy as jnp
import numpy as np
from jax import lax
from jax.experimental import pallas as pl
from jax.experimental.pallas import tpu as pltpu
from jax.sharding import PartitionSpec as P

NP = 8
EX = 8
EY = 8
LAYER = EX * EY
NODES = NP**3
R_DEV = 1024
NC = 512
CHEB = 4
OWNERS = 64
COMPS = 32
HALF = 12
ASK = 8

exact_mode = lax.Precision.HIGHEST
spectrum_high = 8.0
spectrum_low = 0.8
f32 = jnp.float32
bf16 = jnp.bfloat16


def gll_derivative():
    x = np.array(
        [
            -1.0,
            -0.8717401485096066,
            -0.5917001814331423,
            -0.2092992179024789,
            0.2092992179024789,
            0.5917001814331423,
            0.8717401485096066,
            1.0,
        ]
    )
    legendre = (429.0 * x**7 - 693.0 * x**5 + 315.0 * x**3 - 35.0 * x) / 16.0
    distance = x[:, None] - x[None, :]
    same = np.eye(8, dtype=bool)
    table = legendre[:, None] / (legendre[None, :] * np.where(same, 1.0, distance))
    corner = np.zeros((8, 8))
    corner[0, 0] = -14.0
    corner[7, 7] = 14.0
    return np.where(same, corner, table).astype(np.float32).astype(np.float64)


DERIV = gll_derivative()


def chebyshev():
    center = 0.5 * (spectrum_high + spectrum_low)
    half_width = 0.5 * (spectrum_high - spectrum_low)
    sigma_ratio = center / half_width
    rho = 1.0 / sigma_ratio
    steps = [(0.0, 1.0 / center)]
    for _ in range(CHEB - 1):
        rho_next = 1.0 / (2.0 * sigma_ratio - rho)
        steps.append((rho_next * rho, 2.0 * rho_next / half_width))
        rho = rho_next
    return steps


STEPS = chebyshev()


def split3(x):
    hi = x.astype(bf16)
    rest = x - hi.astype(f32)
    mid = rest.astype(bf16)
    low = (rest - mid.astype(f32)).astype(bf16)
    return hi, mid, low


def dot_nn(a, b, precision=None):
    return lax.dot_general(
        a, b, (((1,), (0,)), ((), ())), precision=precision, preferred_element_type=f32
    )


def dot_nt(a, b, precision=None):
    return lax.dot_general(
        a, b, (((1,), (1,)), ((), ())), precision=precision, preferred_element_type=f32
    )


def iota(shape, axis):
    return lax.broadcasted_iota(jnp.int32, shape, axis)


def build_requests(owner_ref, slot_ref, weight_ref, send_ref, rank_ref):
    owner = owner_ref[...]
    hits = iota((OWNERS, R_DEV), 0) == owner
    hits_f = hits.astype(f32)
    hits_b = hits_f.astype(bf16)
    upper = (iota((128, 128), 0) < iota((128, 128), 1)).astype(f32).astype(bf16)
    carry = jnp.zeros((OWNERS, 1), f32)
    ranks = []
    for b in range(R_DEV // 128):
        cols = slice(b * 128, b * 128 + 128)
        block = hits_f[:, cols]
        count = dot_nn(hits_b[:, cols], upper) + carry
        ranks.append(jnp.sum(block * count, axis=0, keepdims=True))
        carry = carry + jnp.sum(block, axis=1, keepdims=True)
    rank = jnp.concatenate(ranks, axis=1)
    rank_ref[...] = rank
    payload = jnp.concatenate(
        [
            weight_ref[...],
            jnp.broadcast_to(slot_ref[...].astype(f32), (COMPS - 3 * NP, R_DEV)),
        ],
        axis=0,
    )
    pieces = split3(payload)
    total = None
    for piece in pieces:
        rows = [
            piece * (rank == float(m)).astype(f32).astype(bf16) for m in range(2 * HALF)
        ]
        part = dot_nt(hits_b, jnp.concatenate(rows, axis=0))
        total = part if total is None else total + part
    for c in range(ASK):
        if c < 2 * HALF * COMPS // 128:
            block = total[:, c * 128 : c * 128 + 128]
        else:
            block = jnp.zeros((OWNERS, 128), f32)
        send_ref[pl.ds(c, OWNERS, stride=ASK), :] = block


def owner_kernel(recv_ref, field_ref, ret_ref):
    cols = [recv_ref[pl.ds(c, OWNERS, stride=ASK), :] for c in range(6)]
    packed = jnp.concatenate(
        [jnp.concatenate(cols[:3], axis=1), jnp.concatenate(cols[3:], axis=1)], axis=0
    )
    comps = packed.T
    pieces = jnp.concatenate(split3(field_ref[...]), axis=1)
    rows = []
    for pair in range(HALF // 2):
        a = comps[(2 * pair) * COMPS : (2 * pair + 1) * COMPS]
        b = comps[(2 * pair + 1) * COMPS : (2 * pair + 2) * COMPS]
        both = jnp.concatenate([a, b], axis=1)
        slot = both[3 * NP : 3 * NP + 1].astype(jnp.int32)
        pick = (iota((128, 256), 0) == slot).astype(f32).astype(bf16)
        gathered = dot_nn(pieces, jnp.concatenate([pick, pick, pick], axis=0))
        wx = both[0:NP]
        wy = both[NP : 2 * NP]
        wz = both[2 * NP : 3 * NP]
        acc = None
        for k in range(NP):
            line = None
            for j in range(NP):
                row = (k * NP + j) * NP
                term = gathered[row : row + NP] * wy[j : j + 1]
                line = term if line is None else line + term
            line = line * wz[k : k + 1]
            acc = line if acc is None else acc + line
        value = jnp.sum(acc * wx, axis=0, keepdims=True)
        rows.append(value[:, :128])
        rows.append(value[:, 128:])
    rows.append(jnp.zeros((128 - HALF, 128), f32))
    turned = jnp.concatenate(rows, axis=0).T
    ret_ref[...] = turned[:OWNERS] + pltpu.roll(turned[OWNERS:], 16, 1)


def deriv8(table, v):
    plus = [v[m] + v[7 - m] for m in range(4)]
    minus = [v[m] - v[7 - m] for m in range(4)]
    out = [None] * 8
    for a in range(4):
        even = odd = None
        for m in range(4):
            ce = 0.5 * (table[a, m] + table[a, 7 - m])
            co = 0.5 * (table[a, m] - table[a, 7 - m])
            te = plus[m] * float(ce)
            to = minus[m] * float(co)
            even = te if even is None else even + te
            odd = to if odd is None else odd + to
        out[a] = odd + even
        out[7 - a] = odd - even
    return out


def apply_line(v, coef):
    grad = deriv8(DERIV, v)
    return deriv8(DERIV.T, [grad[a] * coef(a) for a in range(8)])


def stiff_apply(v_ref, coef_ref, mass_ref, out_ref):
    def per_k(k, carry):
        base = pl.multiple_of(k * 64, 64)
        lines = [v_ref[pl.ds(base + i, 8, stride=8), :] for i in range(8)]
        res = apply_line(lines, lambda a: coef_ref[pl.ds(base + a * 8, 8), :])
        for i in range(8):
            out_ref[pl.ds(base + i, 8, stride=8), :] = res[i]
        rows = [v_ref[pl.ds(base + j * 8, 8), :] for j in range(8)]
        res = apply_line(rows, lambda b: coef_ref[pl.ds(512 + base + b * 8, 8), :])
        for j in range(8):
            at = pl.ds(base + j * 8, 8)
            out_ref[at, :] = out_ref[at, :] + res[j] + mass_ref[at, :] * rows[j]
        return carry

    lax.fori_loop(0, 8, per_k, 0)

    def per_j(j, carry):
        base = pl.multiple_of(j * 8, 8)
        cols = [v_ref[pl.ds(base + k * 64, 8), :] for k in range(8)]
        res = apply_line(cols, lambda c: coef_ref[pl.ds(1024 + base + c * 64, 8), :])
        for k in range(8):
            at = pl.ds(base + k * 64, 8)
            out_ref[at, :] = out_ref[at, :] + res[k]
        return carry

    lax.fori_loop(0, 8, per_j, 0)


def couple(high, low, shift, pos, count):
    lanes = high.shape[-1]
    next_low = pltpu.roll(low, lanes - shift, high.ndim - 1)
    prev_high = pltpu.roll(high, shift, high.ndim - 1)
    new_high = high + jnp.where(pos < count - 1, next_low, 0.0)
    new_low = low + jnp.where(pos > 0, prev_high, 0.0)
    return new_high, new_low


def in_plane(ref, count=NP):
    rows = count * NP
    col = iota((rows, 128), 1) % EX
    high, low = couple(
        ref[pl.ds(7, rows, stride=8), :], ref[pl.ds(0, rows, stride=8), :], 1, col, EX
    )
    ref[pl.ds(7, rows, stride=8), :] = high
    ref[pl.ds(0, rows, stride=8), :] = low
    line = (iota((8, 128), 1) // EX) % EY
    for k in range(count):
        high, low = couple(
            ref[k * 64 + 56 : k * 64 + 64], ref[k * 64 : k * 64 + 8], EX, line, EY
        )
        ref[k * 64 + 56 : k * 64 + 64] = high
        ref[k * 64 : k * 64 + 8] = low


def through(bottom, top, below, above):
    first = iota(bottom.shape, 1) < LAYER
    new_bottom = bottom + pltpu.roll(jnp.where(first, top, below), LAYER, 1)
    new_top = top + pltpu.roll(jnp.where(first, above, bottom), LAYER, 1)
    return new_bottom, new_top


def whole(bottom, ref, top):
    return jnp.concatenate([bottom, ref[64:448], top], axis=0)


def coupled(w_ref, below, above):
    bottom, top = through(w_ref[0:64], w_ref[448:512], below, above)
    return whole(bottom, w_ref, top)


def where_am_i():
    me = lax.axis_index("elem")
    last = lax.axis_size("elem") - 1
    return jnp.bitwise_and(me, 1) == 0, me > 0, me < last


def first_layer(shape):
    return iota(shape, 1) < LAYER


def pack(field, a_ref, b_ref, row, even):
    low, high = field[0:256], field[256:512]
    first = first_layer(low.shape)
    up = jnp.where(first, pltpu.roll(low, LAYER, 1), high)
    down = jnp.where(first, low, pltpu.roll(high, LAYER, 1))
    a_ref[row : row + 256] = jnp.where(even, up, down)
    b_ref[row : row + 256] = jnp.where(even, down, up)


def beside(a, b, place):
    even, has_below, has_above = place
    below = jnp.where(has_below, jnp.where(even, b, a), 0.0)
    above = jnp.where(has_above, jnp.where(even, a, b), 0.0)
    return below, above


def unpack(a_ref, b_ref, row, place, out_ref):
    below, above = beside(a_ref[row : row + 256], b_ref[row : row + 256], place)
    first = first_layer(below.shape)
    out_ref[0:256] = jnp.where(first, above, pltpu.roll(below, LAYER, 1))
    out_ref[256:512] = jnp.where(first, pltpu.roll(above, LAYER, 1), below)


def mirror(ghost_ref, bottom, top):
    first = first_layer(bottom.shape)
    ghost_ref[448:512] = jnp.where(first, ghost_ref[448:512], pltpu.roll(bottom, LAYER, 1))
    ghost_ref[0:64] = jnp.where(first, pltpu.roll(top, LAYER, 1), ghost_ref[0:64])


def message(raw_bottom, raw_top, inner_bottom, mid, inner_top):
    first = first_layer(raw_bottom.shape)
    return jnp.concatenate(
        [
            jnp.where(first, raw_bottom, inner_bottom),
            mid,
            jnp.where(first, inner_top, raw_top),
        ],
        axis=0,
    )


def ghost_apply(ghost_ref, third_ref, planes_ref, face_ref, out_ref):
    first = first_layer((8, 128))
    face_ref[...] = jnp.where(
        first_layer((64, 128)), ghost_ref[0:64], ghost_ref[448:512]
    )
    lines = [face_ref[pl.ds(i, 8, stride=8), :] for i in range(8)]
    res = apply_line(lines, lambda a: planes_ref[a * 8 : a * 8 + 8])
    for i in range(8):
        out_ref[pl.ds(i, 8, stride=8), :] = res[i]
    rows = [face_ref[j * 8 : j * 8 + 8] for j in range(8)]
    res = apply_line(rows, lambda b: planes_ref[64 + b * 8 : 72 + b * 8])
    ends = [
        jnp.where(first, float(DERIV[c, 0]), float(DERIV[c, 7])).astype(f32)
        for c in range(8)
    ]
    for j in range(8):
        total = out_ref[j * 8 : j * 8 + 8] + res[j]
        total = total + planes_ref[128 + j * 8 : 136 + j * 8] * rows[j]
        cols = [ghost_ref[k * 64 + j * 8 : k * 64 + j * 8 + 8] for k in range(8)]
        grad = deriv8(DERIV, cols)
        for c in range(8):
            at = c * 64 + j * 8
            total = total + grad[c] * third_ref[at : at + 8] * ends[c]
        out_ref[j * 8 : j * 8 + 8] = total
    in_plane(out_ref, 1)


def plain8(table, v):
    out = []
    for i in range(8):
        total = None
        for a in range(8):
            if table[a, i] == 0.0:
                continue
            term = v[a] * float(table[a, i])
            total = term if total is None else total + term
        out.append(total)
    return out


def take_lanes(x, index):
    return jnp.take_along_axis(
        x, jnp.broadcast_to(index, x.shape), axis=1, mode="promise_in_bounds"
    )


def local_diagonal(coef_ref, mass_ref, diag_ref):
    squared = DERIV * DERIV

    def per_k(k, carry):
        base = pl.multiple_of(k * 64, 64)
        res = plain8(squared, [coef_ref[pl.ds(base + a * 8, 8), :] for a in range(8)])
        for i in range(8):
            diag_ref[pl.ds(base + i, 8, stride=8), :] = res[i]
        res = plain8(squared, [coef_ref[pl.ds(512 + base + b * 8, 8), :] for b in range(8)])
        for j in range(8):
            at = pl.ds(base + j * 8, 8)
            diag_ref[at, :] = diag_ref[at, :] + res[j] + mass_ref[at, :]
        return carry

    lax.fori_loop(0, 8, per_k, 0)

    def per_j(j, carry):
        base = pl.multiple_of(j * 8, 8)
        res = plain8(squared, [coef_ref[pl.ds(1024 + base + c * 64, 8), :] for c in range(8)])
        for k in range(8):
            at = pl.ds(base + k * 64, 8)
            diag_ref[at, :] = diag_ref[at, :] + res[k]
        return carry

    lax.fori_loop(0, 8, per_j, 0)


BASIS_ROW = 704
GHOST_ROWS = BASIS_ROW + 256


def prepare_kernel(
    owner_ref,
    slot_ref,
    weight_ref,
    order_ref,
    stiff_hbm,
    mass_hbm,
    field_hbm,
    basis_hbm,
    inverse_hbm,
    send_ref,
    rank_ref,
    coef_ref,
    mass_ref,
    start_ref,
    diag_ref,
    inv_ref,
    basis_ref,
    solve_ref,
    a_ref,
    b_ref,
    stiff_in,
    mass_in,
    field_in,
    basis_in,
    inverse_in,
    tmp_ref,
    sems,
):
    copies = [
        pltpu.make_async_copy(src, dst, sems.at[n])
        for n, (src, dst) in enumerate(
            [
                (stiff_hbm, stiff_in),
                (mass_hbm, mass_in),
                (field_hbm, field_in),
                (basis_hbm, basis_in),
                (inverse_hbm, inverse_in),
            ]
        )
    ]
    for copy in copies:
        copy.start()
    build_requests(owner_ref, slot_ref, weight_ref, send_ref, rank_ref)
    order = order_ref[...]
    match = (iota((128, 128), 0) == order).astype(f32)
    inv = jnp.sum(match.T * iota((128, 128), 0).astype(f32), axis=0, keepdims=True)
    inv = inv.astype(jnp.int32)
    inv_ref[...] = inv
    for copy in copies:
        copy.wait()
    tmp_ref[...] = take_lanes(stiff_in[0:512, :], inv)
    for k in range(8):
        for i in range(8):
            coef_ref[k * 64 + i * 8 : k * 64 + i * 8 + 8, :] = tmp_ref[
                pl.ds(k * 64 + i, 8, stride=8), :
            ]
    coef_ref[512:1536, :] = take_lanes(stiff_in[512:1536, :], inv)
    mass_ref[...] = take_lanes(mass_in[...], inv)
    start_ref[...] = take_lanes(field_in[...], inv)
    basis = dot_nn(match, basis_in[...], exact_mode)
    basis_ref[...] = basis
    solve_ref[...] = dot_nn(basis, inverse_in[...], exact_mode)
    local_diagonal(coef_ref, mass_ref, diag_ref)
    in_plane(diag_ref)
    even = where_am_i()[0]
    zeros = jnp.zeros((64, 128), f32)
    pack(coef_ref[1024:1536, :], a_ref, b_ref, 0, even)
    pack(coupled(diag_ref, zeros, zeros), a_ref, b_ref, 256, even)
    rows = [
        (coef_ref[448:512], coef_ref[0:64]),
        (coef_ref[960:1024], coef_ref[512:576]),
        (mass_ref[448:512], mass_ref[0:64]),
    ]
    for c in range(NC // 128):
        cols = slice(c * 128, c * 128 + 128)
        rows.append((basis[LAYER:, cols], basis[:LAYER, cols]))
    for n, (up, down) in enumerate(rows):
        at = 512 + n * 64
        a_ref[at : at + 64] = jnp.where(even, up, down)
        b_ref[at : at + 64] = jnp.where(even, down, up)


def source_kernel(
    ret_ref,
    owner_ref,
    rank_ref,
    ids_ref,
    live_ref,
    load_ref,
    inv_ref,
    start_ref,
    coef_ref,
    mass_ref,
    out_ref,
    a_ref,
    b_ref,
):
    hits = (iota((OWNERS, R_DEV), 0) == owner_ref[...]).astype(f32)
    picked = dot_nn(ret_ref[...].T, hits, exact_mode)[0:32]
    rank = rank_ref[...].astype(jnp.int32)
    place = rank + jnp.where(rank >= HALF, 16 - HALF, 0)
    value = jnp.sum(
        jnp.where(iota((32, R_DEV), 0) == place, picked, 0.0), axis=0, keepdims=True
    )
    value = jnp.where(iota((1, R_DEV), 1) < live_ref[0, 0], value, 0.0)
    ids = ids_ref[...]
    node = lax.shift_right_logical(ids, 7)
    elem = jnp.bitwise_and(ids, 127)
    at_node = (iota((NODES, R_DEV), 0) == node).astype(f32).astype(bf16)
    at_elem = (iota((128, R_DEV), 0) == elem).astype(f32).astype(bf16)
    spread = jnp.concatenate([at_elem * piece for piece in split3(value)], axis=0)
    landed = dot_nt(at_node, spread)
    source = load_ref[...] + (landed[:, 0:128] + landed[:, 128:256] + landed[:, 256:384])
    source = take_lanes(source, inv_ref[...])
    stiff_apply(start_ref, coef_ref, mass_ref, out_ref)
    out_ref[...] = source - out_ref[...]
    in_plane(out_ref)
    zeros = jnp.zeros((64, 128), f32)
    pack(coupled(out_ref, zeros, zeros), a_ref, b_ref, 0, where_am_i()[0])


def opening_half(
    place,
    base_ref,
    y_ref,
    cur_in_ref,
    a_ref,
    b_ref,
    invd_ref,
    third_ref,
    ginvd_ref,
    planes_ref,
    coef_ref,
    mass_ref,
    res_ref,
    upd_ref,
    cur_ref,
    w_ref,
    a_out_ref,
    b_out_ref,
    ghost_ref,
    face_ref,
    side_ref,
):
    unpack(a_ref, b_ref, 0, place, ghost_ref)
    residual = coupled(y_ref, ghost_ref[448:512], ghost_ref[0:64])
    if base_ref is not None:
        residual = residual + base_ref[...]
    mirror(ghost_ref, residual[0:64], residual[448:512])
    invd = invd_ref[...]
    update = residual * invd * STEPS[0][1]
    upd_ref[...] = update
    ghost_ref[...] = ghost_ref[...] * ginvd_ref[...] * STEPS[0][1]
    stiff_apply(upd_ref, coef_ref, mass_ref, w_ref)
    in_plane(w_ref)
    ghost_apply(ghost_ref, third_ref, planes_ref, face_ref, side_ref)
    residual = residual - coupled(w_ref, side_ref[...], side_ref[...])
    res_ref[...] = residual
    alpha, beta = STEPS[1]
    second = alpha * update + beta * invd * residual
    upd_ref[...] = second
    cur_ref[...] = cur_in_ref[...] + (update + second)
    stiff_apply(upd_ref, coef_ref, mass_ref, w_ref)
    in_plane(w_ref)
    alpha, beta = STEPS[2]
    zeros = jnp.zeros((64, 128), f32)
    inner = alpha * upd_ref[...] + beta * invd_ref[...] * (
        res_ref[...] - coupled(w_ref, zeros, zeros)
    )
    pack(
        message(w_ref[0:64], w_ref[448:512], inner[0:64], inner[64:448], inner[448:512]),
        a_out_ref,
        b_out_ref,
        0,
        place[0],
    )


def start_kernel(
    y_ref,
    diag_ref,
    cur_in_ref,
    a_ref,
    b_ref,
    ga_ref,
    gb_ref,
    coef_ref,
    mass_ref,
    res_ref,
    upd_ref,
    cur_ref,
    w_ref,
    a_out_ref,
    b_out_ref,
    invd_ref,
    third_ref,
    ginvd_ref,
    planes_ref,
    outer_ref,
    *scratch,
):
    place = where_am_i()
    unpack(ga_ref, gb_ref, 0, place, third_ref)
    unpack(ga_ref, gb_ref, 256, place, ginvd_ref)
    diag = coupled(diag_ref, ginvd_ref[448:512], ginvd_ref[0:64])
    mirror(ginvd_ref, diag[0:64], diag[448:512])
    invd_ref[...] = 1.0 / diag
    gdiag = ginvd_ref[...]
    there = gdiag > 0.0
    ginvd_ref[...] = jnp.where(there, 1.0 / jnp.where(there, gdiag, 1.0), 0.0)
    below, above = beside(ga_ref[512:704], gb_ref[512:704], place)
    planes_ref[...] = jnp.where(first_layer(below.shape), above, below)
    for c in range(NC // 128):
        at = BASIS_ROW + c * 64
        below, above = beside(ga_ref[at : at + 64], gb_ref[at : at + 64], place)
        outer_ref[0:64, c * 128 : c * 128 + 128] = below
        outer_ref[64:128, c * 128 : c * 128 + 128] = above
    opening_half(
        place,
        None,
        y_ref,
        cur_in_ref,
        a_ref,
        b_ref,
        invd_ref,
        third_ref,
        ginvd_ref,
        planes_ref,
        coef_ref,
        mass_ref,
        res_ref,
        upd_ref,
        cur_ref,
        w_ref,
        a_out_ref,
        b_out_ref,
        *scratch,
    )


def again_kernel(*refs):
    opening_half(where_am_i(), *refs)


def closing_half(
    w_ref,
    res_ref,
    upd_ref,
    cur_ref,
    invd_ref,
    a_ref,
    b_ref,
    third_ref,
    planes_ref,
    coef_ref,
    mass_ref,
    work_ref,
    vec_ref,
    ghost_ref,
    face_ref,
    side_ref,
):
    unpack(a_ref, b_ref, 0, where_am_i(), ghost_ref)
    residual = res_ref[...] - coupled(w_ref, ghost_ref[448:512], ghost_ref[0:64])
    alpha, beta = STEPS[2]
    third = alpha * upd_ref[...] + beta * invd_ref[...] * residual
    vec_ref[...] = third
    mirror(ghost_ref, third[0:64], third[448:512])
    stiff_apply(vec_ref, coef_ref, mass_ref, work_ref)
    in_plane(work_ref)
    ghost_apply(ghost_ref, third_ref, planes_ref, face_ref, side_ref)
    residual = residual - coupled(work_ref, side_ref[...], side_ref[...])
    alpha, beta = STEPS[3]
    fourth = alpha * third + beta * invd_ref[...] * residual
    vec_ref[...] = fourth
    return residual, cur_ref[...] + (third + fourth)


def middle_kernel(
    w_ref,
    res_in_ref,
    upd_ref,
    cur_in_ref,
    invd_ref,
    a_ref,
    b_ref,
    third_ref,
    planes_ref,
    coef_ref,
    mass_ref,
    basis_ref,
    outer_ref,
    res_ref,
    cur_ref,
    w_out_ref,
    part_ref,
    vec_ref,
    *scratch,
):
    residual, current = closing_half(
        w_ref,
        res_in_ref,
        upd_ref,
        cur_in_ref,
        invd_ref,
        a_ref,
        b_ref,
        third_ref,
        planes_ref,
        coef_ref,
        mass_ref,
        w_out_ref,
        vec_ref,
        *scratch,
    )
    res_ref[...] = residual
    cur_ref[...] = current
    stiff_apply(vec_ref, coef_ref, mass_ref, w_out_ref)
    in_plane(w_out_ref)
    zeros = jnp.zeros((64, 128), f32)
    local = res_ref[...] - coupled(w_out_ref, zeros, zeros)
    sums = jnp.sum(local, axis=0, keepdims=True)
    bottom = -jnp.sum(w_out_ref[0:64], axis=0, keepdims=True)
    top = -jnp.sum(w_out_ref[448:512], axis=0, keepdims=True)
    outer = jnp.where(first_layer((1, 128)), bottom, top)
    left = jnp.broadcast_to(jnp.concatenate([sums, outer], axis=1), (8, 256))
    right = jnp.concatenate([basis_ref[...], outer_ref[...]], axis=0)
    part = dot_nn(left, right, exact_mode)[0:1] * (1.0 / math.sqrt(NODES))
    blocks = [part[:, c * 128 : c * 128 + 128] for c in range(NC // 128)]
    eight = jnp.concatenate(blocks + blocks, axis=0)
    for n in range(OWNERS * NC // 1024):
        part_ref[n * 8 : n * 8 + 8] = eight


def restart_kernel(
    parts_ref,
    solve_ref,
    mass_ref,
    w_ref,
    base_ref,
    cur_in_ref,
    y_ref,
    cur_ref,
    a_ref,
    b_ref,
):
    total = parts_ref[0:8]
    for n in range(1, OWNERS * NC // 1024):
        total = total + parts_ref[n * 8 : n * 8 + 8]
    total = total + pltpu.roll(total, 4, 0)
    correction = None
    for c in range(NC // 128):
        row = jnp.broadcast_to(total[c : c + 1], (8, 128))
        term = dot_nt(row, solve_ref[:, c * 128 : c * 128 + 128], exact_mode)
        correction = term if correction is None else correction + term
    correction = correction[0:1]
    cur_ref[...] = cur_in_ref[...] + correction
    y_ref[...] = mass_ref[...] * correction
    in_plane(y_ref)
    y_ref[...] = -(y_ref[...] + w_ref[...])
    zeros = jnp.zeros((64, 128), f32)
    inner = base_ref[...] + coupled(y_ref, zeros, zeros)
    pack(
        message(y_ref[0:64], y_ref[448:512], inner[0:64], inner[64:448], inner[448:512]),
        a_ref,
        b_ref,
        0,
        where_am_i()[0],
    )


def last_kernel(*refs):
    inputs, (order_ref, out_ref), scratch = refs[:11], refs[11:13], refs[13:]
    current = closing_half(*inputs, *scratch)[1]
    out_ref[...] = take_lanes(current, order_ref[...])


def call(kernel, name, outs, *args, scratch=(), smem=(), far=(), copies=0):
    def space(n):
        if n in smem:
            return pltpu.SMEM
        return pl.ANY if n in far else pltpu.VMEM

    scratches = [pltpu.VMEM(s, f32) for s in scratch]
    if copies:
        scratches.append(pltpu.SemaphoreType.DMA((copies,)))
    return pl.pallas_call(
        kernel,
        name=name,
        out_shape=[jax.ShapeDtypeStruct(s, d) for s, d in outs],
        in_specs=[pl.BlockSpec(memory_space=space(n)) for n in range(len(args))],
        out_specs=[pl.BlockSpec(memory_space=pltpu.VMEM) for _ in outs],
        scratch_shapes=scratches,
        compiler_params=pltpu.CompilerParams(vmem_limit_bytes=20 << 20),
    )(*args)


FIELD = ((NODES, 128), f32)
LAYER_MSG = ((256, 128), f32)
GHOST_MSG = ((GHOST_ROWS, 128), f32)
GHOST_WORK = [(NODES, 128), (64, 128), (64, 128)]


def exchange(a, b):
    count = lax.axis_size("elem")
    pairs_a = [(i, i ^ 1) for i in range(count)]
    pairs_b = [(i, (i + (1 if i % 2 else -1)) % count) for i in range(count)]
    return lax.ppermute(a, "elem", pairs_a), lax.ppermute(b, "elem", pairs_b)


def per_device(
    pressure,
    load,
    stiffness,
    helm_mass,
    order_slots,
    recv_ids,
    donor_owner,
    donor_slot,
    interp_weights,
    live_count,
    coarse_basis,
    coarse_inverse,
):
    own_field = pressure.reshape(NODES, 128)
    order = order_slots.reshape(1, 128)
    owner = donor_owner.reshape(1, R_DEV)
    other_field = lax.ppermute(own_field, "sess", [(0, 1), (1, 0)])

    send, rank, coef, mass, start, diag, inv, basis, solve, ghost_a, ghost_b = call(
        prepare_kernel,
        "prepare",
        [
            ((OWNERS * ASK, 128), f32),
            ((1, R_DEV), f32),
            ((3 * NODES, 128), f32),
            FIELD,
            FIELD,
            FIELD,
            ((1, 128), jnp.int32),
            ((128, NC), f32),
            ((128, NC), f32),
            GHOST_MSG,
            GHOST_MSG,
        ],
        owner,
        donor_slot,
        interp_weights.reshape(3 * NP, R_DEV),
        order,
        stiffness.reshape(3 * NODES, 128),
        helm_mass.reshape(NODES, 128),
        own_field,
        coarse_basis.reshape(128, NC),
        coarse_inverse.reshape(NC, NC),
        far=(4, 5, 6, 7, 8),
        scratch=[
            (3 * NODES, 128),
            (NODES, 128),
            (NODES, 128),
            (128, NC),
            (NC, NC),
            (NODES, 128),
        ],
        copies=5,
    )
    ghost_a, ghost_b = exchange(ghost_a, ghost_b)
    received = lax.all_to_all(
        send.reshape(OWNERS, ASK, 128), "elem", split_axis=0, concat_axis=0, tiled=True
    )
    (answer,) = call(
        owner_kernel,
        "owner",
        [((OWNERS, 128), f32)],
        received.reshape(OWNERS * ASK, 128),
        other_field,
    )
    answered = lax.all_to_all(answer, "elem", split_axis=0, concat_axis=0, tiled=True)
    y, a, b = call(
        source_kernel,
        "source",
        [FIELD, LAYER_MSG, LAYER_MSG],
        answered,
        owner,
        rank,
        recv_ids,
        live_count,
        load.reshape(NODES, 128),
        inv,
        start,
        coef,
        mass,
        smem=(4,),
    )
    a, b = exchange(a, b)
    half = [FIELD, FIELD, FIELD, FIELD, LAYER_MSG, LAYER_MSG]
    res, upd, cur, w, a, b, invd, third, ginvd, planes, outer = call(
        start_kernel,
        "start",
        half + [FIELD, FIELD, FIELD, ((192, 128), f32), ((128, NC), f32)],
        y,
        diag,
        start,
        a,
        b,
        ghost_a,
        ghost_b,
        coef,
        mass,
        scratch=GHOST_WORK,
    )
    a, b = exchange(a, b)
    res, cur, w, part = call(
        middle_kernel,
        "middle",
        [FIELD, FIELD, FIELD, ((OWNERS * NC // 128, 128), f32)],
        w,
        res,
        upd,
        cur,
        invd,
        a,
        b,
        third,
        planes,
        coef,
        mass,
        basis,
        outer,
        scratch=[(NODES, 128)] + GHOST_WORK,
    )
    parts = lax.all_to_all(
        part.reshape(OWNERS, NC // 128, 128),
        "elem",
        split_axis=0,
        concat_axis=0,
        tiled=True,
    )
    y, cur, a, b = call(
        restart_kernel,
        "restart",
        [FIELD, FIELD, LAYER_MSG, LAYER_MSG],
        parts.reshape(OWNERS * NC // 128, 128),
        solve,
        mass,
        w,
        res,
        cur,
    )
    a, b = exchange(a, b)
    res, upd, cur, w, a, b = call(
        again_kernel,
        "again",
        half,
        res,
        y,
        cur,
        a,
        b,
        invd,
        third,
        ginvd,
        planes,
        coef,
        mass,
        scratch=GHOST_WORK,
    )
    a, b = exchange(a, b)
    (out,) = call(
        last_kernel,
        "last",
        [FIELD],
        w,
        res,
        upd,
        cur,
        invd,
        a,
        b,
        third,
        planes,
        coef,
        mass,
        order,
        scratch=[(NODES, 128), (NODES, 128)] + GHOST_WORK,
    )
    return out.reshape(1, NP, NP, NP, 128)


def solution(mesh):
    return jax.shard_map(
        per_device,
        mesh=mesh,
        in_specs=(
            P("sess", None, None, None, "elem"),
            P("sess", None, None, None, "elem"),
            P("sess", None, None, None, None, "elem"),
            P("sess", None, None, None, "elem"),
            P("sess", "elem", None),
            P("sess", "elem"),
            P("sess", "elem", None),
            P("sess", "elem"),
            P("sess", None, "elem"),
            P("sess", "elem"),
            P("sess", "elem", None),
            P("sess", None, None),
        ),
        out_specs=P("sess", None, None, None, "elem"),
        check_vma=False,
    )
```

```python
import math

import jax
import jax.numpy as jnp
import numpy as np
from jax import lax
from jax.experimental import pallas as pl
from jax.experimental.pallas import tpu as pltpu
from jax.sharding import PartitionSpec as P

NP = 8
EX = 8
EY = 8
LAYER = EX * EY
NODES = NP**3
R_DEV = 1024
NC = 512
CHEB = 4
OWNERS = 64
COMPS = 32
HALF = 12
ASK = 8

exact_mode = lax.Precision.HIGHEST
spectrum_high = 8.0
spectrum_low = 0.8
f32 = jnp.float32
bf16 = jnp.bfloat16


def gll_derivative():
    x = np.array(
        [
            -1.0,
            -0.8717401485096066,
            -0.5917001814331423,
            -0.2092992179024789,
            0.2092992179024789,
            0.5917001814331423,
            0.8717401485096066,
            1.0,
        ]
    )
    legendre = (429.0 * x**7 - 693.0 * x**5 + 315.0 * x**3 - 35.0 * x) / 16.0
    distance = x[:, None] - x[None, :]
    same = np.eye(8, dtype=bool)
    table = legendre[:, None] / (legendre[None, :] * np.where(same, 1.0, distance))
    corner = np.zeros((8, 8))
    corner[0, 0] = -14.0
    corner[7, 7] = 14.0
    return np.where(same, corner, table).astype(np.float32).astype(np.float64)


DERIV = gll_derivative()


def chebyshev():
    center = 0.5 * (spectrum_high + spectrum_low)
    half_width = 0.5 * (spectrum_high - spectrum_low)
    sigma_ratio = center / half_width
    rho = 1.0 / sigma_ratio
    steps = [(0.0, 1.0 / center)]
    for _ in range(CHEB - 1):
        rho_next = 1.0 / (2.0 * sigma_ratio - rho)
        steps.append((rho_next * rho, 2.0 * rho_next / half_width))
        rho = rho_next
    return steps


STEPS = chebyshev()


def split3(x):
    hi = x.astype(bf16)
    rest = x - hi.astype(f32)
    mid = rest.astype(bf16)
    low = (rest - mid.astype(f32)).astype(bf16)
    return hi, mid, low


def dot_nn(a, b, precision=None):
    return lax.dot_general(
        a, b, (((1,), (0,)), ((), ())), precision=precision, preferred_element_type=f32
    )


def dot_nt(a, b, precision=None):
    return lax.dot_general(
        a, b, (((1,), (1,)), ((), ())), precision=precision, preferred_element_type=f32
    )


def iota(shape, axis):
    return lax.broadcasted_iota(jnp.int32, shape, axis)


def build_requests(owner_ref, slot_ref, weight_ref, send_ref, rank_ref):
    owner = owner_ref[...]
    hits = iota((OWNERS, R_DEV), 0) == owner
    hits_f = hits.astype(f32)
    hits_b = hits_f.astype(bf16)
    upper = (iota((128, 128), 0) < iota((128, 128), 1)).astype(f32).astype(bf16)
    carry = jnp.zeros((OWNERS, 1), f32)
    ranks = []
    for b in range(R_DEV // 128):
        cols = slice(b * 128, b * 128 + 128)
        block = hits_f[:, cols]
        count = dot_nn(hits_b[:, cols], upper) + carry
        ranks.append(jnp.sum(block * count, axis=0, keepdims=True))
        carry = carry + jnp.sum(block, axis=1, keepdims=True)
    rank = jnp.concatenate(ranks, axis=1)
    rank_ref[...] = rank
    payload = jnp.concatenate(
        [
            weight_ref[...],
            jnp.broadcast_to(slot_ref[...].astype(f32), (COMPS - 3 * NP, R_DEV)),
        ],
        axis=0,
    )
    pieces = split3(payload)
    total = None
    for piece in pieces:
        rows = [
            piece * (rank == float(m)).astype(f32).astype(bf16) for m in range(2 * HALF)
        ]
        part = dot_nt(hits_b, jnp.concatenate(rows, axis=0))
        total = part if total is None else total + part
    for c in range(ASK):
        if c < 2 * HALF * COMPS // 128:
            block = total[:, c * 128 : c * 128 + 128]
        else:
            block = jnp.zeros((OWNERS, 128), f32)
        send_ref[pl.ds(c, OWNERS, stride=ASK), :] = block


def owner_kernel(recv_ref, field_ref, ret_ref):
    cols = [recv_ref[pl.ds(c, OWNERS, stride=ASK), :] for c in range(6)]
    packed = jnp.concatenate(
        [jnp.concatenate(cols[:3], axis=1), jnp.concatenate(cols[3:], axis=1)], axis=0
    )
    comps = packed.T
    pieces = jnp.concatenate(split3(field_ref[...]), axis=1)
    rows = []
    for pair in range(HALF // 2):
        a = comps[(2 * pair) * COMPS : (2 * pair + 1) * COMPS]
        b = comps[(2 * pair + 1) * COMPS : (2 * pair + 2) * COMPS]
        both = jnp.concatenate([a, b], axis=1)
        slot = both[3 * NP : 3 * NP + 1].astype(jnp.int32)
        pick = (iota((128, 256), 0) == slot).astype(f32).astype(bf16)
        gathered = dot_nn(pieces, jnp.concatenate([pick, pick, pick], axis=0))
        wx = both[0:NP]
        wy = both[NP : 2 * NP]
        wz = both[2 * NP : 3 * NP]
        acc = None
        for k in range(NP):
            line = None
            for j in range(NP):
                row = (k * NP + j) * NP
                term = gathered[row : row + NP] * wy[j : j + 1]
                line = term if line is None else line + term
            line = line * wz[k : k + 1]
            acc = line if acc is None else acc + line
        value = jnp.sum(acc * wx, axis=0, keepdims=True)
        rows.append(value[:, :128])
        rows.append(value[:, 128:])
    rows.append(jnp.zeros((128 - HALF, 128), f32))
    turned = jnp.concatenate(rows, axis=0).T
    mine = turned[:OWNERS] + pltpu.roll(turned[OWNERS:], 16, 1)
    ret_ref[...] = (
        pltpu.roll(mine, 1, 0)
        + pltpu.roll(mine, 32, 1)
        + pltpu.roll(pltpu.roll(mine, OWNERS - 1, 0), 64, 1)
    )


def deriv8(table, v):
    plus = [v[m] + v[7 - m] for m in range(4)]
    minus = [v[m] - v[7 - m] for m in range(4)]
    out = [None] * 8
    for a in range(4):
        even = odd = None
        for m in range(4):
            ce = 0.5 * (table[a, m] + table[a, 7 - m])
            co = 0.5 * (table[a, m] - table[a, 7 - m])
            te = plus[m] * float(ce)
            to = minus[m] * float(co)
            even = te if even is None else even + te
            odd = to if odd is None else odd + to
        out[a] = odd + even
        out[7 - a] = odd - even
    return out


def apply_line(v, coef):
    grad = deriv8(DERIV, v)
    return deriv8(DERIV.T, [grad[a] * coef(a) for a in range(8)])


def stiff_apply(v_ref, coef_ref, mass_ref, out_ref):
    def per_k(k, carry):
        base = pl.multiple_of(k * 64, 64)
        lines = [v_ref[pl.ds(base + i, 8, stride=8), :] for i in range(8)]
        res = apply_line(lines, lambda a: coef_ref[pl.ds(base + a * 8, 8), :])
        for i in range(8):
            out_ref[pl.ds(base + i, 8, stride=8), :] = res[i]
        rows = [v_ref[pl.ds(base + j * 8, 8), :] for j in range(8)]
        res = apply_line(rows, lambda b: coef_ref[pl.ds(512 + base + b * 8, 8), :])
        for j in range(8):
            at = pl.ds(base + j * 8, 8)
            out_ref[at, :] = out_ref[at, :] + res[j] + mass_ref[at, :] * rows[j]
        return carry

    lax.fori_loop(0, 8, per_k, 0)

    def per_j(j, carry):
        base = pl.multiple_of(j * 8, 8)
        cols = [v_ref[pl.ds(base + k * 64, 8), :] for k in range(8)]
        res = apply_line(cols, lambda c: coef_ref[pl.ds(1024 + base + c * 64, 8), :])
        for k in range(8):
            at = pl.ds(base + k * 64, 8)
            out_ref[at, :] = out_ref[at, :] + res[k]
        return carry

    lax.fori_loop(0, 8, per_j, 0)


def couple(high, low, shift, pos, count):
    lanes = high.shape[-1]
    next_low = pltpu.roll(low, lanes - shift, high.ndim - 1)
    prev_high = pltpu.roll(high, shift, high.ndim - 1)
    new_high = high + jnp.where(pos < count - 1, next_low, 0.0)
    new_low = low + jnp.where(pos > 0, prev_high, 0.0)
    return new_high, new_low


def in_plane(ref, count=NP):
    rows = count * NP
    col = iota((rows, 128), 1) % EX
    high, low = couple(
        ref[pl.ds(7, rows, stride=8), :], ref[pl.ds(0, rows, stride=8), :], 1, col, EX
    )
    ref[pl.ds(7, rows, stride=8), :] = high
    ref[pl.ds(0, rows, stride=8), :] = low
    line = (iota((8, 128), 1) // EX) % EY
    for k in range(count):
        high, low = couple(
            ref[k * 64 + 56 : k * 64 + 64], ref[k * 64 : k * 64 + 8], EX, line, EY
        )
        ref[k * 64 + 56 : k * 64 + 64] = high
        ref[k * 64 : k * 64 + 8] = low


def through(bottom, top, below, above):
    first = iota(bottom.shape, 1) < LAYER
    new_bottom = bottom + pltpu.roll(jnp.where(first, top, below), LAYER, 1)
    new_top = top + pltpu.roll(jnp.where(first, above, bottom), LAYER, 1)
    return new_bottom, new_top


def whole(bottom, ref, top):
    return jnp.concatenate([bottom, ref[64:448], top], axis=0)


def coupled(w_ref, below, above):
    bottom, top = through(w_ref[0:64], w_ref[448:512], below, above)
    return whole(bottom, w_ref, top)


def where_am_i():
    me = lax.axis_index("elem")
    last = lax.axis_size("elem") - 1
    return jnp.bitwise_and(me, 1) == 0, me > 0, me < last


def first_layer(shape):
    return iota(shape, 1) < LAYER


def pack(field, a_ref, b_ref, row, even):
    low, high = field[0:256], field[256:512]
    first = first_layer(low.shape)
    up = jnp.where(first, pltpu.roll(low, LAYER, 1), high)
    down = jnp.where(first, low, pltpu.roll(high, LAYER, 1))
    a_ref[row : row + 256] = jnp.where(even, up, down)
    b_ref[row : row + 256] = jnp.where(even, down, up)


def beside(a, b, place):
    even, has_below, has_above = place
    below = jnp.where(has_below, jnp.where(even, b, a), 0.0)
    above = jnp.where(has_above, jnp.where(even, a, b), 0.0)
    return below, above


def unpack(a_ref, b_ref, row, place, out_ref):
    below, above = beside(a_ref[row : row + 256], b_ref[row : row + 256], place)
    first = first_layer(below.shape)
    out_ref[0:256] = jnp.where(first, above, pltpu.roll(below, LAYER, 1))
    out_ref[256:512] = jnp.where(first, pltpu.roll(above, LAYER, 1), below)


def mirror(ghost_ref, bottom, top):
    first = first_layer(bottom.shape)
    ghost_ref[448:512] = jnp.where(first, ghost_ref[448:512], pltpu.roll(bottom, LAYER, 1))
    ghost_ref[0:64] = jnp.where(first, pltpu.roll(top, LAYER, 1), ghost_ref[0:64])


def message(raw_bottom, raw_top, inner_bottom, mid, inner_top):
    first = first_layer(raw_bottom.shape)
    return jnp.concatenate(
        [
            jnp.where(first, raw_bottom, inner_bottom),
            mid,
            jnp.where(first, inner_top, raw_top),
        ],
        axis=0,
    )


def ghost_apply(ghost_ref, third_ref, planes_ref, face_ref, out_ref):
    first = first_layer((8, 128))
    face_ref[...] = jnp.where(
        first_layer((64, 128)), ghost_ref[0:64], ghost_ref[448:512]
    )
    lines = [face_ref[pl.ds(i, 8, stride=8), :] for i in range(8)]
    res = apply_line(lines, lambda a: planes_ref[a * 8 : a * 8 + 8])
    for i in range(8):
        out_ref[pl.ds(i, 8, stride=8), :] = res[i]
    rows = [face_ref[j * 8 : j * 8 + 8] for j in range(8)]
    res = apply_line(rows, lambda b: planes_ref[64 + b * 8 : 72 + b * 8])
    ends = [
        jnp.where(first, float(DERIV[c, 0]), float(DERIV[c, 7])).astype(f32)
        for c in range(8)
    ]
    for j in range(8):
        total = out_ref[j * 8 : j * 8 + 8] + res[j]
        total = total + planes_ref[128 + j * 8 : 136 + j * 8] * rows[j]
        cols = [ghost_ref[k * 64 + j * 8 : k * 64 + j * 8 + 8] for k in range(8)]
        grad = deriv8(DERIV, cols)
        for c in range(8):
            at = c * 64 + j * 8
            total = total + grad[c] * third_ref[at : at + 8] * ends[c]
        out_ref[j * 8 : j * 8 + 8] = total
    in_plane(out_ref, 1)


def plain8(table, v):
    out = []
    for i in range(8):
        total = None
        for a in range(8):
            if table[a, i] == 0.0:
                continue
            term = v[a] * float(table[a, i])
            total = term if total is None else total + term
        out.append(total)
    return out


def take_lanes(x, index):
    return jnp.take_along_axis(
        x, jnp.broadcast_to(index, x.shape), axis=1, mode="promise_in_bounds"
    )


def local_diagonal(coef_ref, mass_ref, diag_ref):
    squared = DERIV * DERIV

    def per_k(k, carry):
        base = pl.multiple_of(k * 64, 64)
        res = plain8(squared, [coef_ref[pl.ds(base + a * 8, 8), :] for a in range(8)])
        for i in range(8):
            diag_ref[pl.ds(base + i, 8, stride=8), :] = res[i]
        res = plain8(squared, [coef_ref[pl.ds(512 + base + b * 8, 8), :] for b in range(8)])
        for j in range(8):
            at = pl.ds(base + j * 8, 8)
            diag_ref[at, :] = diag_ref[at, :] + res[j] + mass_ref[at, :]
        return carry

    lax.fori_loop(0, 8, per_k, 0)

    def per_j(j, carry):
        base = pl.multiple_of(j * 8, 8)
        res = plain8(squared, [coef_ref[pl.ds(1024 + base + c * 64, 8), :] for c in range(8)])
        for k in range(8):
            at = pl.ds(base + k * 64, 8)
            diag_ref[at, :] = diag_ref[at, :] + res[k]
        return carry

    lax.fori_loop(0, 8, per_j, 0)


PLANE_ROW = 512
BASIS_ROW = PLANE_ROW + 192
STATIC_ROW = BASIS_ROW + 256
MASS_ROW = STATIC_ROW + 256
SOLVE_ROW = MASS_ROW + 256
POINT_ROW = SOLVE_ROW + 512
GHOST_ROWS = POINT_ROW + 40


def prepare_kernel(
    owner_ref,
    slot_ref,
    weight_ref,
    order_ref,
    ids_ref,
    live_ref,
    stiff_hbm,
    mass_hbm,
    field_hbm,
    load_hbm,
    basis_hbm,
    inverse_hbm,
    send_ref,
    points_ref,
    coef_ref,
    mass_ref,
    start_ref,
    diag_ref,
    static_ref,
    basis_ref,
    solve_ref,
    a_ref,
    b_ref,
    stiff_in,
    mass_in,
    field_in,
    load_in,
    basis_in,
    inverse_in,
    tmp_ref,
    rank_ref,
    sems,
):
    copies = [
        pltpu.make_async_copy(src, dst, sems.at[n])
        for n, (src, dst) in enumerate(
            [
                (stiff_hbm, stiff_in),
                (mass_hbm, mass_in),
                (field_hbm, field_in),
                (load_hbm, load_in),
                (basis_hbm, basis_in),
                (inverse_hbm, inverse_in),
            ]
        )
    ]
    for copy in copies:
        copy.start()
    build_requests(owner_ref, slot_ref, weight_ref, send_ref, rank_ref)
    order = order_ref[...]
    match = (iota((128, 128), 0) == order).astype(f32)
    inv_f = jnp.sum(match.T * iota((128, 128), 0).astype(f32), axis=0, keepdims=True)
    inv = inv_f.astype(jnp.int32)
    rank = rank_ref[...]
    ids = ids_ref[...]
    live = iota((1, R_DEV), 1) < live_ref[0, 0]
    node = jnp.where(live, lax.shift_right_logical(ids, 7), -1)
    point_rows = [
        owner_ref[...].astype(f32),
        rank + jnp.where(rank >= float(HALF), float(16 - HALF), 0.0),
        node.astype(f32),
        jnp.bitwise_and(ids, 127).astype(f32),
    ]
    for n, row in enumerate(point_rows):
        for c in range(8):
            points_ref[n * 8 + c : n * 8 + c + 1] = row[:, c * 128 : c * 128 + 128]
    points_ref[32:40] = jnp.broadcast_to(inv_f, (8, 128))
    for copy in copies:
        copy.wait()
    tmp_ref[...] = take_lanes(stiff_in[0:512, :], inv)
    for k in range(8):
        for i in range(8):
            coef_ref[k * 64 + i * 8 : k * 64 + i * 8 + 8, :] = tmp_ref[
                pl.ds(k * 64 + i, 8, stride=8), :
            ]
    coef_ref[512:1536, :] = take_lanes(stiff_in[512:1536, :], inv)
    mass_ref[...] = take_lanes(mass_in[...], inv)
    start_ref[...] = take_lanes(field_in[...], inv)
    stiff_apply(start_ref, coef_ref, mass_ref, static_ref)
    static_ref[...] = take_lanes(load_in[...], inv) - static_ref[...]
    in_plane(static_ref)
    basis = dot_nn(match, basis_in[...], exact_mode)
    basis_ref[...] = basis
    solve = dot_nn(basis, inverse_in[...], exact_mode)
    solve_ref[...] = solve
    local_diagonal(coef_ref, mass_ref, diag_ref)
    in_plane(diag_ref)
    even = where_am_i()[0]
    zeros = jnp.zeros((64, 128), f32)
    pack(coef_ref[1024:1536, :], a_ref, b_ref, 0, even)
    pack(coupled(diag_ref, zeros, zeros), a_ref, b_ref, 256, even)
    pack(coupled(static_ref, zeros, zeros), a_ref, b_ref, STATIC_ROW, even)
    pack(mass_ref[...], a_ref, b_ref, MASS_ROW, even)
    rows = [
        (coef_ref[448:512], coef_ref[0:64]),
        (coef_ref[960:1024], coef_ref[512:576]),
        (mass_ref[448:512], mass_ref[0:64]),
    ]
    for c in range(NC // 128):
        cols = slice(c * 128, c * 128 + 128)
        rows.append((basis[LAYER:, cols], basis[:LAYER, cols]))
    for n, (up, down) in enumerate(rows):
        at = PLANE_ROW + n * 64
        a_ref[at : at + 64] = jnp.where(even, up, down)
        b_ref[at : at + 64] = jnp.where(even, down, up)
    for c in range(NC // 128):
        at = SOLVE_ROW + c * 128
        cols = solve[:, c * 128 : c * 128 + 128]
        a_ref[at : at + 128] = cols
        b_ref[at : at + 128] = cols
    a_ref[POINT_ROW:GHOST_ROWS] = points_ref[...]
    b_ref[POINT_ROW:GHOST_ROWS] = points_ref[...]


def scatter_points(points, answers):
    def row(n):
        return jnp.concatenate(
            [points[n * 8 + c : n * 8 + c + 1] for c in range(8)], axis=1
        ).astype(jnp.int32)

    owner, place, node, elem = row(0), row(1), row(2), row(3)
    hits = (iota((OWNERS, R_DEV), 0) == owner).astype(f32)
    picked = dot_nn(answers, hits, exact_mode)
    value = jnp.sum(
        jnp.where(iota((32, R_DEV), 0) == place, picked, 0.0), axis=0, keepdims=True
    )
    at_node = (iota((NODES, R_DEV), 0) == node).astype(f32).astype(bf16)
    at_elem = (iota((128, R_DEV), 0) == elem).astype(f32).astype(bf16)
    spread = jnp.concatenate([at_elem * piece for piece in split3(value)], axis=0)
    landed = dot_nt(at_node, spread)
    landed = landed[:, 0:128] + landed[:, 128:256] + landed[:, 256:384]
    return take_lanes(landed, points[32:33].astype(jnp.int32))


def ghost_assemble(ghost_ref, beyond_ref):
    in_plane(ghost_ref)
    in_plane(beyond_ref, 1)
    first = first_layer((64, 128))
    turned = pltpu.roll(beyond_ref[...], LAYER, 1)
    ghost_ref[0:64] = ghost_ref[0:64] + jnp.where(first, 0.0, turned)
    ghost_ref[448:512] = ghost_ref[448:512] + jnp.where(first, turned, 0.0)


def opening_half(
    place,
    base_ref,
    y_ref,
    cur_in,
    invd_ref,
    third_ref,
    ginvd_ref,
    planes_ref,
    coef_ref,
    mass_ref,
    res_ref,
    upd_ref,
    cur_ref,
    w_ref,
    a_out_ref,
    b_out_ref,
    ghost_ref,
    face_ref,
    side_ref,
):
    residual = coupled(y_ref, ghost_ref[448:512], ghost_ref[0:64])
    if base_ref is not None:
        residual = residual + base_ref[...]
    mirror(ghost_ref, residual[0:64], residual[448:512])
    invd = invd_ref[...]
    update = residual * invd * STEPS[0][1]
    upd_ref[...] = update
    ghost_ref[...] = ghost_ref[...] * ginvd_ref[...] * STEPS[0][1]
    stiff_apply(upd_ref, coef_ref, mass_ref, w_ref)
    in_plane(w_ref)
    ghost_apply(ghost_ref, third_ref, planes_ref, face_ref, side_ref)
    residual = residual - coupled(w_ref, side_ref[...], side_ref[...])
    res_ref[...] = residual
    alpha, beta = STEPS[1]
    second = alpha * update + beta * invd * residual
    upd_ref[...] = second
    cur_ref[...] = cur_in + (update + second)
    stiff_apply(upd_ref, coef_ref, mass_ref, w_ref)
    in_plane(w_ref)
    alpha, beta = STEPS[2]
    zeros = jnp.zeros((64, 128), f32)
    inner = alpha * upd_ref[...] + beta * invd_ref[...] * (
        res_ref[...] - coupled(w_ref, zeros, zeros)
    )
    pack(
        message(w_ref[0:64], w_ref[448:512], inner[0:64], inner[64:448], inner[448:512]),
        a_out_ref,
        b_out_ref,
        0,
        place[0],
    )


def start_kernel(
    ret_ref,
    points_ref,
    static_ref,
    diag_ref,
    cur_in_ref,
    ga_ref,
    gb_ref,
    coef_ref,
    mass_ref,
    res_ref,
    upd_ref,
    cur_ref,
    w_ref,
    a_out_ref,
    b_out_ref,
    invd_ref,
    third_ref,
    ginvd_ref,
    planes_ref,
    outer_ref,
    gmass_ref,
    beyond_mass_ref,
    y_ref,
    gstatic_ref,
    ghost_ref,
    face_ref,
    side_ref,
):
    place = where_am_i()
    even, has_below, has_above = place
    unpack(ga_ref, gb_ref, 0, place, third_ref)
    unpack(ga_ref, gb_ref, 256, place, ginvd_ref)
    unpack(ga_ref, gb_ref, STATIC_ROW, place, gstatic_ref)
    unpack(ga_ref, gb_ref, MASS_ROW, place, gmass_ref)
    diag = coupled(diag_ref, ginvd_ref[448:512], ginvd_ref[0:64])
    mirror(ginvd_ref, diag[0:64], diag[448:512])
    invd_ref[...] = 1.0 / diag
    gdiag = ginvd_ref[...]
    there = gdiag > 0.0
    ginvd_ref[...] = jnp.where(there, 1.0 / jnp.where(there, gdiag, 1.0), 0.0)
    span = slice(PLANE_ROW, BASIS_ROW)
    below, above = beside(ga_ref[span], gb_ref[span], place)
    planes_ref[...] = jnp.where(first_layer(below.shape), above, below)
    beyond_mass_ref[...] = jnp.where(first_layer((64, 128)), below[128:], above[128:])
    for c in range(NC // 128):
        at = BASIS_ROW + c * 64
        below, above = beside(ga_ref[at : at + 64], gb_ref[at : at + 64], place)
        outer_ref[0:64, c * 128 : c * 128 + 128] = below
        outer_ref[64:128, c * 128 : c * 128 + 128] = above
    answers = ret_ref[...].T
    y_ref[...] = scatter_points(points_ref[...], answers[32:64])
    in_plane(y_ref)
    y_ref[...] = y_ref[...] + static_ref[...]
    span = slice(POINT_ROW, GHOST_ROWS)
    below, above = beside(ga_ref[span], gb_ref[span], place)
    under = jnp.where(has_below, scatter_points(below, answers[0:32]), 0.0)
    over = jnp.where(has_above, scatter_points(above, answers[64:96]), 0.0)
    ghost_ref[...] = jnp.where(first_layer(over.shape), over, under)
    side_ref[...] = jnp.where(first_layer((64, 128)), under[448:512], over[0:64])
    ghost_assemble(ghost_ref, side_ref)
    ghost_ref[...] = ghost_ref[...] + gstatic_ref[...]
    opening_half(
        place,
        None,
        y_ref,
        cur_in_ref[...],
        invd_ref,
        third_ref,
        ginvd_ref,
        planes_ref,
        coef_ref,
        mass_ref,
        res_ref,
        upd_ref,
        cur_ref,
        w_ref,
        a_out_ref,
        b_out_ref,
        ghost_ref,
        face_ref,
        side_ref,
    )


def again_kernel(
    parts_ref,
    solve_ref,
    ga_ref,
    gb_ref,
    gmass_ref,
    beyond_mass_ref,
    y_in_ref,
    base_ref,
    cur_in_ref,
    a_ref,
    b_ref,
    invd_ref,
    third_ref,
    ginvd_ref,
    planes_ref,
    coef_ref,
    mass_ref,
    res_ref,
    upd_ref,
    cur_ref,
    w_ref,
    a_out_ref,
    b_out_ref,
    y_ref,
    gc_ref,
    ghost_ref,
    face_ref,
    side_ref,
):
    place = where_am_i()
    total = parts_ref[0:8]
    for n in range(1, OWNERS * NC // 1024):
        total = total + parts_ref[n * 8 : n * 8 + 8]
    total = total + pltpu.roll(total, 4, 0)
    both = None
    for c in range(NC // 128):
        row = jnp.broadcast_to(total[c : c + 1], (8, 128))
        at = SOLVE_ROW + c * 128
        rows = jnp.concatenate(
            [
                solve_ref[:, c * 128 : c * 128 + 128],
                ga_ref[at : at + 128],
                gb_ref[at : at + 128],
            ],
            axis=0,
        )
        term = dot_nt(row, rows, exact_mode)
        both = term if both is None else both + term
    correction = both[0:1, 0:128]
    below, above = beside(both[0:1, 128:256], both[0:1, 256:384], place)
    y_ref[...] = mass_ref[...] * correction
    in_plane(y_ref)
    y_ref[...] = -(y_ref[...] + y_in_ref[...])
    unpack(a_ref, b_ref, 0, place, ghost_ref)
    first = first_layer((1, 128))
    gc_ref[...] = gmass_ref[...] * jnp.where(first, above, below)
    side_ref[...] = beyond_mass_ref[...] * jnp.where(first, below, above)
    ghost_assemble(gc_ref, side_ref)
    ghost_ref[...] = ghost_ref[...] - gc_ref[...]
    opening_half(
        place,
        base_ref,
        y_ref,
        cur_in_ref[...] + correction,
        invd_ref,
        third_ref,
        ginvd_ref,
        planes_ref,
        coef_ref,
        mass_ref,
        res_ref,
        upd_ref,
        cur_ref,
        w_ref,
        a_out_ref,
        b_out_ref,
        ghost_ref,
        face_ref,
        side_ref,
    )


def closing_half(
    w_ref,
    res_ref,
    upd_ref,
    cur_ref,
    invd_ref,
    a_ref,
    b_ref,
    third_ref,
    planes_ref,
    coef_ref,
    mass_ref,
    work_ref,
    vec_ref,
    ghost_ref,
    face_ref,
    side_ref,
):
    unpack(a_ref, b_ref, 0, where_am_i(), ghost_ref)
    residual = res_ref[...] - coupled(w_ref, ghost_ref[448:512], ghost_ref[0:64])
    alpha, beta = STEPS[2]
    third = alpha * upd_ref[...] + beta * invd_ref[...] * residual
    vec_ref[...] = third
    mirror(ghost_ref, third[0:64], third[448:512])
    stiff_apply(vec_ref, coef_ref, mass_ref, work_ref)
    in_plane(work_ref)
    ghost_apply(ghost_ref, third_ref, planes_ref, face_ref, side_ref)
    residual = residual - coupled(work_ref, side_ref[...], side_ref[...])
    alpha, beta = STEPS[3]
    fourth = alpha * third + beta * invd_ref[...] * residual
    vec_ref[...] = fourth
    return residual, cur_ref[...] + (third + fourth)


def middle_kernel(
    w_ref,
    res_in_ref,
    upd_ref,
    cur_in_ref,
    invd_ref,
    a_ref,
    b_ref,
    third_ref,
    planes_ref,
    coef_ref,
    mass_ref,
    basis_ref,
    outer_ref,
    res_ref,
    cur_ref,
    w_out_ref,
    part_ref,
    a_out_ref,
    b_out_ref,
    vec_ref,
    *scratch,
):
    residual, current = closing_half(
        w_ref,
        res_in_ref,
        upd_ref,
        cur_in_ref,
        invd_ref,
        a_ref,
        b_ref,
        third_ref,
        planes_ref,
        coef_ref,
        mass_ref,
        w_out_ref,
        vec_ref,
        *scratch,
    )
    res_ref[...] = residual
    cur_ref[...] = current
    stiff_apply(vec_ref, coef_ref, mass_ref, w_out_ref)
    in_plane(w_out_ref)
    zeros = jnp.zeros((64, 128), f32)
    local = res_ref[...] - coupled(w_out_ref, zeros, zeros)
    pack(
        message(
            -w_out_ref[0:64], -w_out_ref[448:512], local[0:64], local[64:448], local[448:512]
        ),
        a_out_ref,
        b_out_ref,
        0,
        where_am_i()[0],
    )
    sums = jnp.sum(local, axis=0, keepdims=True)
    bottom = -jnp.sum(w_out_ref[0:64], axis=0, keepdims=True)
    top = -jnp.sum(w_out_ref[448:512], axis=0, keepdims=True)
    outer = jnp.where(first_layer((1, 128)), bottom, top)
    left = jnp.broadcast_to(jnp.concatenate([sums, outer], axis=1), (8, 256))
    right = jnp.concatenate([basis_ref[...], outer_ref[...]], axis=0)
    part = dot_nn(left, right, exact_mode)[0:1] * (1.0 / math.sqrt(NODES))
    blocks = [part[:, c * 128 : c * 128 + 128] for c in range(NC // 128)]
    eight = jnp.concatenate(blocks + blocks, axis=0)
    for n in range(OWNERS * NC // 1024):
        part_ref[n * 8 : n * 8 + 8] = eight


def last_kernel(*refs):
    inputs, (order_ref, out_ref), scratch = refs[:11], refs[11:13], refs[13:]
    current = closing_half(*inputs, *scratch)[1]
    out_ref[...] = take_lanes(current, order_ref[...])


def call(kernel, name, outs, *args, scratch=(), smem=(), far=(), copies=0):
    def space(n):
        if n in smem:
            return pltpu.SMEM
        return pltpu.HBM if n in far else pltpu.VMEM

    scratches = [pltpu.VMEM(s, f32) for s in scratch]
    if copies:
        scratches.append(pltpu.SemaphoreType.DMA((copies,)))
    return pl.pallas_call(
        kernel,
        name=name,
        out_shape=[jax.ShapeDtypeStruct(s, d) for s, d in outs],
        in_specs=[pl.BlockSpec(memory_space=space(n)) for n in range(len(args))],
        out_specs=[pl.BlockSpec(memory_space=pltpu.VMEM) for _ in outs],
        scratch_shapes=scratches,
        compiler_params=pltpu.CompilerParams(vmem_limit_bytes=20 << 20),
    )(*args)


FIELD = ((NODES, 128), f32)
PLANE = ((64, 128), f32)
LAYER_MSG = ((256, 128), f32)
GHOST_MSG = ((GHOST_ROWS, 128), f32)
GHOST_WORK = [(NODES, 128), (64, 128), (64, 128)]


def exchange(a, b):
    count = lax.axis_size("elem")
    pairs_a = [(i, i ^ 1) for i in range(count)]
    pairs_b = [(i, (i + (1 if i % 2 else -1)) % count) for i in range(count)]
    return lax.ppermute(a, "elem", pairs_a), lax.ppermute(b, "elem", pairs_b)


def per_device(
    pressure,
    load,
    stiffness,
    helm_mass,
    order_slots,
    recv_ids,
    donor_owner,
    donor_slot,
    interp_weights,
    live_count,
    coarse_basis,
    coarse_inverse,
):
    own_field = pressure.reshape(NODES, 128)
    order = order_slots.reshape(1, 128)
    owner = donor_owner.reshape(1, R_DEV)
    other_field = lax.ppermute(own_field, "sess", [(0, 1), (1, 0)])

    send, points, coef, mass, start, diag, static, basis, solve, ga, gb = call(
        prepare_kernel,
        "prepare",
        [
            ((OWNERS * ASK, 128), f32),
            ((40, 128), f32),
            ((3 * NODES, 128), f32),
            FIELD,
            FIELD,
            FIELD,
            FIELD,
            ((128, NC), f32),
            ((128, NC), f32),
            GHOST_MSG,
            GHOST_MSG,
        ],
        owner,
        donor_slot,
        interp_weights.reshape(3 * NP, R_DEV),
        order,
        recv_ids,
        live_count,
        stiffness.reshape(3 * NODES, 128),
        helm_mass.reshape(NODES, 128),
        own_field,
        load.reshape(NODES, 128),
        coarse_basis.reshape(128, NC),
        coarse_inverse.reshape(NC, NC),
        smem=(5,),
        far=(6, 7, 8, 9, 10, 11),
        scratch=[
            (3 * NODES, 128),
            (NODES, 128),
            (NODES, 128),
            (NODES, 128),
            (128, NC),
            (NC, NC),
            (NODES, 128),
            (1, R_DEV),
        ],
        copies=6,
    )
    ga, gb = exchange(ga, gb)
    received = lax.all_to_all(
        send.reshape(OWNERS, ASK, 128), "elem", split_axis=0, concat_axis=0, tiled=True
    )
    (answer,) = call(
        owner_kernel,
        "owner",
        [((OWNERS, 128), f32)],
        received.reshape(OWNERS * ASK, 128),
        other_field,
    )
    answered = lax.all_to_all(answer, "elem", split_axis=0, concat_axis=0, tiled=True)
    half = [FIELD, FIELD, FIELD, FIELD, LAYER_MSG, LAYER_MSG]
    res, upd, cur, w, a, b, invd, third, ginvd, planes, outer, gmass, beyond = call(
        start_kernel,
        "start",
        half + [FIELD, FIELD, FIELD, ((192, 128), f32), ((128, NC), f32), FIELD, PLANE],
        answered,
        points,
        static,
        diag,
        start,
        ga,
        gb,
        coef,
        mass,
        scratch=[(NODES, 128), (NODES, 128)] + GHOST_WORK,
    )
    a, b = exchange(a, b)
    res, cur, w, part, a, b = call(
        middle_kernel,
        "middle",
        [FIELD, FIELD, FIELD, ((OWNERS * NC // 128, 128), f32), LAYER_MSG, LAYER_MSG],
        w,
        res,
        upd,
        cur,
        invd,
        a,
        b,
        third,
        planes,
        coef,
        mass,
        basis,
        outer,
        scratch=[(NODES, 128)] + GHOST_WORK,
    )
    a, b = exchange(a, b)
    parts = lax.all_to_all(
        part.reshape(OWNERS, NC // 128, 128),
        "elem",
        split_axis=0,
        concat_axis=0,
        tiled=True,
    )
    res, upd, cur, w, a, b = call(
        again_kernel,
        "again",
        half,
        parts.reshape(OWNERS * NC // 128, 128),
        solve,
        ga,
        gb,
        gmass,
        beyond,
        w,
        res,
        cur,
        a,
        b,
        invd,
        third,
        ginvd,
        planes,
        coef,
        mass,
        scratch=[(NODES, 128), (NODES, 128)] + GHOST_WORK,
    )
    a, b = exchange(a, b)
    (out,) = call(
        last_kernel,
        "last",
        [FIELD],
        w,
        res,
        upd,
        cur,
        invd,
        a,
        b,
        third,
        planes,
        coef,
        mass,
        order,
        scratch=[(NODES, 128), (NODES, 128)] + GHOST_WORK,
    )
    return out.reshape(1, NP, NP, NP, 128)


def solution(mesh):
    return jax.shard_map(
        per_device,
        mesh=mesh,
        in_specs=(
            P("sess", None, None, None, "elem"),
            P("sess", None, None, None, "elem"),
            P("sess", None, None, None, None, "elem"),
            P("sess", None, None, None, "elem"),
            P("sess", "elem", None),
            P("sess", "elem"),
            P("sess", "elem", None),
            P("sess", "elem"),
            P("sess", None, "elem"),
            P("sess", "elem"),
            P("sess", "elem", None),
            P("sess", None, None),
        ),
        out_specs=P("sess", None, None, None, "elem"),
        check_vma=False,
    )
```

```python
import math

import jax
import jax.numpy as jnp
import numpy as np
from jax import lax
from jax.experimental import pallas as pl
from jax.experimental.pallas import tpu as pltpu
from jax.sharding import PartitionSpec as P

NP = 8
EX = 8
EY = 8
LAYER = EX * EY
NODES = NP**3
R_DEV = 1024
NC = 512
CHEB = 4
OWNERS = 64
COMPS = 32
HALF = 12
ASK = 8

exact_mode = lax.Precision.HIGHEST
spectrum_high = 8.0
spectrum_low = 0.8
f32 = jnp.float32
bf16 = jnp.bfloat16


def gll_derivative():
    x = np.array(
        [
            -1.0,
            -0.8717401485096066,
            -0.5917001814331423,
            -0.2092992179024789,
            0.2092992179024789,
            0.5917001814331423,
            0.8717401485096066,
            1.0,
        ]
    )
    legendre = (429.0 * x**7 - 693.0 * x**5 + 315.0 * x**3 - 35.0 * x) / 16.0
    distance = x[:, None] - x[None, :]
    same = np.eye(8, dtype=bool)
    table = legendre[:, None] / (legendre[None, :] * np.where(same, 1.0, distance))
    corner = np.zeros((8, 8))
    corner[0, 0] = -14.0
    corner[7, 7] = 14.0
    return np.where(same, corner, table).astype(np.float32).astype(np.float64)


DERIV = gll_derivative()


def chebyshev():
    center = 0.5 * (spectrum_high + spectrum_low)
    half_width = 0.5 * (spectrum_high - spectrum_low)
    sigma_ratio = center / half_width
    rho = 1.0 / sigma_ratio
    steps = [(0.0, 1.0 / center)]
    for _ in range(CHEB - 1):
        rho_next = 1.0 / (2.0 * sigma_ratio - rho)
        steps.append((rho_next * rho, 2.0 * rho_next / half_width))
        rho = rho_next
    return steps


STEPS = chebyshev()


def split3(x):
    hi = x.astype(bf16)
    rest = x - hi.astype(f32)
    mid = rest.astype(bf16)
    low = (rest - mid.astype(f32)).astype(bf16)
    return hi, mid, low


def dot_nn(a, b, precision=None):
    return lax.dot_general(
        a, b, (((1,), (0,)), ((), ())), precision=precision, preferred_element_type=f32
    )


def dot_nt(a, b, precision=None):
    return lax.dot_general(
        a, b, (((1,), (1,)), ((), ())), precision=precision, preferred_element_type=f32
    )


def iota(shape, axis):
    return lax.broadcasted_iota(jnp.int32, shape, axis)


def request_kernel(
    owner_ref, slot_ref, weight_ref, ids_ref, live_ref, send_ref, points_ref
):
    owner = owner_ref[...]
    hits = iota((OWNERS, R_DEV), 0) == owner
    hits_f = hits.astype(f32)
    hits_b = hits_f.astype(bf16)
    upper = (iota((128, 128), 0) < iota((128, 128), 1)).astype(f32).astype(bf16)
    carry = jnp.zeros((OWNERS, 1), f32)
    ranks = []
    for b in range(R_DEV // 128):
        cols = slice(b * 128, b * 128 + 128)
        block = hits_f[:, cols]
        count = dot_nn(hits_b[:, cols], upper) + carry
        ranks.append(jnp.sum(block * count, axis=0, keepdims=True))
        carry = carry + jnp.sum(block, axis=1, keepdims=True)
    rank = jnp.concatenate(ranks, axis=1)
    ids = ids_ref[...]
    live = iota((1, R_DEV), 1) < live_ref[0, 0]
    points_ref[0:1] = owner
    points_ref[1:2] = rank.astype(jnp.int32) + jnp.where(rank >= float(HALF), 16 - HALF, 0)
    points_ref[2:3] = jnp.where(live, lax.shift_right_logical(ids, 7), -1)
    points_ref[3:4] = jnp.bitwise_and(ids, 127)
    points_ref[4:8] = jnp.zeros((4, R_DEV), jnp.int32)
    payload = jnp.concatenate(
        [
            weight_ref[...],
            jnp.broadcast_to(slot_ref[...].astype(f32), (COMPS - 3 * NP, R_DEV)),
        ],
        axis=0,
    )
    pieces = split3(payload)
    total = None
    for piece in pieces:
        rows = [
            piece * (rank == float(m)).astype(f32).astype(bf16) for m in range(2 * HALF)
        ]
        part = dot_nt(hits_b, jnp.concatenate(rows, axis=0))
        total = part if total is None else total + part
    for c in range(ASK):
        if c < 2 * HALF * COMPS // 128:
            block = total[:, c * 128 : c * 128 + 128]
        else:
            block = jnp.zeros((OWNERS, 128), f32)
        send_ref[pl.ds(c, OWNERS, stride=ASK), :] = block


def owner_kernel(recv_ref, field_ref, ret_ref):
    cols = [recv_ref[pl.ds(c, OWNERS, stride=ASK), :] for c in range(6)]
    packed = jnp.concatenate(
        [jnp.concatenate(cols[:3], axis=1), jnp.concatenate(cols[3:], axis=1)], axis=0
    )
    comps = packed.T
    pieces = jnp.concatenate(split3(field_ref[...]), axis=1)
    rows = []
    for pair in range(HALF // 2):
        a = comps[(2 * pair) * COMPS : (2 * pair + 1) * COMPS]
        b = comps[(2 * pair + 1) * COMPS : (2 * pair + 2) * COMPS]
        both = jnp.concatenate([a, b], axis=1)
        slot = both[3 * NP : 3 * NP + 1].astype(jnp.int32)
        pick = (iota((128, 256), 0) == slot).astype(f32).astype(bf16)
        gathered = dot_nn(pieces, jnp.concatenate([pick, pick, pick], axis=0))
        wx = both[0:NP]
        wy = both[NP : 2 * NP]
        wz = both[2 * NP : 3 * NP]
        acc = None
        for k in range(NP):
            line = None
            for j in range(NP):
                row = (k * NP + j) * NP
                term = gathered[row : row + NP] * wy[j : j + 1]
                line = term if line is None else line + term
            line = line * wz[k : k + 1]
            acc = line if acc is None else acc + line
        value = jnp.sum(acc * wx, axis=0, keepdims=True)
        rows.append(value[:, :128])
        rows.append(value[:, 128:])
    rows.append(jnp.zeros((128 - HALF, 128), f32))
    turned = jnp.concatenate(rows, axis=0).T
    ret_ref[...] = turned[:OWNERS] + pltpu.roll(turned[OWNERS:], 16, 1)


def deriv8(table, v):
    plus = [v[m] + v[7 - m] for m in range(4)]
    minus = [v[m] - v[7 - m] for m in range(4)]
    out = [None] * 8
    for a in range(4):
        even = odd = None
        for m in range(4):
            ce = 0.5 * (table[a, m] + table[a, 7 - m])
            co = 0.5 * (table[a, m] - table[a, 7 - m])
            te = plus[m] * float(ce)
            to = minus[m] * float(co)
            even = te if even is None else even + te
            odd = to if odd is None else odd + to
        out[a] = odd + even
        out[7 - a] = odd - even
    return out


def apply_line(v, coef):
    grad = deriv8(DERIV, v)
    return deriv8(DERIV.T, [grad[a] * coef(a) for a in range(8)])


def stiff_apply(v_ref, coef_ref, mass_ref, out_ref):
    def per_k(k, carry):
        base = pl.multiple_of(k * 64, 64)
        lines = [v_ref[pl.ds(base + i, 8, stride=8), :] for i in range(8)]
        res = apply_line(lines, lambda a: coef_ref[pl.ds(base + a * 8, 8), :])
        for i in range(8):
            out_ref[pl.ds(base + i, 8, stride=8), :] = res[i]
        rows = [v_ref[pl.ds(base + j * 8, 8), :] for j in range(8)]
        res = apply_line(rows, lambda b: coef_ref[pl.ds(512 + base + b * 8, 8), :])
        for j in range(8):
            at = pl.ds(base + j * 8, 8)
            out_ref[at, :] = out_ref[at, :] + res[j] + mass_ref[at, :] * rows[j]
        return carry

    lax.fori_loop(0, 8, per_k, 0)

    def per_j(j, carry):
        base = pl.multiple_of(j * 8, 8)
        cols = [v_ref[pl.ds(base + k * 64, 8), :] for k in range(8)]
        res = apply_line(cols, lambda c: coef_ref[pl.ds(1024 + base + c * 64, 8), :])
        for k in range(8):
            at = pl.ds(base + k * 64, 8)
            out_ref[at, :] = out_ref[at, :] + res[k]
        return carry

    lax.fori_loop(0, 8, per_j, 0)


def couple(high, low, shift, pos, count):
    lanes = high.shape[-1]
    next_low = pltpu.roll(low, lanes - shift, high.ndim - 1)
    prev_high = pltpu.roll(high, shift, high.ndim - 1)
    new_high = high + jnp.where(pos < count - 1, next_low, 0.0)
    new_low = low + jnp.where(pos > 0, prev_high, 0.0)
    return new_high, new_low


def in_plane(ref, count=NP):
    rows = count * NP
    col = iota((rows, 128), 1) % EX
    high, low = couple(
        ref[pl.ds(7, rows, stride=8), :], ref[pl.ds(0, rows, stride=8), :], 1, col, EX
    )
    ref[pl.ds(7, rows, stride=8), :] = high
    ref[pl.ds(0, rows, stride=8), :] = low
    line = (iota((8, 128), 1) // EX) % EY
    for k in range(count):
        high, low = couple(
            ref[k * 64 + 56 : k * 64 + 64], ref[k * 64 : k * 64 + 8], EX, line, EY
        )
        ref[k * 64 + 56 : k * 64 + 64] = high
        ref[k * 64 : k * 64 + 8] = low


def through(bottom, top, below, above):
    first = iota(bottom.shape, 1) < LAYER
    new_bottom = bottom + pltpu.roll(jnp.where(first, top, below), LAYER, 1)
    new_top = top + pltpu.roll(jnp.where(first, above, bottom), LAYER, 1)
    return new_bottom, new_top


def whole(bottom, ref, top):
    return jnp.concatenate([bottom, ref[64:448], top], axis=0)


def coupled(w_ref, below, above):
    bottom, top = through(w_ref[0:64], w_ref[448:512], below, above)
    return whole(bottom, w_ref, top)


def where_am_i():
    me = lax.axis_index("elem")
    last = lax.axis_size("elem") - 1
    return jnp.bitwise_and(me, 1) == 0, me > 0, me < last


def first_layer(shape):
    return iota(shape, 1) < LAYER


def pack(up, down, a_ref, b_ref, row, even):
    half = up.shape[0] // 2
    first = first_layer((half, 128))
    up = jnp.where(first, pltpu.roll(up[:half], LAYER, 1), up[half:])
    down = jnp.where(first, down[:half], pltpu.roll(down[half:], LAYER, 1))
    a_ref[row : row + half] = jnp.where(even, up, down)
    b_ref[row : row + half] = jnp.where(even, down, up)


def beside(a, b, place):
    even, has_below, has_above = place
    below = jnp.where(has_below, jnp.where(even, b, a), 0.0)
    above = jnp.where(has_above, jnp.where(even, a, b), 0.0)
    return below, above


def unpack(a_ref, b_ref, row, half, place):
    below, above = beside(a_ref[row : row + half], b_ref[row : row + half], place)
    first = first_layer(below.shape)
    low = jnp.where(first, above, pltpu.roll(below, LAYER, 1))
    high = jnp.where(first, pltpu.roll(above, LAYER, 1), below)
    return jnp.concatenate([low, high], axis=0)


def mirror(ghost_ref, bottom, top):
    first = first_layer(bottom.shape)
    ghost_ref[448:512] = jnp.where(first, ghost_ref[448:512], pltpu.roll(bottom, LAYER, 1))
    ghost_ref[0:64] = jnp.where(first, pltpu.roll(top, LAYER, 1), ghost_ref[0:64])


def message(raw_bottom, raw_top, inner_bottom, mid, inner_top):
    first = first_layer(raw_bottom.shape)
    return jnp.concatenate(
        [
            jnp.where(first, raw_bottom, inner_bottom),
            mid,
            jnp.where(first, inner_top, raw_top),
        ],
        axis=0,
    )


def ghost_apply(ghost_ref, third_ref, planes_ref, face_ref, out_ref):
    first = first_layer((8, 128))
    face_ref[...] = jnp.where(
        first_layer((64, 128)), ghost_ref[0:64], ghost_ref[448:512]
    )
    lines = [face_ref[pl.ds(i, 8, stride=8), :] for i in range(8)]
    res = apply_line(lines, lambda a: planes_ref[a * 8 : a * 8 + 8])
    for i in range(8):
        out_ref[pl.ds(i, 8, stride=8), :] = res[i]
    rows = [face_ref[j * 8 : j * 8 + 8] for j in range(8)]
    res = apply_line(rows, lambda b: planes_ref[64 + b * 8 : 72 + b * 8])
    ends = [
        jnp.where(first, float(DERIV[c, 0]), float(DERIV[c, 7])).astype(f32)
        for c in range(8)
    ]
    for j in range(8):
        total = out_ref[j * 8 : j * 8 + 8] + res[j]
        total = total + planes_ref[128 + j * 8 : 136 + j * 8] * rows[j]
        cols = [ghost_ref[k * 64 + j * 8 : k * 64 + j * 8 + 8] for k in range(8)]
        grad = deriv8(DERIV, cols)
        for c in range(8):
            at = c * 64 + j * 8
            total = total + grad[c] * third_ref[at : at + 8] * ends[c]
        out_ref[j * 8 : j * 8 + 8] = total
    in_plane(out_ref, 1)


def plain8(table, v):
    out = []
    for i in range(8):
        total = None
        for a in range(8):
            if table[a, i] == 0.0:
                continue
            term = v[a] * float(table[a, i])
            total = term if total is None else total + term
        out.append(total)
    return out


def take_lanes(x, index):
    return jnp.take_along_axis(
        x, jnp.broadcast_to(index, x.shape), axis=1, mode="promise_in_bounds"
    )


def local_diagonal(coef_ref, mass_ref, diag_ref):
    squared = DERIV * DERIV

    def per_k(k, carry):
        base = pl.multiple_of(k * 64, 64)
        res = plain8(squared, [coef_ref[pl.ds(base + a * 8, 8), :] for a in range(8)])
        for i in range(8):
            diag_ref[pl.ds(base + i, 8, stride=8), :] = res[i]
        res = plain8(squared, [coef_ref[pl.ds(512 + base + b * 8, 8), :] for b in range(8)])
        for j in range(8):
            at = pl.ds(base + j * 8, 8)
            diag_ref[at, :] = diag_ref[at, :] + res[j] + mass_ref[at, :]
        return carry

    lax.fori_loop(0, 8, per_k, 0)

    def per_j(j, carry):
        base = pl.multiple_of(j * 8, 8)
        res = plain8(squared, [coef_ref[pl.ds(1024 + base + c * 64, 8), :] for c in range(8)])
        for k in range(8):
            at = pl.ds(base + k * 64, 8)
            diag_ref[at, :] = diag_ref[at, :] + res[k]
        return carry

    lax.fori_loop(0, 8, per_j, 0)


THIRD_ROW = 256
PLANE_ROW = THIRD_ROW + 256
BASIS_ROW = PLANE_ROW + 128
GHOST_ROWS = BASIS_ROW + 256


def setup_kernel(
    order_ref,
    stiff_hbm,
    mass_hbm,
    field_hbm,
    load_hbm,
    basis_hbm,
    inverse_hbm,
    coef_ref,
    mass_ref,
    start_ref,
    static_ref,
    diag_ref,
    invd_ref,
    inv_ref,
    basis_ref,
    solve_ref,
    a_ref,
    b_ref,
    stiff_in,
    mass_in,
    field_in,
    load_in,
    basis_in,
    inverse_in,
    tmp_ref,
    sems,
):
    copies = [
        pltpu.make_async_copy(src, dst, sems.at[n])
        for n, (src, dst) in enumerate(
            [
                (stiff_hbm, stiff_in),
                (mass_hbm, mass_in),
                (field_hbm, field_in),
                (load_hbm, load_in),
                (basis_hbm, basis_in),
                (inverse_hbm, inverse_in),
            ]
        )
    ]
    for copy in copies:
        copy.start()
    order = order_ref[...]
    match = (iota((128, 128), 0) == order).astype(f32)
    inv = jnp.sum(match.T * iota((128, 128), 0).astype(f32), axis=0, keepdims=True)
    inv = inv.astype(jnp.int32)
    inv_ref[...] = inv
    copies[0].wait()
    tmp_ref[...] = take_lanes(stiff_in[0:512, :], inv)
    for k in range(8):
        for i in range(8):
            coef_ref[k * 64 + i * 8 : k * 64 + i * 8 + 8, :] = tmp_ref[
                pl.ds(k * 64 + i, 8, stride=8), :
            ]
    coef_ref[512:1536, :] = take_lanes(stiff_in[512:1536, :], inv)
    for copy in copies[1:]:
        copy.wait()
    mass_ref[...] = take_lanes(mass_in[...], inv)
    start_ref[...] = take_lanes(field_in[...], inv)
    stiff_apply(start_ref, coef_ref, mass_ref, static_ref)
    static_ref[...] = take_lanes(load_in[...], inv) - static_ref[...]
    in_plane(static_ref)
    basis = dot_nn(match, basis_in[...], exact_mode)
    basis_ref[...] = basis
    solve_ref[...] = dot_nn(basis, inverse_in[...], exact_mode)
    local_diagonal(coef_ref, mass_ref, diag_ref)
    in_plane(diag_ref)
    zeros = jnp.zeros((64, 128), f32)
    invd_ref[...] = 1.0 / coupled(diag_ref, zeros, zeros)
    even = where_am_i()[0]
    third = coef_ref[1024:1536, :]
    pack(third, third, a_ref, b_ref, THIRD_ROW, even)
    tops = [coef_ref[448:512], coef_ref[960:1024], mass_ref[448:512], diag_ref[448:512]]
    bottoms = [coef_ref[0:64], coef_ref[512:576], mass_ref[0:64], diag_ref[0:64]]
    pack(
        jnp.concatenate(tops, axis=0),
        jnp.concatenate(bottoms, axis=0),
        a_ref,
        b_ref,
        PLANE_ROW,
        even,
    )
    for c in range(NC // 128):
        at = BASIS_ROW + c * 64
        up = basis[LAYER:, c * 128 : c * 128 + 128]
        down = basis[:LAYER, c * 128 : c * 128 + 128]
        a_ref[at : at + 64] = jnp.where(even, up, down)
        b_ref[at : at + 64] = jnp.where(even, down, up)
    a_ref[0:THIRD_ROW] = jnp.zeros((THIRD_ROW, 128), f32)
    b_ref[0:THIRD_ROW] = jnp.zeros((THIRD_ROW, 128), f32)


def send_first(y_ref, base, invd, a_ref, b_ref):
    zeros = jnp.zeros((64, 128), f32)
    inner = coupled(y_ref, zeros, zeros)
    if base is not None:
        inner = inner + base
    inner = inner * invd * STEPS[0][1]
    out = message(
        y_ref[0:64], y_ref[448:512], inner[0:64], inner[64:448], inner[448:512]
    )
    pack(out, out, a_ref, b_ref, 0, where_am_i()[0])


def source_kernel(
    ret_ref,
    points_ref,
    inv_ref,
    static_ref,
    invd_ref,
    a_in_ref,
    b_in_ref,
    y_ref,
    a_ref,
    b_ref,
):
    owner, place = points_ref[0:1], points_ref[1:2]
    node, elem = points_ref[2:3], points_ref[3:4]
    hits = (iota((OWNERS, R_DEV), 0) == owner).astype(f32)
    picked = dot_nn(ret_ref[...].T, hits, exact_mode)[0:32]
    value = jnp.sum(
        jnp.where(iota((32, R_DEV), 0) == place, picked, 0.0), axis=0, keepdims=True
    )
    at_node = (iota((NODES, R_DEV), 0) == node).astype(f32).astype(bf16)
    at_elem = (iota((128, R_DEV), 0) == elem).astype(f32).astype(bf16)
    spread = jnp.concatenate([at_elem * piece for piece in split3(value)], axis=0)
    landed = dot_nt(at_node, spread)
    landed = landed[:, 0:128] + landed[:, 128:256] + landed[:, 256:384]
    y_ref[...] = take_lanes(landed, inv_ref[...])
    in_plane(y_ref)
    y_ref[...] = y_ref[...] + static_ref[...]
    send_first(y_ref, None, invd_ref[...], a_ref, b_ref)
    a_ref[THIRD_ROW:] = a_in_ref[THIRD_ROW:]
    b_ref[THIRD_ROW:] = b_in_ref[THIRD_ROW:]


def opening_half(
    place,
    base_ref,
    y_ref,
    cur_in_ref,
    a_ref,
    b_ref,
    invd_ref,
    third_ref,
    planes_ref,
    coef_ref,
    mass_ref,
    res_ref,
    upd_ref,
    cur_ref,
    w_ref,
    a_out_ref,
    b_out_ref,
    ghost_ref,
    face_ref,
    side_ref,
):
    ghost_ref[...] = unpack(a_ref, b_ref, 0, 256, place)
    residual = coupled(y_ref, ghost_ref[448:512], ghost_ref[0:64])
    if base_ref is not None:
        residual = residual + base_ref[...]
    invd = invd_ref[...]
    update = residual * invd * STEPS[0][1]
    upd_ref[...] = update
    mirror(ghost_ref, update[0:64], update[448:512])
    stiff_apply(upd_ref, coef_ref, mass_ref, w_ref)
    in_plane(w_ref)
    ghost_apply(ghost_ref, third_ref, planes_ref, face_ref, side_ref)
    residual = residual - coupled(w_ref, side_ref[...], side_ref[...])
    res_ref[...] = residual
    alpha, beta = STEPS[1]
    second = alpha * update + beta * invd * residual
    upd_ref[...] = second
    cur_ref[...] = cur_in_ref[...] + (update + second)
    stiff_apply(upd_ref, coef_ref, mass_ref, w_ref)
    in_plane(w_ref)
    alpha, beta = STEPS[2]
    zeros = jnp.zeros((64, 128), f32)
    inner = alpha * upd_ref[...] + beta * invd_ref[...] * (
        res_ref[...] - coupled(w_ref, zeros, zeros)
    )
    out = message(
        w_ref[0:64], w_ref[448:512], inner[0:64], inner[64:448], inner[448:512]
    )
    pack(out, out, a_out_ref, b_out_ref, 0, place[0])


def start_kernel(
    y_ref,
    diag_ref,
    invd_in_ref,
    cur_in_ref,
    a_ref,
    b_ref,
    coef_ref,
    mass_ref,
    res_ref,
    upd_ref,
    cur_ref,
    w_ref,
    a_out_ref,
    b_out_ref,
    invd_ref,
    third_ref,
    planes_ref,
    outer_ref,
    *scratch,
):
    place = where_am_i()
    third_ref[...] = unpack(a_ref, b_ref, THIRD_ROW, 256, place)
    planes = unpack(a_ref, b_ref, PLANE_ROW, 128, place)
    planes_ref[...] = planes[0:192]
    bottom, top = through(
        diag_ref[0:64], diag_ref[448:512], planes[192:256], planes[192:256]
    )
    invd_ref[...] = whole(1.0 / bottom, invd_in_ref, 1.0 / top)
    for c in range(NC // 128):
        at = BASIS_ROW + c * 64
        below, above = beside(a_ref[at : at + 64], b_ref[at : at + 64], place)
        outer_ref[0:64, c * 128 : c * 128 + 128] = below
        outer_ref[64:128, c * 128 : c * 128 + 128] = above
    opening_half(
        place,
        None,
        y_ref,
        cur_in_ref,
        a_ref,
        b_ref,
        invd_ref,
        third_ref,
        planes_ref,
        coef_ref,
        mass_ref,
        res_ref,
        upd_ref,
        cur_ref,
        w_ref,
        a_out_ref,
        b_out_ref,
        *scratch,
    )


def again_kernel(*refs):
    opening_half(where_am_i(), *refs)


def closing_half(
    w_ref,
    res_ref,
    upd_ref,
    cur_ref,
    invd_ref,
    a_ref,
    b_ref,
    third_ref,
    planes_ref,
    coef_ref,
    mass_ref,
    work_ref,
    vec_ref,
    ghost_ref,
    face_ref,
    side_ref,
):
    ghost_ref[...] = unpack(a_ref, b_ref, 0, 256, where_am_i())
    residual = res_ref[...] - coupled(w_ref, ghost_ref[448:512], ghost_ref[0:64])
    alpha, beta = STEPS[2]
    third = alpha * upd_ref[...] + beta * invd_ref[...] * residual
    vec_ref[...] = third
    mirror(ghost_ref, third[0:64], third[448:512])
    stiff_apply(vec_ref, coef_ref, mass_ref, work_ref)
    in_plane(work_ref)
    ghost_apply(ghost_ref, third_ref, planes_ref, face_ref, side_ref)
    residual = residual - coupled(work_ref, side_ref[...], side_ref[...])
    alpha, beta = STEPS[3]
    fourth = alpha * third + beta * invd_ref[...] * residual
    vec_ref[...] = fourth
    return residual, cur_ref[...] + (third + fourth)


def middle_kernel(
    w_ref,
    res_in_ref,
    upd_ref,
    cur_in_ref,
    invd_ref,
    a_ref,
    b_ref,
    third_ref,
    planes_ref,
    coef_ref,
    mass_ref,
    basis_ref,
    outer_ref,
    res_ref,
    cur_ref,
    w_out_ref,
    part_ref,
    vec_ref,
    *scratch,
):
    residual, current = closing_half(
        w_ref,
        res_in_ref,
        upd_ref,
        cur_in_ref,
        invd_ref,
        a_ref,
        b_ref,
        third_ref,
        planes_ref,
        coef_ref,
        mass_ref,
        w_out_ref,
        vec_ref,
        *scratch,
    )
    res_ref[...] = residual
    cur_ref[...] = current
    stiff_apply(vec_ref, coef_ref, mass_ref, w_out_ref)
    in_plane(w_out_ref)
    zeros = jnp.zeros((64, 128), f32)
    local = res_ref[...] - coupled(w_out_ref, zeros, zeros)
    sums = jnp.sum(local, axis=0, keepdims=True)
    bottom = -jnp.sum(w_out_ref[0:64], axis=0, keepdims=True)
    top = -jnp.sum(w_out_ref[448:512], axis=0, keepdims=True)
    outer = jnp.where(first_layer((1, 128)), bottom, top)
    left = jnp.broadcast_to(jnp.concatenate([sums, outer], axis=1), (8, 256))
    right = jnp.concatenate([basis_ref[...], outer_ref[...]], axis=0)
    part = dot_nn(left, right, exact_mode)[0:1] * (1.0 / math.sqrt(NODES))
    blocks = [part[:, c * 128 : c * 128 + 128] for c in range(NC // 128)]
    eight = jnp.concatenate(blocks + blocks, axis=0)
    for n in range(OWNERS * NC // 1024):
        part_ref[n * 8 : n * 8 + 8] = eight


def restart_kernel(
    parts_ref,
    solve_ref,
    mass_ref,
    w_ref,
    base_ref,
    cur_in_ref,
    invd_ref,
    y_ref,
    cur_ref,
    a_ref,
    b_ref,
):
    total = parts_ref[0:8]
    for n in range(1, OWNERS * NC // 1024):
        total = total + parts_ref[n * 8 : n * 8 + 8]
    total = total + pltpu.roll(total, 4, 0)
    correction = None
    for c in range(NC // 128):
        row = jnp.broadcast_to(total[c : c + 1], (8, 128))
        term = dot_nt(row, solve_ref[:, c * 128 : c * 128 + 128], exact_mode)
        correction = term if correction is None else correction + term
    correction = correction[0:1]
    cur_ref[...] = cur_in_ref[...] + correction
    y_ref[...] = mass_ref[...] * correction
    in_plane(y_ref)
    y_ref[...] = -(y_ref[...] + w_ref[...])
    send_first(y_ref, base_ref[...], invd_ref[...], a_ref, b_ref)


def last_kernel(*refs):
    inputs, (order_ref, out_ref), scratch = refs[:11], refs[11:13], refs[13:]
    current = closing_half(*inputs, *scratch)[1]
    out_ref[...] = take_lanes(current, order_ref[...])


def call(kernel, name, outs, *args, scratch=(), smem=(), far=(), near=(), copies=0):
    def stay(x):
        return pltpu.with_memory_space_constraint(x, pltpu.HBM)

    def space(n):
        if n in smem:
            return pltpu.SMEM
        return pltpu.HBM if n in far else pltpu.VMEM

    scratches = [pltpu.VMEM(s, f32) for s in scratch]
    if copies:
        scratches.append(pltpu.SemaphoreType.DMA((copies,)))
    return pl.pallas_call(
        kernel,
        name=name,
        out_shape=[jax.ShapeDtypeStruct(s, d) for s, d in outs],
        in_specs=[pl.BlockSpec(memory_space=space(n)) for n in range(len(args))],
        out_specs=[pl.BlockSpec(memory_space=pltpu.VMEM) for _ in outs],
        scratch_shapes=scratches,
        compiler_params=pltpu.CompilerParams(vmem_limit_bytes=20 << 20),
    )(*[stay(x) if n in far + near else x for n, x in enumerate(args)])


FIELD = ((NODES, 128), f32)
LAYER_MSG = ((256, 128), f32)
GHOST_MSG = ((GHOST_ROWS, 128), f32)
GHOST_WORK = [(NODES, 128), (64, 128), (64, 128)]


def exchange(a, b):
    count = lax.axis_size("elem")
    pairs_a, pairs_b = [], []
    for d in range(2 * count):
        base, slab = d - d % count, d % count
        pairs_a.append((d, base + (slab ^ 1)))
        other = slab + (1 if slab % 2 else -1)
        inside = 0 <= other < count
        pairs_b.append((d, base + other if inside else (d + count) % (2 * count)))
    axes = ("sess", "elem")
    return lax.ppermute(a, axes, pairs_a), lax.ppermute(b, axes, pairs_b)


def per_device(
    pressure,
    load,
    stiffness,
    helm_mass,
    order_slots,
    recv_ids,
    donor_owner,
    donor_slot,
    interp_weights,
    live_count,
    coarse_basis,
    coarse_inverse,
):
    own_field = pressure.reshape(NODES, 128)
    order = order_slots.reshape(1, 128)
    owner = donor_owner.reshape(1, R_DEV)
    other_field = lax.ppermute(own_field, "sess", [(0, 1), (1, 0)])

    send, points = call(
        request_kernel,
        "request",
        [((OWNERS * ASK, 128), f32), ((8, R_DEV), jnp.int32)],
        owner,
        donor_slot,
        interp_weights.reshape(3 * NP, R_DEV),
        recv_ids,
        live_count,
        smem=(4,),
        near=(0, 1, 2, 3),
    )
    received = lax.all_to_all(
        send.reshape(OWNERS, ASK, 128), "elem", split_axis=0, concat_axis=0, tiled=True
    )
    coef, mass, start, static, diag, invd, inv, basis, solve, ga, gb = call(
        setup_kernel,
        "setup",
        [
            ((3 * NODES, 128), f32),
            FIELD,
            FIELD,
            FIELD,
            FIELD,
            FIELD,
            ((1, 128), jnp.int32),
            ((128, NC), f32),
            ((128, NC), f32),
            GHOST_MSG,
            GHOST_MSG,
        ],
        order,
        stiffness.reshape(3 * NODES, 128),
        helm_mass.reshape(NODES, 128),
        own_field,
        load.reshape(NODES, 128),
        coarse_basis.reshape(128, NC),
        coarse_inverse.reshape(NC, NC),
        near=(0,),
        far=(1, 2, 3, 4, 5, 6),
        scratch=[
            (3 * NODES, 128),
            (NODES, 128),
            (NODES, 128),
            (NODES, 128),
            (128, NC),
            (NC, NC),
            (NODES, 128),
        ],
        copies=6,
    )
    (answer,) = call(
        owner_kernel,
        "owner",
        [((OWNERS, 128), f32)],
        received.reshape(OWNERS * ASK, 128),
        other_field,
    )
    answered = lax.all_to_all(answer, "elem", split_axis=0, concat_axis=0, tiled=True)
    y, a, b = call(
        source_kernel,
        "source",
        [FIELD, GHOST_MSG, GHOST_MSG],
        answered,
        points,
        inv,
        static,
        invd,
        ga,
        gb,
    )
    a, b = exchange(a, b)
    half = [FIELD, FIELD, FIELD, FIELD, LAYER_MSG, LAYER_MSG]
    res, upd, cur, w, a, b, invd, third, planes, outer = call(
        start_kernel,
        "start",
        half + [FIELD, FIELD, ((192, 128), f32), ((128, NC), f32)],
        y,
        diag,
        invd,
        start,
        a,
        b,
        coef,
        mass,
        scratch=GHOST_WORK,
    )
    a, b = exchange(a, b)
    res, cur, w, part = call(
        middle_kernel,
        "middle",
        [FIELD, FIELD, FIELD, ((OWNERS * NC // 128, 128), f32)],
        w,
        res,
        upd,
        cur,
        invd,
        a,
        b,
        third,
        planes,
        coef,
        mass,
        basis,
        outer,
        scratch=[(NODES, 128)] + GHOST_WORK,
    )
    parts = lax.all_to_all(
        part.reshape(OWNERS, NC // 128, 128),
        "elem",
        split_axis=0,
        concat_axis=0,
        tiled=True,
    )
    y, cur, a, b = call(
        restart_kernel,
        "restart",
        [FIELD, FIELD, LAYER_MSG, LAYER_MSG],
        parts.reshape(OWNERS * NC // 128, 128),
        solve,
        mass,
        w,
        res,
        cur,
        invd,
    )
    a, b = exchange(a, b)
    res, upd, cur, w, a, b = call(
        again_kernel,
        "again",
        half,
        res,
        y,
        cur,
        a,
        b,
        invd,
        third,
        planes,
        coef,
        mass,
        scratch=GHOST_WORK,
    )
    a, b = exchange(a, b)
    (out,) = call(
        last_kernel,
        "last",
        [FIELD],
        w,
        res,
        upd,
        cur,
        invd,
        a,
        b,
        third,
        planes,
        coef,
        mass,
        order,
        scratch=[(NODES, 128), (NODES, 128)] + GHOST_WORK,
    )
    return out.reshape(1, NP, NP, NP, 128)


def solution(mesh):
    return jax.shard_map(
        per_device,
        mesh=mesh,
        in_specs=(
            P("sess", None, None, None, "elem"),
            P("sess", None, None, None, "elem"),
            P("sess", None, None, None, None, "elem"),
            P("sess", None, None, None, "elem"),
            P("sess", "elem", None),
            P("sess", "elem"),
            P("sess", "elem", None),
            P("sess", "elem"),
            P("sess", None, "elem"),
            P("sess", "elem"),
            P("sess", "elem", None),
            P("sess", None, None),
        ),
        out_specs=P("sess", None, None, None, "elem"),
        check_vma=False,
    )
```

```python
import math

import jax
import jax.numpy as jnp
import numpy as np
from jax import lax
from jax.experimental import pallas as pl
from jax.experimental.pallas import tpu as pltpu
from jax.sharding import PartitionSpec as P

NP = 8
EX = 8
EY = 8
LAYER = EX * EY
NODES = NP**3
R_DEV = 1024
NC = 512
CHEB = 4
OWNERS = 64
COMPS = 32
HALF = 12
ASK = 8

exact_mode = lax.Precision.HIGHEST
spectrum_high = 8.0
spectrum_low = 0.8
f32 = jnp.float32
bf16 = jnp.bfloat16


def gll_derivative():
    x = np.array(
        [
            -1.0,
            -0.8717401485096066,
            -0.5917001814331423,
            -0.2092992179024789,
            0.2092992179024789,
            0.5917001814331423,
            0.8717401485096066,
            1.0,
        ]
    )
    legendre = (429.0 * x**7 - 693.0 * x**5 + 315.0 * x**3 - 35.0 * x) / 16.0
    distance = x[:, None] - x[None, :]
    same = np.eye(8, dtype=bool)
    table = legendre[:, None] / (legendre[None, :] * np.where(same, 1.0, distance))
    corner = np.zeros((8, 8))
    corner[0, 0] = -14.0
    corner[7, 7] = 14.0
    return np.where(same, corner, table).astype(np.float32).astype(np.float64)


DERIV = gll_derivative()


def chebyshev():
    center = 0.5 * (spectrum_high + spectrum_low)
    half_width = 0.5 * (spectrum_high - spectrum_low)
    sigma_ratio = center / half_width
    rho = 1.0 / sigma_ratio
    steps = [(0.0, 1.0 / center)]
    for _ in range(CHEB - 1):
        rho_next = 1.0 / (2.0 * sigma_ratio - rho)
        steps.append((rho_next * rho, 2.0 * rho_next / half_width))
        rho = rho_next
    return steps


STEPS = chebyshev()


def split3(x):
    hi = x.astype(bf16)
    rest = x - hi.astype(f32)
    mid = rest.astype(bf16)
    low = (rest - mid.astype(f32)).astype(bf16)
    return hi, mid, low


def dot_nn(a, b, precision=None):
    return lax.dot_general(
        a, b, (((1,), (0,)), ((), ())), precision=precision, preferred_element_type=f32
    )


def dot_nt(a, b, precision=None):
    return lax.dot_general(
        a, b, (((1,), (1,)), ((), ())), precision=precision, preferred_element_type=f32
    )


def iota(shape, axis):
    return lax.broadcasted_iota(jnp.int32, shape, axis)


def request_kernel(owner_ref, slot_ref, weight_ref, send_ref, rank_ref):
    owner = owner_ref[...]
    hits = iota((OWNERS, R_DEV), 0) == owner
    hits_f = hits.astype(f32)
    hits_b = hits_f.astype(bf16)
    upper = (iota((128, 128), 0) < iota((128, 128), 1)).astype(f32).astype(bf16)
    carry = jnp.zeros((OWNERS, 1), f32)
    ranks = []
    for b in range(R_DEV // 128):
        cols = slice(b * 128, b * 128 + 128)
        block = hits_f[:, cols]
        count = dot_nn(hits_b[:, cols], upper) + carry
        ranks.append(jnp.sum(block * count, axis=0, keepdims=True))
        carry = carry + jnp.sum(block, axis=1, keepdims=True)
    rank = jnp.concatenate(ranks, axis=1)
    rank_ref[...] = rank
    payload = jnp.concatenate(
        [
            weight_ref[...],
            jnp.broadcast_to(slot_ref[...].astype(f32), (COMPS - 3 * NP, R_DEV)),
        ],
        axis=0,
    )
    pieces = split3(payload)
    total = None
    for piece in pieces:
        rows = [
            piece * (rank == float(m)).astype(f32).astype(bf16) for m in range(2 * HALF)
        ]
        part = dot_nt(hits_b, jnp.concatenate(rows, axis=0))
        total = part if total is None else total + part
    for c in range(ASK):
        if c < 2 * HALF * COMPS // 128:
            block = total[:, c * 128 : c * 128 + 128]
        else:
            block = jnp.zeros((OWNERS, 128), f32)
        send_ref[pl.ds(c, OWNERS, stride=ASK), :] = block


def owner_kernel(recv_ref, field_ref, before_ref, ret_ref, after_ref):
    cols = [recv_ref[pl.ds(c, OWNERS, stride=ASK), :] for c in range(6)]
    packed = jnp.concatenate(
        [jnp.concatenate(cols[:3], axis=1), jnp.concatenate(cols[3:], axis=1)], axis=0
    )
    comps = packed.T
    pieces = jnp.concatenate(split3(field_ref[...]), axis=1)
    rows = []
    for pair in range(HALF // 2):
        a = comps[(2 * pair) * COMPS : (2 * pair + 1) * COMPS]
        b = comps[(2 * pair + 1) * COMPS : (2 * pair + 2) * COMPS]
        both = jnp.concatenate([a, b], axis=1)
        slot = both[3 * NP : 3 * NP + 1].astype(jnp.int32)
        pick = (iota((128, 256), 0) == slot).astype(f32).astype(bf16)
        gathered = dot_nn(pieces, jnp.concatenate([pick, pick, pick], axis=0))
        wx = both[0:NP]
        wy = both[NP : 2 * NP]
        wz = both[2 * NP : 3 * NP]
        acc = None
        for k in range(NP):
            line = None
            for j in range(NP):
                row = (k * NP + j) * NP
                term = gathered[row : row + NP] * wy[j : j + 1]
                line = term if line is None else line + term
            line = line * wz[k : k + 1]
            acc = line if acc is None else acc + line
        value = jnp.sum(acc * wx, axis=0, keepdims=True)
        rows.append(value[:, :128])
        rows.append(value[:, 128:])
    rows.append(jnp.zeros((128 - HALF, 128), f32))
    turned = jnp.concatenate(rows, axis=0).T
    ret_ref[...] = turned[:OWNERS] + pltpu.roll(turned[OWNERS:], 16, 1)
    after_ref[...] = before_ref[...]


def deriv8(table, v):
    plus = [v[m] + v[7 - m] for m in range(4)]
    minus = [v[m] - v[7 - m] for m in range(4)]
    out = [None] * 8
    for a in range(4):
        even = odd = None
        for m in range(4):
            ce = 0.5 * (table[a, m] + table[a, 7 - m])
            co = 0.5 * (table[a, m] - table[a, 7 - m])
            te = plus[m] * float(ce)
            to = minus[m] * float(co)
            even = te if even is None else even + te
            odd = to if odd is None else odd + to
        out[a] = odd + even
        out[7 - a] = odd - even
    return out


def apply_line(v, coef):
    grad = deriv8(DERIV, v)
    return deriv8(DERIV.T, [grad[a] * coef(a) for a in range(8)])


def stiff_apply(v_ref, coef_ref, mass_ref, out_ref):
    def per_k(k, carry):
        base = pl.multiple_of(k * 64, 64)
        lines = [v_ref[pl.ds(base + i, 8, stride=8), :] for i in range(8)]
        res = apply_line(lines, lambda a: coef_ref[pl.ds(base + a * 8, 8), :])
        for i in range(8):
            out_ref[pl.ds(base + i, 8, stride=8), :] = res[i]
        rows = [v_ref[pl.ds(base + j * 8, 8), :] for j in range(8)]
        res = apply_line(rows, lambda b: coef_ref[pl.ds(512 + base + b * 8, 8), :])
        for j in range(8):
            at = pl.ds(base + j * 8, 8)
            out_ref[at, :] = out_ref[at, :] + res[j] + mass_ref[at, :] * rows[j]
        return carry

    lax.fori_loop(0, 8, per_k, 0)

    def per_j(j, carry):
        base = pl.multiple_of(j * 8, 8)
        cols = [v_ref[pl.ds(base + k * 64, 8), :] for k in range(8)]
        res = apply_line(cols, lambda c: coef_ref[pl.ds(1024 + base + c * 64, 8), :])
        for k in range(8):
            at = pl.ds(base + k * 64, 8)
            out_ref[at, :] = out_ref[at, :] + res[k]
        return carry

    lax.fori_loop(0, 8, per_j, 0)


def couple(high, low, shift, pos, count):
    lanes = high.shape[-1]
    next_low = pltpu.roll(low, lanes - shift, high.ndim - 1)
    prev_high = pltpu.roll(high, shift, high.ndim - 1)
    new_high = high + jnp.where(pos < count - 1, next_low, 0.0)
    new_low = low + jnp.where(pos > 0, prev_high, 0.0)
    return new_high, new_low


def in_plane(ref, count=NP):
    rows = count * NP
    col = iota((rows, 128), 1) % EX
    high, low = couple(
        ref[pl.ds(7, rows, stride=8), :], ref[pl.ds(0, rows, stride=8), :], 1, col, EX
    )
    ref[pl.ds(7, rows, stride=8), :] = high
    ref[pl.ds(0, rows, stride=8), :] = low
    line = (iota((8, 128), 1) // EX) % EY
    for k in range(count):
        high, low = couple(
            ref[k * 64 + 56 : k * 64 + 64], ref[k * 64 : k * 64 + 8], EX, line, EY
        )
        ref[k * 64 + 56 : k * 64 + 64] = high
        ref[k * 64 : k * 64 + 8] = low


def through(bottom, top, below, above):
    first = iota(bottom.shape, 1) < LAYER
    new_bottom = bottom + pltpu.roll(jnp.where(first, top, below), LAYER, 1)
    new_top = top + pltpu.roll(jnp.where(first, above, bottom), LAYER, 1)
    return new_bottom, new_top


def whole(bottom, ref, top):
    return jnp.concatenate([bottom, ref[64:448], top], axis=0)


def coupled(w_ref, below, above):
    bottom, top = through(w_ref[0:64], w_ref[448:512], below, above)
    return whole(bottom, w_ref, top)


def where_am_i():
    me = lax.axis_index("elem")
    last = lax.axis_size("elem") - 1
    return jnp.bitwise_and(me, 1) == 0, me > 0, me < last


def first_layer(shape):
    return iota(shape, 1) < LAYER


def pack(up, down, a_ref, b_ref, row, even):
    half = up.shape[0] // 2
    first = first_layer((half, 128))
    up = jnp.where(first, pltpu.roll(up[:half], LAYER, 1), up[half:])
    down = jnp.where(first, down[:half], pltpu.roll(down[half:], LAYER, 1))
    a_ref[row : row + half] = jnp.where(even, up, down)
    b_ref[row : row + half] = jnp.where(even, down, up)


def beside(a, b, place):
    even, has_below, has_above = place
    below = jnp.where(has_below, jnp.where(even, b, a), 0.0)
    above = jnp.where(has_above, jnp.where(even, a, b), 0.0)
    return below, above


def unpack(a_ref, b_ref, row, half, place):
    below, above = beside(a_ref[row : row + half], b_ref[row : row + half], place)
    first = first_layer(below.shape)
    low = jnp.where(first, above, pltpu.roll(below, LAYER, 1))
    high = jnp.where(first, pltpu.roll(above, LAYER, 1), below)
    return jnp.concatenate([low, high], axis=0)


def blend(bottom, top):
    return jnp.where(first_layer(bottom.shape), bottom, top)


def end_rows():
    first = first_layer((8, 128))
    return [
        jnp.where(first, float(DERIV[c, 0]), float(DERIV[c, 7])).astype(f32)
        for c in range(8)
    ]


def send_planes(w_ref, next_ref, coef_ref, work_ref, a_ref, b_ref, even):
    first = first_layer((8, 128))
    ends = end_rows()
    work_ref[0:64] = blend(w_ref[0:64], w_ref[448:512])
    for j in range(8):
        cols = [next_ref[k * 64 + j * 8 : k * 64 + j * 8 + 8] for k in range(8)]
        cols[0] = jnp.where(first, 0.0, cols[0])
        cols[7] = jnp.where(first, cols[7], 0.0)
        grad = deriv8(DERIV, cols)
        total = None
        for c in range(8):
            at = 1024 + c * 64 + j * 8
            term = grad[c] * coef_ref[at : at + 8] * ends[c]
            total = term if total is None else total + term
        work_ref[64 + j * 8 : 72 + j * 8] = total
    both = work_ref[...]
    pack(both, both, a_ref, b_ref, 0, even)


def ghost_side(update_ref, inner, planes_ref, face_ref, side_ref):
    face_ref[...] = pltpu.roll(blend(update_ref[0:64], update_ref[448:512]), LAYER, 1)
    lines = [face_ref[pl.ds(i, 8, stride=8), :] for i in range(8)]
    res = apply_line(lines, lambda a: planes_ref[a * 8 : a * 8 + 8])
    for i in range(8):
        side_ref[pl.ds(i, 8, stride=8), :] = res[i]
    rows = [face_ref[j * 8 : j * 8 + 8] for j in range(8)]
    res = apply_line(rows, lambda b: planes_ref[64 + b * 8 : 72 + b * 8])
    for j in range(8):
        at = slice(j * 8, j * 8 + 8)
        side_ref[at] = (
            side_ref[at]
            + res[j]
            + planes_ref[128 + j * 8 : 136 + j * 8] * rows[j]
            + inner[at]
        )
    in_plane(side_ref, 1)


def plain8(table, v):
    out = []
    for i in range(8):
        total = None
        for a in range(8):
            if table[a, i] == 0.0:
                continue
            term = v[a] * float(table[a, i])
            total = term if total is None else total + term
        out.append(total)
    return out


def take_lanes(x, index):
    return jnp.take_along_axis(
        x, jnp.broadcast_to(index, x.shape), axis=1, mode="promise_in_bounds"
    )


def local_diagonal(coef_ref, mass_ref, diag_ref):
    squared = DERIV * DERIV

    def per_k(k, carry):
        base = pl.multiple_of(k * 64, 64)
        res = plain8(squared, [coef_ref[pl.ds(base + a * 8, 8), :] for a in range(8)])
        for i in range(8):
            diag_ref[pl.ds(base + i, 8, stride=8), :] = res[i]
        res = plain8(squared, [coef_ref[pl.ds(512 + base + b * 8, 8), :] for b in range(8)])
        for j in range(8):
            at = pl.ds(base + j * 8, 8)
            diag_ref[at, :] = diag_ref[at, :] + res[j] + mass_ref[at, :]
        return carry

    lax.fori_loop(0, 8, per_k, 0)

    def per_j(j, carry):
        base = pl.multiple_of(j * 8, 8)
        res = plain8(squared, [coef_ref[pl.ds(1024 + base + c * 64, 8), :] for c in range(8)])
        for k in range(8):
            at = pl.ds(base + k * 64, 8)
            diag_ref[at, :] = diag_ref[at, :] + res[k]
        return carry

    lax.fori_loop(0, 8, per_j, 0)


PLANE_ROW = 64
BASIS_ROW = PLANE_ROW + 128
GHOST_ROWS = BASIS_ROW + 256


def setup_kernel(
    order_ref,
    stiff_hbm,
    mass_hbm,
    field_hbm,
    load_hbm,
    basis_hbm,
    inverse_hbm,
    coef_ref,
    mass_ref,
    start_ref,
    static_ref,
    diag_ref,
    invd_ref,
    inv_ref,
    basis_ref,
    solve_ref,
    ends_ref,
    stiff_in,
    mass_in,
    field_in,
    load_in,
    basis_in,
    inverse_in,
    tmp_ref,
    sems,
):
    copies = [
        pltpu.make_async_copy(src, dst, sems.at[n])
        for n, (src, dst) in enumerate(
            [
                (stiff_hbm, stiff_in),
                (mass_hbm, mass_in),
                (field_hbm, field_in),
                (load_hbm, load_in),
                (basis_hbm, basis_in),
                (inverse_hbm, inverse_in),
            ]
        )
    ]
    for copy in copies:
        copy.start()
    order = order_ref[...]
    match = (iota((128, 128), 0) == order).astype(f32)
    inv = jnp.sum(match.T * iota((128, 128), 0).astype(f32), axis=0, keepdims=True)
    inv = inv.astype(jnp.int32)
    inv_ref[...] = inv
    copies[0].wait()
    tmp_ref[...] = take_lanes(stiff_in[0:512, :], inv)
    for k in range(8):
        for i in range(8):
            coef_ref[k * 64 + i * 8 : k * 64 + i * 8 + 8, :] = tmp_ref[
                pl.ds(k * 64 + i, 8, stride=8), :
            ]
    coef_ref[512:1536, :] = take_lanes(stiff_in[512:1536, :], inv)
    for copy in copies[1:]:
        copy.wait()
    mass_ref[...] = take_lanes(mass_in[...], inv)
    start_ref[...] = take_lanes(field_in[...], inv)
    stiff_apply(start_ref, coef_ref, mass_ref, static_ref)
    static_ref[...] = take_lanes(load_in[...], inv) - static_ref[...]
    in_plane(static_ref)
    basis = dot_nn(match, basis_in[...], exact_mode)
    basis_ref[...] = basis
    solve_ref[...] = dot_nn(basis, inverse_in[...], exact_mode)
    local_diagonal(coef_ref, mass_ref, diag_ref)
    in_plane(diag_ref)
    zeros = jnp.zeros((64, 128), f32)
    invd_ref[...] = 1.0 / coupled(diag_ref, zeros, zeros)
    ends = end_rows()
    for j in range(8):
        total = None
        for c in range(8):
            at = 1024 + c * 64 + j * 8
            term = coef_ref[at : at + 8] * (ends[c] * ends[c])
            total = term if total is None else total + term
        tmp_ref[j * 8 : j * 8 + 8] = total
    ends_ref[0:64] = blend(coef_ref[0:64], coef_ref[448:512])
    ends_ref[64:128] = blend(coef_ref[512:576], coef_ref[960:1024])
    ends_ref[128:192] = blend(mass_ref[0:64], mass_ref[448:512]) + tmp_ref[0:64]
    ends_ref[192:256] = blend(diag_ref[0:64], diag_ref[448:512])


def send_first(y_ref, base, invd, coef_ref, next_ref, work_ref, a_ref, b_ref):
    zeros = jnp.zeros((64, 128), f32)
    inner = coupled(y_ref, zeros, zeros)
    if base is not None:
        inner = inner + base
    next_ref[...] = inner * invd * STEPS[0][1]
    send_planes(y_ref, next_ref, coef_ref, work_ref, a_ref, b_ref, where_am_i()[0])


def source_kernel(
    ret_ref,
    owner_ref,
    rank_ref,
    ids_ref,
    live_ref,
    inv_ref,
    static_ref,
    invd_ref,
    coef_ref,
    ends_ref,
    basis_ref,
    y_ref,
    a_ref,
    b_ref,
    next_ref,
    work_ref,
):
    rank = rank_ref[...].astype(jnp.int32)
    place = rank + jnp.where(rank >= HALF, 16 - HALF, 0)
    ids = ids_ref[...]
    live = iota((1, R_DEV), 1) < live_ref[0, 0]
    node = jnp.where(live, lax.shift_right_logical(ids, 7), -1)
    elem = jnp.bitwise_and(ids, 127)
    hits = (iota((OWNERS, R_DEV), 0) == owner_ref[...]).astype(f32)
    picked = dot_nn(ret_ref[...].T, hits, exact_mode)[0:32]
    value = jnp.sum(
        jnp.where(iota((32, R_DEV), 0) == place, picked, 0.0), axis=0, keepdims=True
    )
    at_node = (iota((NODES, R_DEV), 0) == node).astype(f32).astype(bf16)
    at_elem = (iota((128, R_DEV), 0) == elem).astype(f32).astype(bf16)
    spread = jnp.concatenate([at_elem * piece for piece in split3(value)], axis=0)
    landed = dot_nt(at_node, spread)
    landed = landed[:, 0:128] + landed[:, 128:256] + landed[:, 256:384]
    y_ref[...] = take_lanes(landed, inv_ref[...])
    in_plane(y_ref)
    y_ref[...] = y_ref[...] + static_ref[...]
    send_first(y_ref, None, invd_ref[...], coef_ref, next_ref, work_ref, a_ref, b_ref)
    even = where_am_i()[0]
    ends = ends_ref[...]
    pack(ends, ends, a_ref, b_ref, PLANE_ROW, even)
    for c in range(NC // 128):
        at = BASIS_ROW + c * 64
        up = basis_ref[LAYER:, c * 128 : c * 128 + 128]
        down = basis_ref[:LAYER, c * 128 : c * 128 + 128]
        a_ref[at : at + 64] = jnp.where(even, up, down)
        b_ref[at : at + 64] = jnp.where(even, down, up)


def opening_half(
    place,
    base_ref,
    y_ref,
    cur_in_ref,
    a_ref,
    b_ref,
    invd_ref,
    planes_ref,
    coef_ref,
    mass_ref,
    res_ref,
    upd_ref,
    cur_ref,
    w_ref,
    a_out_ref,
    b_out_ref,
    next_ref,
    work_ref,
    face_ref,
    side_ref,
):
    came = unpack(a_ref, b_ref, 0, 64, place)
    residual = coupled(y_ref, came[0:64], came[0:64])
    if base_ref is not None:
        residual = residual + base_ref[...]
    update = residual * invd_ref[...] * STEPS[0][1]
    upd_ref[...] = update
    ghost_side(upd_ref, came[64:128], planes_ref, face_ref, side_ref)
    stiff_apply(upd_ref, coef_ref, mass_ref, w_ref)
    in_plane(w_ref)
    residual = residual - coupled(w_ref, side_ref[...], side_ref[...])
    res_ref[...] = residual
    alpha, beta = STEPS[1]
    second = alpha * update + beta * invd_ref[...] * residual
    upd_ref[...] = second
    cur_ref[...] = cur_in_ref[...] + (update + second)
    stiff_apply(upd_ref, coef_ref, mass_ref, w_ref)
    in_plane(w_ref)
    alpha, beta = STEPS[2]
    zeros = jnp.zeros((64, 128), f32)
    next_ref[...] = alpha * upd_ref[...] + beta * invd_ref[...] * (
        res_ref[...] - coupled(w_ref, zeros, zeros)
    )
    send_planes(w_ref, next_ref, coef_ref, work_ref, a_out_ref, b_out_ref, place[0])


def start_kernel(
    y_ref,
    diag_ref,
    invd_in_ref,
    cur_in_ref,
    a_ref,
    b_ref,
    coef_ref,
    mass_ref,
    res_ref,
    upd_ref,
    cur_ref,
    w_ref,
    a_out_ref,
    b_out_ref,
    invd_ref,
    planes_ref,
    outer_ref,
    *scratch,
):
    place = where_am_i()
    planes = unpack(a_ref, b_ref, PLANE_ROW, 128, place)
    planes_ref[...] = planes[0:192]
    bottom, top = through(
        diag_ref[0:64], diag_ref[448:512], planes[192:256], planes[192:256]
    )
    invd_ref[...] = whole(1.0 / bottom, invd_in_ref, 1.0 / top)
    for c in range(NC // 128):
        at = BASIS_ROW + c * 64
        below, above = beside(a_ref[at : at + 64], b_ref[at : at + 64], place)
        outer_ref[0:64, c * 128 : c * 128 + 128] = below
        outer_ref[64:128, c * 128 : c * 128 + 128] = above
    opening_half(
        place,
        None,
        y_ref,
        cur_in_ref,
        a_ref,
        b_ref,
        invd_ref,
        planes_ref,
        coef_ref,
        mass_ref,
        res_ref,
        upd_ref,
        cur_ref,
        w_ref,
        a_out_ref,
        b_out_ref,
        *scratch,
    )


def again_kernel(*refs):
    opening_half(where_am_i(), *refs)


def closing_half(
    w_ref,
    res_ref,
    upd_ref,
    cur_ref,
    invd_ref,
    a_ref,
    b_ref,
    planes_ref,
    coef_ref,
    mass_ref,
    work_ref,
    vec_ref,
    face_ref,
    side_ref,
):
    came = unpack(a_ref, b_ref, 0, 64, where_am_i())
    residual = res_ref[...] - coupled(w_ref, came[0:64], came[0:64])
    alpha, beta = STEPS[2]
    third = alpha * upd_ref[...] + beta * invd_ref[...] * residual
    vec_ref[...] = third
    ghost_side(vec_ref, came[64:128], planes_ref, face_ref, side_ref)
    stiff_apply(vec_ref, coef_ref, mass_ref, work_ref)
    in_plane(work_ref)
    residual = residual - coupled(work_ref, side_ref[...], side_ref[...])
    alpha, beta = STEPS[3]
    fourth = alpha * third + beta * invd_ref[...] * residual
    vec_ref[...] = fourth
    return residual, cur_ref[...] + (third + fourth)


def middle_kernel(
    w_ref,
    res_in_ref,
    upd_ref,
    cur_in_ref,
    invd_ref,
    a_ref,
    b_ref,
    planes_ref,
    coef_ref,
    mass_ref,
    basis_ref,
    outer_ref,
    res_ref,
    cur_ref,
    w_out_ref,
    part_ref,
    vec_ref,
    *scratch,
):
    residual, current = closing_half(
        w_ref,
        res_in_ref,
        upd_ref,
        cur_in_ref,
        invd_ref,
        a_ref,
        b_ref,
            planes_ref,
        coef_ref,
        mass_ref,
        w_out_ref,
        vec_ref,
        *scratch,
    )
    res_ref[...] = residual
    cur_ref[...] = current
    stiff_apply(vec_ref, coef_ref, mass_ref, w_out_ref)
    in_plane(w_out_ref)
    zeros = jnp.zeros((64, 128), f32)
    local = res_ref[...] - coupled(w_out_ref, zeros, zeros)
    sums = jnp.sum(local, axis=0, keepdims=True)
    bottom = -jnp.sum(w_out_ref[0:64], axis=0, keepdims=True)
    top = -jnp.sum(w_out_ref[448:512], axis=0, keepdims=True)
    outer = jnp.where(first_layer((1, 128)), bottom, top)
    left = jnp.broadcast_to(jnp.concatenate([sums, outer], axis=1), (8, 256))
    right = jnp.concatenate([basis_ref[...], outer_ref[...]], axis=0)
    part = dot_nn(left, right, exact_mode)[0:1] * (1.0 / math.sqrt(NODES))
    blocks = [part[:, c * 128 : c * 128 + 128] for c in range(NC // 128)]
    eight = jnp.concatenate(blocks + blocks, axis=0)
    for n in range(OWNERS * NC // 1024):
        part_ref[n * 8 : n * 8 + 8] = eight


def restart_kernel(
    parts_ref,
    solve_ref,
    mass_ref,
    w_ref,
    base_ref,
    cur_in_ref,
    invd_ref,
    coef_ref,
    y_ref,
    cur_ref,
    a_ref,
    b_ref,
    next_ref,
    work_ref,
):
    total = parts_ref[0:8]
    for n in range(1, OWNERS * NC // 1024):
        total = total + parts_ref[n * 8 : n * 8 + 8]
    total = total + pltpu.roll(total, 4, 0)
    correction = None
    for c in range(NC // 128):
        row = jnp.broadcast_to(total[c : c + 1], (8, 128))
        term = dot_nt(row, solve_ref[:, c * 128 : c * 128 + 128], exact_mode)
        correction = term if correction is None else correction + term
    correction = correction[0:1]
    cur_ref[...] = cur_in_ref[...] + correction
    y_ref[...] = mass_ref[...] * correction
    in_plane(y_ref)
    y_ref[...] = -(y_ref[...] + w_ref[...])
    send_first(
        y_ref, base_ref[...], invd_ref[...], coef_ref, next_ref, work_ref, a_ref, b_ref
    )


def last_kernel(*refs):
    inputs, (order_ref, out_ref), scratch = refs[:10], refs[10:12], refs[12:]
    current = closing_half(*inputs, *scratch)[1]
    out_ref[...] = take_lanes(current, order_ref[...])


def call(kernel, name, outs, *args, scratch=(), smem=(), far=(), near=(), copies=0):
    def stay(x):
        return pltpu.with_memory_space_constraint(x, pltpu.HBM)

    def space(n):
        if n in smem:
            return pltpu.SMEM
        return pltpu.HBM if n in far else pltpu.VMEM

    scratches = [pltpu.VMEM(s, f32) for s in scratch]
    if copies:
        scratches.append(pltpu.SemaphoreType.DMA((copies,)))
    return pl.pallas_call(
        kernel,
        name=name,
        out_shape=[jax.ShapeDtypeStruct(s, d) for s, d in outs],
        in_specs=[pl.BlockSpec(memory_space=space(n)) for n in range(len(args))],
        out_specs=[pl.BlockSpec(memory_space=pltpu.VMEM) for _ in outs],
        scratch_shapes=scratches,
        compiler_params=pltpu.CompilerParams(vmem_limit_bytes=20 << 20),
    )(*[stay(x) if n in far + near else x for n, x in enumerate(args)])


FIELD = ((NODES, 128), f32)
SIDE_MSG = ((64, 128), f32)
GHOST_MSG = ((GHOST_ROWS, 128), f32)
SIDE_WORK = [(64, 128), (64, 128)]
SEND_WORK = [(NODES, 128), (128, 128)]


def exchange(a, b):
    count = lax.axis_size("elem")
    pairs_a, pairs_b = [], []
    for d in range(2 * count):
        base, slab = d - d % count, d % count
        pairs_a.append((d, base + (slab ^ 1)))
        other = slab + (1 if slab % 2 else -1)
        inside = 0 <= other < count
        pairs_b.append((d, base + other if inside else (d + count) % (2 * count)))
    axes = ("sess", "elem")
    return lax.ppermute(a, axes, pairs_a), lax.ppermute(b, axes, pairs_b)


def per_device(
    pressure,
    load,
    stiffness,
    helm_mass,
    order_slots,
    recv_ids,
    donor_owner,
    donor_slot,
    interp_weights,
    live_count,
    coarse_basis,
    coarse_inverse,
):
    own_field = pressure.reshape(NODES, 128)
    order = order_slots.reshape(1, 128)
    owner = donor_owner.reshape(1, R_DEV)
    other_field = lax.ppermute(own_field, "sess", [(0, 1), (1, 0)])

    send, rank = call(
        request_kernel,
        "request",
        [((OWNERS * ASK, 128), f32), ((1, R_DEV), f32)],
        owner,
        donor_slot,
        interp_weights.reshape(3 * NP, R_DEV),
        near=(0, 1, 2),
    )
    received = lax.all_to_all(
        send.reshape(OWNERS, ASK, 128), "elem", split_axis=0, concat_axis=0, tiled=True
    )
    coef, mass, start, static, diag, invd, inv, basis, solve, ends = call(
        setup_kernel,
        "setup",
        [
            ((3 * NODES, 128), f32),
            FIELD,
            FIELD,
            FIELD,
            FIELD,
            FIELD,
            ((1, 128), jnp.int32),
            ((128, NC), f32),
            ((128, NC), f32),
            ((256, 128), f32),
        ],
        order,
        stiffness.reshape(3 * NODES, 128),
        helm_mass.reshape(NODES, 128),
        own_field,
        load.reshape(NODES, 128),
        coarse_basis.reshape(128, NC),
        coarse_inverse.reshape(NC, NC),
        near=(0,),
        far=(1, 2, 3, 4, 5, 6),
        scratch=[
            (3 * NODES, 128),
            (NODES, 128),
            (NODES, 128),
            (NODES, 128),
            (128, NC),
            (NC, NC),
            (NODES, 128),
        ],
        copies=6,
    )
    answer, inv = call(
        owner_kernel,
        "owner",
        [((OWNERS, 128), f32), ((1, 128), jnp.int32)],
        received.reshape(OWNERS * ASK, 128),
        other_field,
        inv,
    )
    answered = lax.all_to_all(answer, "elem", split_axis=0, concat_axis=0, tiled=True)
    y, a, b = call(
        source_kernel,
        "source",
        [FIELD, GHOST_MSG, GHOST_MSG],
        answered,
        owner,
        rank,
        recv_ids,
        live_count,
        inv,
        static,
        invd,
        coef,
        ends,
        basis,
        smem=(4,),
        near=(1, 3),
        scratch=SEND_WORK,
    )
    a, b = exchange(a, b)
    half = [FIELD, FIELD, FIELD, FIELD, SIDE_MSG, SIDE_MSG]
    res, upd, cur, w, a, b, invd, planes, outer = call(
        start_kernel,
        "start",
        half + [FIELD, ((192, 128), f32), ((128, NC), f32)],
        y,
        diag,
        invd,
        start,
        a,
        b,
        coef,
        mass,
        scratch=SEND_WORK + SIDE_WORK,
    )
    a, b = exchange(a, b)
    res, cur, w, part = call(
        middle_kernel,
        "middle",
        [FIELD, FIELD, FIELD, ((OWNERS * NC // 128, 128), f32)],
        w,
        res,
        upd,
        cur,
        invd,
        a,
        b,
        planes,
        coef,
        mass,
        basis,
        outer,
        scratch=[(NODES, 128)] + SIDE_WORK,
    )
    parts = lax.all_to_all(
        part.reshape(OWNERS, NC // 128, 128),
        "elem",
        split_axis=0,
        concat_axis=0,
        tiled=True,
    )
    y, cur, a, b = call(
        restart_kernel,
        "restart",
        [FIELD, FIELD, SIDE_MSG, SIDE_MSG],
        parts.reshape(OWNERS * NC // 128, 128),
        solve,
        mass,
        w,
        res,
        cur,
        invd,
        coef,
        scratch=SEND_WORK,
    )
    a, b = exchange(a, b)
    res, upd, cur, w, a, b = call(
        again_kernel,
        "again",
        half,
        res,
        y,
        cur,
        a,
        b,
        invd,
        planes,
        coef,
        mass,
        scratch=SEND_WORK + SIDE_WORK,
    )
    a, b = exchange(a, b)
    (out,) = call(
        last_kernel,
        "last",
        [FIELD],
        w,
        res,
        upd,
        cur,
        invd,
        a,
        b,
        planes,
        coef,
        mass,
        order,
        near=(10,),
        scratch=[(NODES, 128), (NODES, 128)] + SIDE_WORK,
    )
    return out.reshape(1, NP, NP, NP, 128)


def solution(mesh):
    return jax.shard_map(
        per_device,
        mesh=mesh,
        in_specs=(
            P("sess", None, None, None, "elem"),
            P("sess", None, None, None, "elem"),
            P("sess", None, None, None, None, "elem"),
            P("sess", None, None, None, "elem"),
            P("sess", "elem", None),
            P("sess", "elem"),
            P("sess", "elem", None),
            P("sess", "elem"),
            P("sess", None, "elem"),
            P("sess", "elem"),
            P("sess", "elem", None),
            P("sess", None, None),
        ),
        out_specs=P("sess", None, None, None, "elem"),
        check_vma=False,
    )
```

```python
import math

import jax
import jax.numpy as jnp
import numpy as np
from jax import lax
from jax.experimental import pallas as pl
from jax.experimental.pallas import tpu as pltpu
from jax.sharding import PartitionSpec as P


NP = 8
EX = 8
EY = 8
LAYER = EX * EY
NODES = NP**3
R_DEV = 1024
NC = 512
CHEB = 4
OWNERS = 64
COMPS = 32
HALF = 12
ASK = 8

exact_mode = lax.Precision.HIGHEST
spectrum_high = 8.0
spectrum_low = 0.8
f32 = jnp.float32
bf16 = jnp.bfloat16


def gll_derivative():
    x = np.array(
        [
            -1.0,
            -0.8717401485096066,
            -0.5917001814331423,
            -0.2092992179024789,
            0.2092992179024789,
            0.5917001814331423,
            0.8717401485096066,
            1.0,
        ]
    )
    legendre = (429.0 * x**7 - 693.0 * x**5 + 315.0 * x**3 - 35.0 * x) / 16.0
    distance = x[:, None] - x[None, :]
    same = np.eye(8, dtype=bool)
    table = legendre[:, None] / (legendre[None, :] * np.where(same, 1.0, distance))
    corner = np.zeros((8, 8))
    corner[0, 0] = -14.0
    corner[7, 7] = 14.0
    return np.where(same, corner, table).astype(np.float32).astype(np.float64)


DERIV = gll_derivative()


def chebyshev():
    center = 0.5 * (spectrum_high + spectrum_low)
    half_width = 0.5 * (spectrum_high - spectrum_low)
    sigma_ratio = center / half_width
    rho = 1.0 / sigma_ratio
    steps = [(0.0, 1.0 / center)]
    for _ in range(CHEB - 1):
        rho_next = 1.0 / (2.0 * sigma_ratio - rho)
        steps.append((rho_next * rho, 2.0 * rho_next / half_width))
        rho = rho_next
    return steps


STEPS = chebyshev()


def split3(x):
    hi = x.astype(bf16)
    rest = x - hi.astype(f32)
    mid = rest.astype(bf16)
    low = (rest - mid.astype(f32)).astype(bf16)
    return hi, mid, low


def dot_nn(a, b, precision=None):
    return lax.dot_general(
        a, b, (((1,), (0,)), ((), ())), precision=precision, preferred_element_type=f32
    )


def dot_nt(a, b, precision=None):
    return lax.dot_general(
        a, b, (((1,), (1,)), ((), ())), precision=precision, preferred_element_type=f32
    )


def iota(shape, axis):
    return lax.broadcasted_iota(jnp.int32, shape, axis)


def request_kernel(
    owner_ref, slot_ref, weight_ref, ids_ref, send_ref, rank_ref, owner_out_ref, ids_out_ref
):
    owner = owner_ref[...]
    hits = iota((OWNERS, R_DEV), 0) == owner
    hits_f = hits.astype(f32)
    hits_b = hits_f.astype(bf16)
    upper = (iota((128, 128), 0) < iota((128, 128), 1)).astype(f32).astype(bf16)
    carry = jnp.zeros((OWNERS, 1), f32)
    ranks = []
    for b in range(R_DEV // 128):
        cols = slice(b * 128, b * 128 + 128)
        block = hits_f[:, cols]
        count = dot_nn(hits_b[:, cols], upper) + carry
        ranks.append(jnp.sum(block * count, axis=0, keepdims=True))
        carry = carry + jnp.sum(block, axis=1, keepdims=True)
    rank = jnp.concatenate(ranks, axis=1)
    rank_ref[...] = rank
    owner_out_ref[...] = owner
    ids_out_ref[...] = ids_ref[...]
    payload = jnp.concatenate(
        [
            weight_ref[...],
            jnp.broadcast_to(slot_ref[...].astype(f32), (COMPS - 3 * NP, R_DEV)),
        ],
        axis=0,
    )
    pieces = split3(payload)
    total = None
    for piece in pieces:
        rows = [
            piece * (rank == float(m)).astype(f32).astype(bf16) for m in range(2 * HALF)
        ]
        part = dot_nt(hits_b, jnp.concatenate(rows, axis=0))
        total = part if total is None else total + part
    for c in range(ASK):
        if c < 2 * HALF * COMPS // 128:
            block = total[:, c * 128 : c * 128 + 128]
        else:
            block = jnp.zeros((OWNERS, 128), f32)
        send_ref[pl.ds(c, OWNERS, stride=ASK), :] = block


def owner_kernel(recv_ref, field_ref, before_ref, ret_ref, after_ref):
    cols = [recv_ref[pl.ds(c, OWNERS, stride=ASK), :] for c in range(6)]
    packed = jnp.concatenate(
        [jnp.concatenate(cols[:3], axis=1), jnp.concatenate(cols[3:], axis=1)], axis=0
    )
    comps = packed.T
    pieces = jnp.concatenate(split3(field_ref[...]), axis=1)
    rows = []
    for pair in range(HALF // 2):
        a = comps[(2 * pair) * COMPS : (2 * pair + 1) * COMPS]
        b = comps[(2 * pair + 1) * COMPS : (2 * pair + 2) * COMPS]
        both = jnp.concatenate([a, b], axis=1)
        slot = both[3 * NP : 3 * NP + 1].astype(jnp.int32)
        pick = (iota((128, 256), 0) == slot).astype(f32).astype(bf16)
        gathered = dot_nn(pieces, jnp.concatenate([pick, pick, pick], axis=0))
        wx = both[0:NP]
        wy = both[NP : 2 * NP]
        wz = both[2 * NP : 3 * NP]
        acc = None
        for k in range(NP):
            line = None
            for j in range(NP):
                row = (k * NP + j) * NP
                term = gathered[row : row + NP] * wy[j : j + 1]
                line = term if line is None else line + term
            line = line * wz[k : k + 1]
            acc = line if acc is None else acc + line
        value = jnp.sum(acc * wx, axis=0, keepdims=True)
        rows.append(value[:, :128])
        rows.append(value[:, 128:])
    rows.append(jnp.zeros((128 - HALF, 128), f32))
    turned = jnp.concatenate(rows, axis=0).T
    ret_ref[...] = turned[:OWNERS] + pltpu.roll(turned[OWNERS:], 16, 1)
    after_ref[...] = before_ref[...]


def deriv8(table, v):
    plus = [v[m] + v[7 - m] for m in range(4)]
    minus = [v[m] - v[7 - m] for m in range(4)]
    out = [None] * 8
    for a in range(4):
        even = odd = None
        for m in range(4):
            ce = 0.5 * (table[a, m] + table[a, 7 - m])
            co = 0.5 * (table[a, m] - table[a, 7 - m])
            te = plus[m] * float(ce)
            to = minus[m] * float(co)
            even = te if even is None else even + te
            odd = to if odd is None else odd + to
        out[a] = odd + even
        out[7 - a] = odd - even
    return out


def apply_line(v, coef):
    grad = deriv8(DERIV, v)
    return deriv8(DERIV.T, [grad[a] * coef(a) for a in range(8)])


def stiff_apply(v_ref, coef_ref, mass_ref, out_ref):
    def per_k(k, carry):
        base = pl.multiple_of(k * 64, 64)
        lines = [v_ref[pl.ds(base + i, 8, stride=8), :] for i in range(8)]
        res = apply_line(lines, lambda a: coef_ref[pl.ds(base + a * 8, 8), :])
        for i in range(8):
            out_ref[pl.ds(base + i, 8, stride=8), :] = res[i]
        rows = [v_ref[pl.ds(base + j * 8, 8), :] for j in range(8)]
        res = apply_line(rows, lambda b: coef_ref[pl.ds(512 + base + b * 8, 8), :])
        for j in range(8):
            at = pl.ds(base + j * 8, 8)
            out_ref[at, :] = out_ref[at, :] + res[j] + mass_ref[at, :] * rows[j]
        return carry

    lax.fori_loop(0, 8, per_k, 0)

    def per_j(j, carry):
        base = pl.multiple_of(j * 8, 8)
        cols = [v_ref[pl.ds(base + k * 64, 8), :] for k in range(8)]
        res = apply_line(cols, lambda c: coef_ref[pl.ds(1024 + base + c * 64, 8), :])
        for k in range(8):
            at = pl.ds(base + k * 64, 8)
            out_ref[at, :] = out_ref[at, :] + res[k]
        return carry

    lax.fori_loop(0, 8, per_j, 0)


def couple(high, low, shift, pos, count):
    lanes = high.shape[-1]
    next_low = pltpu.roll(low, lanes - shift, high.ndim - 1)
    prev_high = pltpu.roll(high, shift, high.ndim - 1)
    new_high = high + jnp.where(pos < count - 1, next_low, 0.0)
    new_low = low + jnp.where(pos > 0, prev_high, 0.0)
    return new_high, new_low


def in_plane(ref, count=NP):
    rows = count * NP
    col = iota((rows, 128), 1) % EX
    high, low = couple(
        ref[pl.ds(7, rows, stride=8), :], ref[pl.ds(0, rows, stride=8), :], 1, col, EX
    )
    ref[pl.ds(7, rows, stride=8), :] = high
    ref[pl.ds(0, rows, stride=8), :] = low
    line = (iota((8, 128), 1) // EX) % EY
    for k in range(count):
        high, low = couple(
            ref[k * 64 + 56 : k * 64 + 64], ref[k * 64 : k * 64 + 8], EX, line, EY
        )
        ref[k * 64 + 56 : k * 64 + 64] = high
        ref[k * 64 : k * 64 + 8] = low


def through(bottom, top, below, above):
    first = iota(bottom.shape, 1) < LAYER
    new_bottom = bottom + pltpu.roll(jnp.where(first, top, below), LAYER, 1)
    new_top = top + pltpu.roll(jnp.where(first, above, bottom), LAYER, 1)
    return new_bottom, new_top


def whole(bottom, ref, top):
    return jnp.concatenate([bottom, ref[64:448], top], axis=0)


def coupled(w_ref, below, above):
    bottom, top = through(w_ref[0:64], w_ref[448:512], below, above)
    return whole(bottom, w_ref, top)


def where_am_i():
    me = lax.axis_index("elem")
    last = lax.axis_size("elem") - 1
    return jnp.bitwise_and(me, 1) == 0, me > 0, me < last


def first_layer(shape):
    return iota(shape, 1) < LAYER


def pack(up, down, a_ref, b_ref, row, even):
    half = up.shape[0] // 2
    first = first_layer((half, 128))
    up = jnp.where(first, pltpu.roll(up[:half], LAYER, 1), up[half:])
    down = jnp.where(first, down[:half], pltpu.roll(down[half:], LAYER, 1))
    a_ref[row : row + half] = jnp.where(even, up, down)
    b_ref[row : row + half] = jnp.where(even, down, up)


def beside(a, b, place):
    even, has_below, has_above = place
    below = jnp.where(has_below, jnp.where(even, b, a), 0.0)
    above = jnp.where(has_above, jnp.where(even, a, b), 0.0)
    return below, above


def unpack(a_ref, b_ref, row, half, place):
    below, above = beside(a_ref[row : row + half], b_ref[row : row + half], place)
    first = first_layer(below.shape)
    low = jnp.where(first, above, pltpu.roll(below, LAYER, 1))
    high = jnp.where(first, pltpu.roll(above, LAYER, 1), below)
    return jnp.concatenate([low, high], axis=0)


def blend(bottom, top):
    return jnp.where(first_layer(bottom.shape), bottom, top)


def end_rows():
    first = first_layer((8, 128))
    return [
        jnp.where(first, float(DERIV[c, 0]), float(DERIV[c, 7])).astype(f32)
        for c in range(8)
    ]


def send_planes(w_ref, next_ref, coef_ref, work_ref, a_ref, b_ref, even):
    first = first_layer((8, 128))
    ends = end_rows()
    work_ref[0:64] = blend(w_ref[0:64], w_ref[448:512])
    for j in range(8):
        cols = [next_ref[k * 64 + j * 8 : k * 64 + j * 8 + 8] for k in range(8)]
        cols[0] = jnp.where(first, 0.0, cols[0])
        cols[7] = jnp.where(first, cols[7], 0.0)
        grad = deriv8(DERIV, cols)
        total = None
        for c in range(8):
            at = 1024 + c * 64 + j * 8
            term = grad[c] * coef_ref[at : at + 8] * ends[c]
            total = term if total is None else total + term
        work_ref[64 + j * 8 : 72 + j * 8] = total
    both = work_ref[...]
    pack(both, both, a_ref, b_ref, 0, even)


def ghost_side(update_ref, inner, planes_ref, face_ref, side_ref):
    face_ref[...] = pltpu.roll(blend(update_ref[0:64], update_ref[448:512]), LAYER, 1)
    lines = [face_ref[pl.ds(i, 8, stride=8), :] for i in range(8)]
    res = apply_line(lines, lambda a: planes_ref[a * 8 : a * 8 + 8])
    for i in range(8):
        side_ref[pl.ds(i, 8, stride=8), :] = res[i]
    rows = [face_ref[j * 8 : j * 8 + 8] for j in range(8)]
    res = apply_line(rows, lambda b: planes_ref[64 + b * 8 : 72 + b * 8])
    for j in range(8):
        at = slice(j * 8, j * 8 + 8)
        side_ref[at] = (
            side_ref[at]
            + res[j]
            + planes_ref[128 + j * 8 : 136 + j * 8] * rows[j]
            + inner[at]
        )
    in_plane(side_ref, 1)


def plain8(table, v):
    out = []
    for i in range(8):
        total = None
        for a in range(8):
            if table[a, i] == 0.0:
                continue
            term = v[a] * float(table[a, i])
            total = term if total is None else total + term
        out.append(total)
    return out


def take_lanes(x, index):
    return jnp.take_along_axis(
        x, jnp.broadcast_to(index, x.shape), axis=1, mode="promise_in_bounds"
    )


def local_diagonal(coef_ref, mass_ref, diag_ref):
    squared = DERIV * DERIV

    def per_k(k, carry):
        base = pl.multiple_of(k * 64, 64)
        res = plain8(squared, [coef_ref[pl.ds(base + a * 8, 8), :] for a in range(8)])
        for i in range(8):
            diag_ref[pl.ds(base + i, 8, stride=8), :] = res[i]
        res = plain8(squared, [coef_ref[pl.ds(512 + base + b * 8, 8), :] for b in range(8)])
        for j in range(8):
            at = pl.ds(base + j * 8, 8)
            diag_ref[at, :] = diag_ref[at, :] + res[j] + mass_ref[at, :]
        return carry

    lax.fori_loop(0, 8, per_k, 0)

    def per_j(j, carry):
        base = pl.multiple_of(j * 8, 8)
        res = plain8(squared, [coef_ref[pl.ds(1024 + base + c * 64, 8), :] for c in range(8)])
        for k in range(8):
            at = pl.ds(base + k * 64, 8)
            diag_ref[at, :] = diag_ref[at, :] + res[k]
        return carry

    lax.fori_loop(0, 8, per_j, 0)


BASIS_ROW = 128
GHOST_ROWS = BASIS_ROW + 256


def setup_kernel(
    order_ref,
    stiff_hbm,
    mass_hbm,
    field_hbm,
    load_hbm,
    basis_hbm,
    inverse_hbm,
    coef_ref,
    mass_ref,
    start_ref,
    static_ref,
    diag_ref,
    invd_ref,
    inv_ref,
    basis_ref,
    solve_ref,
    order_out_ref,
    a_ref,
    b_ref,
    stiff_in,
    mass_in,
    field_in,
    load_in,
    basis_in,
    inverse_in,
    tmp_ref,
    sems,
):
    copies = [
        pltpu.make_async_copy(src, dst, sems.at[n])
        for n, (src, dst) in enumerate(
            [
                (stiff_hbm, stiff_in),
                (mass_hbm, mass_in),
                (field_hbm, field_in),
                (load_hbm, load_in),
                (basis_hbm, basis_in),
                (inverse_hbm, inverse_in),
            ]
        )
    ]
    for copy in copies:
        copy.start()
    order = order_ref[...]
    match = (iota((128, 128), 0) == order).astype(f32)
    inv = jnp.sum(match.T * iota((128, 128), 0).astype(f32), axis=0, keepdims=True)
    inv = inv.astype(jnp.int32)
    inv_ref[...] = inv
    order_out_ref[...] = order
    copies[0].wait()
    tmp_ref[...] = take_lanes(stiff_in[0:512, :], inv)
    for k in range(8):
        for i in range(8):
            coef_ref[k * 64 + i * 8 : k * 64 + i * 8 + 8, :] = tmp_ref[
                pl.ds(k * 64 + i, 8, stride=8), :
            ]
    coef_ref[512:1536, :] = take_lanes(stiff_in[512:1536, :], inv)
    for copy in copies[1:]:
        copy.wait()
    mass_ref[...] = take_lanes(mass_in[...], inv)
    start_ref[...] = take_lanes(field_in[...], inv)
    stiff_apply(start_ref, coef_ref, mass_ref, static_ref)
    static_ref[...] = take_lanes(load_in[...], inv) - static_ref[...]
    in_plane(static_ref)
    basis = dot_nn(match, basis_in[...], exact_mode)
    basis_ref[...] = basis
    solve_ref[...] = dot_nn(basis, inverse_in[...], exact_mode)
    local_diagonal(coef_ref, mass_ref, diag_ref)
    in_plane(diag_ref)
    zeros = jnp.zeros((64, 128), f32)
    invd_ref[...] = 1.0 / coupled(diag_ref, zeros, zeros)
    ends = end_rows()
    for j in range(8):
        total = None
        for c in range(8):
            at = 1024 + c * 64 + j * 8
            term = coef_ref[at : at + 8] * (ends[c] * ends[c])
            total = term if total is None else total + term
        tmp_ref[j * 8 : j * 8 + 8] = total
    planes = jnp.concatenate(
        [
            blend(coef_ref[0:64], coef_ref[448:512]),
            blend(coef_ref[512:576], coef_ref[960:1024]),
            blend(mass_ref[0:64], mass_ref[448:512]) + tmp_ref[0:64],
            blend(diag_ref[0:64], diag_ref[448:512]),
        ],
        axis=0,
    )
    even = where_am_i()[0]
    pack(planes, planes, a_ref, b_ref, 0, even)
    for c in range(NC // 128):
        at = BASIS_ROW + c * 64
        up = basis[LAYER:, c * 128 : c * 128 + 128]
        down = basis[:LAYER, c * 128 : c * 128 + 128]
        a_ref[at : at + 64] = jnp.where(even, up, down)
        b_ref[at : at + 64] = jnp.where(even, down, up)


def send_first(y_ref, base, invd, coef_ref, next_ref, work_ref, a_ref, b_ref):
    zeros = jnp.zeros((64, 128), f32)
    inner = coupled(y_ref, zeros, zeros)
    if base is not None:
        inner = inner + base
    next_ref[...] = inner * invd * STEPS[0][1]
    send_planes(y_ref, next_ref, coef_ref, work_ref, a_ref, b_ref, where_am_i()[0])


def source_kernel(
    ret_ref,
    owner_ref,
    rank_ref,
    ids_ref,
    live_ref,
    inv_ref,
    static_ref,
    invd_ref,
    coef_ref,
    y_ref,
    a_ref,
    b_ref,
    next_ref,
    work_ref,
):
    rank = rank_ref[...].astype(jnp.int32)
    place = rank + jnp.where(rank >= HALF, 16 - HALF, 0)
    ids = ids_ref[...]
    live = iota((1, R_DEV), 1) < live_ref[0, 0]
    node = jnp.where(live, lax.shift_right_logical(ids, 7), -1)
    elem = jnp.bitwise_and(ids, 127)
    hits = (iota((OWNERS, R_DEV), 0) == owner_ref[...]).astype(f32)
    picked = dot_nn(ret_ref[...].T, hits, exact_mode)[0:32]
    value = jnp.sum(
        jnp.where(iota((32, R_DEV), 0) == place, picked, 0.0), axis=0, keepdims=True
    )
    at_node = (iota((NODES, R_DEV), 0) == node).astype(f32).astype(bf16)
    at_elem = (iota((128, R_DEV), 0) == elem).astype(f32).astype(bf16)
    spread = jnp.concatenate([at_elem * piece for piece in split3(value)], axis=0)
    landed = dot_nt(at_node, spread)
    landed = landed[:, 0:128] + landed[:, 128:256] + landed[:, 256:384]
    y_ref[...] = take_lanes(landed, inv_ref[...])
    in_plane(y_ref)
    y_ref[...] = y_ref[...] + static_ref[...]
    send_first(y_ref, None, invd_ref[...], coef_ref, next_ref, work_ref, a_ref, b_ref)


def opening_half(
    place,
    base_ref,
    y_ref,
    cur_in_ref,
    a_ref,
    b_ref,
    invd_ref,
    planes_ref,
    coef_ref,
    mass_ref,
    res_ref,
    upd_ref,
    cur_ref,
    w_ref,
    a_out_ref,
    b_out_ref,
    next_ref,
    work_ref,
    face_ref,
    side_ref,
):
    came = unpack(a_ref, b_ref, 0, 64, place)
    residual = coupled(y_ref, came[0:64], came[0:64])
    if base_ref is not None:
        residual = residual + base_ref[...]
    update = residual * invd_ref[...] * STEPS[0][1]
    upd_ref[...] = update
    ghost_side(upd_ref, came[64:128], planes_ref, face_ref, side_ref)
    stiff_apply(upd_ref, coef_ref, mass_ref, w_ref)
    in_plane(w_ref)
    residual = residual - coupled(w_ref, side_ref[...], side_ref[...])
    res_ref[...] = residual
    alpha, beta = STEPS[1]
    second = alpha * update + beta * invd_ref[...] * residual
    upd_ref[...] = second
    cur_ref[...] = cur_in_ref[...] + (update + second)
    stiff_apply(upd_ref, coef_ref, mass_ref, w_ref)
    in_plane(w_ref)
    alpha, beta = STEPS[2]
    zeros = jnp.zeros((64, 128), f32)
    next_ref[...] = alpha * upd_ref[...] + beta * invd_ref[...] * (
        res_ref[...] - coupled(w_ref, zeros, zeros)
    )
    send_planes(w_ref, next_ref, coef_ref, work_ref, a_out_ref, b_out_ref, place[0])


def start_kernel(
    y_ref,
    diag_ref,
    invd_in_ref,
    cur_in_ref,
    a_ref,
    b_ref,
    ga_ref,
    gb_ref,
    coef_ref,
    mass_ref,
    res_ref,
    upd_ref,
    cur_ref,
    w_ref,
    a_out_ref,
    b_out_ref,
    invd_ref,
    planes_ref,
    *scratch,
):
    place = where_am_i()
    planes = unpack(ga_ref, gb_ref, 0, 128, place)
    planes_ref[...] = planes[0:192]
    bottom, top = through(
        diag_ref[0:64], diag_ref[448:512], planes[192:256], planes[192:256]
    )
    invd_ref[...] = whole(1.0 / bottom, invd_in_ref, 1.0 / top)
    opening_half(
        place,
        None,
        y_ref,
        cur_in_ref,
        a_ref,
        b_ref,
        invd_ref,
        planes_ref,
        coef_ref,
        mass_ref,
        res_ref,
        upd_ref,
        cur_ref,
        w_ref,
        a_out_ref,
        b_out_ref,
        *scratch,
    )


def again_kernel(*refs):
    opening_half(where_am_i(), *refs)


def closing_half(
    w_ref,
    res_ref,
    upd_ref,
    cur_ref,
    invd_ref,
    a_ref,
    b_ref,
    planes_ref,
    coef_ref,
    mass_ref,
    work_ref,
    vec_ref,
    face_ref,
    side_ref,
):
    came = unpack(a_ref, b_ref, 0, 64, where_am_i())
    residual = res_ref[...] - coupled(w_ref, came[0:64], came[0:64])
    alpha, beta = STEPS[2]
    third = alpha * upd_ref[...] + beta * invd_ref[...] * residual
    vec_ref[...] = third
    ghost_side(vec_ref, came[64:128], planes_ref, face_ref, side_ref)
    stiff_apply(vec_ref, coef_ref, mass_ref, work_ref)
    in_plane(work_ref)
    residual = residual - coupled(work_ref, side_ref[...], side_ref[...])
    alpha, beta = STEPS[3]
    fourth = alpha * third + beta * invd_ref[...] * residual
    vec_ref[...] = fourth
    return residual, cur_ref[...] + (third + fourth)


def middle_kernel(
    w_ref,
    res_in_ref,
    upd_ref,
    cur_in_ref,
    invd_ref,
    a_ref,
    b_ref,
    planes_ref,
    coef_ref,
    mass_ref,
    basis_ref,
    ga_ref,
    gb_ref,
    res_ref,
    cur_ref,
    w_out_ref,
    part_ref,
    vec_ref,
    *scratch,
):
    residual, current = closing_half(
        w_ref,
        res_in_ref,
        upd_ref,
        cur_in_ref,
        invd_ref,
        a_ref,
        b_ref,
            planes_ref,
        coef_ref,
        mass_ref,
        w_out_ref,
        vec_ref,
        *scratch,
    )
    res_ref[...] = residual
    cur_ref[...] = current
    stiff_apply(vec_ref, coef_ref, mass_ref, w_out_ref)
    in_plane(w_out_ref)
    zeros = jnp.zeros((64, 128), f32)
    local = res_ref[...] - coupled(w_out_ref, zeros, zeros)
    sums = jnp.sum(local, axis=0, keepdims=True)
    bottom = -jnp.sum(w_out_ref[0:64], axis=0, keepdims=True)
    top = -jnp.sum(w_out_ref[448:512], axis=0, keepdims=True)
    outer = jnp.where(first_layer((1, 128)), bottom, top)
    left = jnp.broadcast_to(jnp.concatenate([sums, outer], axis=1), (8, 256))
    place = where_am_i()
    blocks = []
    for c in range(NC // 128):
        at = BASIS_ROW + c * 64
        below, above = beside(ga_ref[at : at + 64], gb_ref[at : at + 64], place)
        own = basis_ref[:, c * 128 : c * 128 + 128]
        right = jnp.concatenate([own, below, above], axis=0)
        part = dot_nn(left, right, exact_mode)[0:1]
        blocks.append(part * (1.0 / math.sqrt(NODES)))
    eight = jnp.concatenate(blocks + blocks, axis=0)
    for n in range(OWNERS * NC // 1024):
        part_ref[n * 8 : n * 8 + 8] = eight


def restart_kernel(
    parts_ref,
    solve_ref,
    mass_ref,
    w_ref,
    base_ref,
    cur_in_ref,
    invd_ref,
    coef_ref,
    y_ref,
    cur_ref,
    a_ref,
    b_ref,
    next_ref,
    work_ref,
):
    total = parts_ref[0:8]
    for n in range(1, OWNERS * NC // 1024):
        total = total + parts_ref[n * 8 : n * 8 + 8]
    total = total + pltpu.roll(total, 4, 0)
    correction = None
    for c in range(NC // 128):
        row = jnp.broadcast_to(total[c : c + 1], (8, 128))
        term = dot_nt(row, solve_ref[:, c * 128 : c * 128 + 128], exact_mode)
        correction = term if correction is None else correction + term
    correction = correction[0:1]
    cur_ref[...] = cur_in_ref[...] + correction
    y_ref[...] = mass_ref[...] * correction
    in_plane(y_ref)
    y_ref[...] = -(y_ref[...] + w_ref[...])
    send_first(
        y_ref, base_ref[...], invd_ref[...], coef_ref, next_ref, work_ref, a_ref, b_ref
    )


def last_kernel(*refs):
    inputs, (order_ref, out_ref), scratch = refs[:10], refs[10:12], refs[12:]
    current = closing_half(*inputs, *scratch)[1]
    out_ref[...] = take_lanes(current, order_ref[...])


def call(kernel, outs, *args, scratch=(), smem=(), far=(), near=(), copies=0):
    def stay(x):
        return pltpu.with_memory_space_constraint(x, pltpu.HBM)

    def space(n):
        if n in smem:
            return pltpu.SMEM
        return pltpu.HBM if n in far else pltpu.VMEM

    scratches = [pltpu.VMEM(s, f32) for s in scratch]
    if copies:
        scratches.append(pltpu.SemaphoreType.DMA((copies,)))
    return pl.pallas_call(
        kernel,
        out_shape=[jax.ShapeDtypeStruct(s, d) for s, d in outs],
        in_specs=[pl.BlockSpec(memory_space=space(n)) for n in range(len(args))],
        out_specs=[pl.BlockSpec(memory_space=pltpu.VMEM) for _ in outs],
        scratch_shapes=scratches,
        compiler_params=pltpu.CompilerParams(vmem_limit_bytes=20 << 20),
    )(*[stay(x) if n in far + near else x for n, x in enumerate(args)])


FIELD = ((NODES, 128), f32)
SIDE_MSG = ((64, 128), f32)
GHOST_MSG = ((GHOST_ROWS, 128), f32)
SIDE_WORK = [(64, 128), (64, 128)]
SEND_WORK = [(NODES, 128), (128, 128)]


def exchange(a, b):
    count = lax.axis_size("elem")
    pairs_a, pairs_b = [], []
    for d in range(2 * count):
        base, slab = d - d % count, d % count
        pairs_a.append((d, base + (slab ^ 1)))
        other = slab + (1 if slab % 2 else -1)
        inside = 0 <= other < count
        pairs_b.append((d, base + other if inside else (d + count) % (2 * count)))
    axes = ("sess", "elem")
    return lax.ppermute(a, axes, pairs_a), lax.ppermute(b, axes, pairs_b)


def one_device(
    pressure,
    load,
    stiffness,
    helm_mass,
    order_slots,
    recv_ids,
    donor_owner,
    donor_slot,
    interp_weights,
    live_count,
    coarse_basis,
    coarse_inverse,
):
    own_field = pressure.reshape(NODES, 128)
    order = order_slots.reshape(1, 128)
    owner = donor_owner.reshape(1, R_DEV)
    other_field = lax.ppermute(own_field, "sess", [(0, 1), (1, 0)])

    send, rank, owner, ids = call(
        request_kernel,
        [
            ((OWNERS * ASK, 128), f32),
            ((1, R_DEV), f32),
            ((1, R_DEV), jnp.int32),
            ((1, R_DEV), jnp.int32),
        ],
        owner,
        donor_slot,
        interp_weights.reshape(3 * NP, R_DEV),
        recv_ids,
        near=(0, 1, 2, 3),
    )
    received = lax.all_to_all(
        send.reshape(OWNERS, ASK, 128), "elem", split_axis=0, concat_axis=0, tiled=True
    )
    coef, mass, start, static, diag, invd, inv, basis, solve, order, ga, gb = call(
        setup_kernel,
        [
            ((3 * NODES, 128), f32),
            FIELD,
            FIELD,
            FIELD,
            FIELD,
            FIELD,
            ((1, 128), jnp.int32),
            ((128, NC), f32),
            ((128, NC), f32),
            ((1, 128), jnp.int32),
            GHOST_MSG,
            GHOST_MSG,
        ],
        order,
        stiffness.reshape(3 * NODES, 128),
        helm_mass.reshape(NODES, 128),
        own_field,
        load.reshape(NODES, 128),
        coarse_basis.reshape(128, NC),
        coarse_inverse.reshape(NC, NC),
        near=(0,),
        far=(1, 2, 3, 4, 5, 6),
        scratch=[
            (3 * NODES, 128),
            (NODES, 128),
            (NODES, 128),
            (NODES, 128),
            (128, NC),
            (NC, NC),
            (NODES, 128),
        ],
        copies=6,
    )
    answer, inv = call(
        owner_kernel,
        [((OWNERS, 128), f32), ((1, 128), jnp.int32)],
        received.reshape(OWNERS * ASK, 128),
        other_field,
        inv,
    )
    answered = lax.all_to_all(answer, "elem", split_axis=0, concat_axis=0, tiled=True)
    ga, gb = exchange(ga, gb)
    y, a, b = call(
        source_kernel,
        [FIELD, SIDE_MSG, SIDE_MSG],
        answered,
        owner,
        rank,
        ids,
        live_count,
        inv,
        static,
        invd,
        coef,
        smem=(4,),
        scratch=SEND_WORK,
    )
    a, b = exchange(a, b)
    half = [FIELD, FIELD, FIELD, FIELD, SIDE_MSG, SIDE_MSG]
    res, upd, cur, w, a, b, invd, planes = call(
        start_kernel,
        half + [FIELD, ((192, 128), f32)],
        y,
        diag,
        invd,
        start,
        a,
        b,
        ga,
        gb,
        coef,
        mass,
        scratch=SEND_WORK + SIDE_WORK,
    )
    a, b = exchange(a, b)
    res, cur, w, part = call(
        middle_kernel,
        [FIELD, FIELD, FIELD, ((OWNERS * NC // 128, 128), f32)],
        w,
        res,
        upd,
        cur,
        invd,
        a,
        b,
        planes,
        coef,
        mass,
        basis,
        ga,
        gb,
        scratch=[(NODES, 128)] + SIDE_WORK,
    )
    parts = lax.all_to_all(
        part.reshape(OWNERS, NC // 128, 128),
        "elem",
        split_axis=0,
        concat_axis=0,
        tiled=True,
    )
    y, cur, a, b = call(
        restart_kernel,
        [FIELD, FIELD, SIDE_MSG, SIDE_MSG],
        parts.reshape(OWNERS * NC // 128, 128),
        solve,
        mass,
        w,
        res,
        cur,
        invd,
        coef,
        scratch=SEND_WORK,
    )
    a, b = exchange(a, b)
    res, upd, cur, w, a, b = call(
        again_kernel,
        half,
        res,
        y,
        cur,
        a,
        b,
        invd,
        planes,
        coef,
        mass,
        scratch=SEND_WORK + SIDE_WORK,
    )
    a, b = exchange(a, b)
    (out,) = call(
        last_kernel,
        [FIELD],
        w,
        res,
        upd,
        cur,
        invd,
        a,
        b,
        planes,
        coef,
        mass,
        order,
        scratch=[(NODES, 128), (NODES, 128)] + SIDE_WORK,
    )
    return out.reshape(1, NP, NP, NP, 128)


def solution(mesh):
    return jax.shard_map(
        one_device,
        mesh=mesh,
        in_specs=(
            P("sess", None, None, None, "elem"),
            P("sess", None, None, None, "elem"),
            P("sess", None, None, None, None, "elem"),
            P("sess", None, None, None, "elem"),
            P("sess", "elem", None),
            P("sess", "elem"),
            P("sess", "elem", None),
            P("sess", "elem"),
            P("sess", None, "elem"),
            P("sess", "elem"),
            P("sess", "elem", None),
            P("sess", None, None),
        ),
        out_specs=P("sess", None, None, None, "elem"),
        check_vma=False,
    )
```

```python
import math

import jax
import jax.numpy as jnp
import numpy as np
from jax import lax
from jax.experimental import pallas as pl
from jax.experimental.pallas import tpu as pltpu
from jax.sharding import PartitionSpec as P


NP = 8
EX = 8
EY = 8
LAYER = EX * EY
NODES = NP**3
R_DEV = 1024
NC = 512
CHEB = 4
OWNERS = 64
COMPS = 32
HALF = 12
ASK = 8

exact_mode = lax.Precision.HIGHEST
spectrum_high = 8.0
spectrum_low = 0.8
f32 = jnp.float32
bf16 = jnp.bfloat16


def gll_derivative():
    x = np.array(
        [
            -1.0,
            -0.8717401485096066,
            -0.5917001814331423,
            -0.2092992179024789,
            0.2092992179024789,
            0.5917001814331423,
            0.8717401485096066,
            1.0,
        ]
    )
    legendre = (429.0 * x**7 - 693.0 * x**5 + 315.0 * x**3 - 35.0 * x) / 16.0
    distance = x[:, None] - x[None, :]
    same = np.eye(8, dtype=bool)
    table = legendre[:, None] / (legendre[None, :] * np.where(same, 1.0, distance))
    corner = np.zeros((8, 8))
    corner[0, 0] = -14.0
    corner[7, 7] = 14.0
    return np.where(same, corner, table).astype(np.float32).astype(np.float64)


DERIV = gll_derivative()


def chebyshev():
    center = 0.5 * (spectrum_high + spectrum_low)
    half_width = 0.5 * (spectrum_high - spectrum_low)
    sigma_ratio = center / half_width
    rho = 1.0 / sigma_ratio
    steps = [(0.0, 1.0 / center)]
    for _ in range(CHEB - 1):
        rho_next = 1.0 / (2.0 * sigma_ratio - rho)
        steps.append((rho_next * rho, 2.0 * rho_next / half_width))
        rho = rho_next
    return steps


STEPS = chebyshev()


def split3(x):
    hi = x.astype(bf16)
    rest = x - hi.astype(f32)
    mid = rest.astype(bf16)
    low = (rest - mid.astype(f32)).astype(bf16)
    return hi, mid, low


def dot_nn(a, b, precision=None):
    return lax.dot_general(
        a, b, (((1,), (0,)), ((), ())), precision=precision, preferred_element_type=f32
    )


def dot_nt(a, b, precision=None):
    return lax.dot_general(
        a, b, (((1,), (1,)), ((), ())), precision=precision, preferred_element_type=f32
    )


def iota(shape, axis):
    return lax.broadcasted_iota(jnp.int32, shape, axis)


def request_kernel(
    owner_ref, slot_ref, weight_ref, ids_ref, send_ref, rank_ref, owner_out_ref, ids_out_ref
):
    owner = owner_ref[...]
    hits = iota((OWNERS, R_DEV), 0) == owner
    hits_f = hits.astype(f32)
    hits_b = hits_f.astype(bf16)
    upper = (iota((128, 128), 0) < iota((128, 128), 1)).astype(f32).astype(bf16)
    carry = jnp.zeros((OWNERS, 1), f32)
    ranks = []
    for b in range(R_DEV // 128):
        cols = slice(b * 128, b * 128 + 128)
        block = hits_f[:, cols]
        count = dot_nn(hits_b[:, cols], upper) + carry
        ranks.append(jnp.sum(block * count, axis=0, keepdims=True))
        carry = carry + jnp.sum(block, axis=1, keepdims=True)
    rank = jnp.concatenate(ranks, axis=1)
    rank_ref[...] = rank
    owner_out_ref[...] = owner
    ids_out_ref[...] = ids_ref[...]
    payload = jnp.concatenate(
        [
            weight_ref[...],
            jnp.broadcast_to(slot_ref[...].astype(f32), (COMPS - 3 * NP, R_DEV)),
        ],
        axis=0,
    )
    pieces = split3(payload)
    total = None
    for piece in pieces:
        rows = [
            piece * (rank == float(m)).astype(f32).astype(bf16) for m in range(2 * HALF)
        ]
        part = dot_nt(hits_b, jnp.concatenate(rows, axis=0))
        total = part if total is None else total + part
    for c in range(ASK):
        if c < 2 * HALF * COMPS // 128:
            block = total[:, c * 128 : c * 128 + 128]
        else:
            block = jnp.zeros((OWNERS, 128), f32)
        send_ref[pl.ds(c, OWNERS, stride=ASK), :] = block


def owner_kernel(recv_ref, field_ref, before_ref, ret_ref, after_ref):
    cols = [recv_ref[pl.ds(c, OWNERS, stride=ASK), :] for c in range(6)]
    packed = jnp.concatenate(
        [jnp.concatenate(cols[:3], axis=1), jnp.concatenate(cols[3:], axis=1)], axis=0
    )
    comps = packed.T
    pieces = jnp.concatenate(split3(field_ref[...]), axis=1)
    rows = []
    for pair in range(HALF // 2):
        a = comps[(2 * pair) * COMPS : (2 * pair + 1) * COMPS]
        b = comps[(2 * pair + 1) * COMPS : (2 * pair + 2) * COMPS]
        both = jnp.concatenate([a, b], axis=1)
        slot = both[3 * NP : 3 * NP + 1].astype(jnp.int32)
        pick = (iota((128, 256), 0) == slot).astype(f32).astype(bf16)
        gathered = dot_nn(pieces, jnp.concatenate([pick, pick, pick], axis=0))
        wx = both[0:NP]
        wy = both[NP : 2 * NP]
        wz = both[2 * NP : 3 * NP]
        acc = None
        for k in range(NP):
            line = None
            for j in range(NP):
                row = (k * NP + j) * NP
                term = gathered[row : row + NP] * wy[j : j + 1]
                line = term if line is None else line + term
            line = line * wz[k : k + 1]
            acc = line if acc is None else acc + line
        value = jnp.sum(acc * wx, axis=0, keepdims=True)
        rows.append(value[:, :128])
        rows.append(value[:, 128:])
    rows.append(jnp.zeros((128 - HALF, 128), f32))
    turned = jnp.concatenate(rows, axis=0).T
    ret_ref[...] = turned[:OWNERS] + pltpu.roll(turned[OWNERS:], 16, 1)
    after_ref[...] = before_ref[...]


def deriv8(table, v):
    plus = [v[m] + v[7 - m] for m in range(4)]
    minus = [v[m] - v[7 - m] for m in range(4)]
    out = [None] * 8
    for a in range(4):
        even = odd = None
        for m in range(4):
            ce = 0.5 * (table[a, m] + table[a, 7 - m])
            co = 0.5 * (table[a, m] - table[a, 7 - m])
            te = plus[m] * float(ce)
            to = minus[m] * float(co)
            even = te if even is None else even + te
            odd = to if odd is None else odd + to
        out[a] = odd + even
        out[7 - a] = odd - even
    return out


def apply_line(v, coef):
    grad = deriv8(DERIV, v)
    return deriv8(DERIV.T, [grad[a] * coef(a) for a in range(8)])


def stiff_apply(v_ref, coef_ref, mass_ref, out_ref):
    def per_k(k, carry):
        base = pl.multiple_of(k * 64, 64)
        lines = [v_ref[pl.ds(base + i, 8, stride=8), :] for i in range(8)]
        res = apply_line(lines, lambda a: coef_ref[pl.ds(base + a * 8, 8), :])
        for i in range(8):
            out_ref[pl.ds(base + i, 8, stride=8), :] = res[i]
        rows = [v_ref[pl.ds(base + j * 8, 8), :] for j in range(8)]
        res = apply_line(rows, lambda b: coef_ref[pl.ds(512 + base + b * 8, 8), :])
        for j in range(8):
            at = pl.ds(base + j * 8, 8)
            out_ref[at, :] = out_ref[at, :] + res[j] + mass_ref[at, :] * rows[j]
        return carry

    lax.fori_loop(0, 8, per_k, 0)

    def per_j(j, carry):
        base = pl.multiple_of(j * 8, 8)
        cols = [v_ref[pl.ds(base + k * 64, 8), :] for k in range(8)]
        res = apply_line(cols, lambda c: coef_ref[pl.ds(1024 + base + c * 64, 8), :])
        for k in range(8):
            at = pl.ds(base + k * 64, 8)
            out_ref[at, :] = out_ref[at, :] + res[k]
        return carry

    lax.fori_loop(0, 8, per_j, 0)


def couple(high, low, shift, pos, count):
    lanes = high.shape[-1]
    next_low = pltpu.roll(low, lanes - shift, high.ndim - 1)
    prev_high = pltpu.roll(high, shift, high.ndim - 1)
    new_high = high + jnp.where(pos < count - 1, next_low, 0.0)
    new_low = low + jnp.where(pos > 0, prev_high, 0.0)
    return new_high, new_low


def in_plane(ref, count=NP):
    rows = count * NP
    col = iota((rows, 128), 1) % EX
    high, low = couple(
        ref[pl.ds(7, rows, stride=8), :], ref[pl.ds(0, rows, stride=8), :], 1, col, EX
    )
    ref[pl.ds(7, rows, stride=8), :] = high
    ref[pl.ds(0, rows, stride=8), :] = low
    line = (iota((8, 128), 1) // EX) % EY
    for k in range(count):
        high, low = couple(
            ref[k * 64 + 56 : k * 64 + 64], ref[k * 64 : k * 64 + 8], EX, line, EY
        )
        ref[k * 64 + 56 : k * 64 + 64] = high
        ref[k * 64 : k * 64 + 8] = low


def through(bottom, top, below, above):
    first = iota(bottom.shape, 1) < LAYER
    new_bottom = bottom + pltpu.roll(jnp.where(first, top, below), LAYER, 1)
    new_top = top + pltpu.roll(jnp.where(first, above, bottom), LAYER, 1)
    return new_bottom, new_top


def whole(bottom, ref, top):
    return jnp.concatenate([bottom, ref[64:448], top], axis=0)


def coupled(w_ref, below, above):
    bottom, top = through(w_ref[0:64], w_ref[448:512], below, above)
    return whole(bottom, w_ref, top)


def where_am_i():
    me = lax.axis_index("elem")
    last = lax.axis_size("elem") - 1
    return jnp.bitwise_and(me, 1) == 0, me > 0, me < last


def first_layer(shape):
    return iota(shape, 1) < LAYER


def pack(up, down, a_ref, b_ref, row, even):
    half = up.shape[0] // 2
    first = first_layer((half, 128))
    up = jnp.where(first, pltpu.roll(up[:half], LAYER, 1), up[half:])
    down = jnp.where(first, down[:half], pltpu.roll(down[half:], LAYER, 1))
    a_ref[row : row + half] = jnp.where(even, up, down)
    b_ref[row : row + half] = jnp.where(even, down, up)


def beside(a, b, place):
    even, has_below, has_above = place
    below = jnp.where(has_below, jnp.where(even, b, a), 0.0)
    above = jnp.where(has_above, jnp.where(even, a, b), 0.0)
    return below, above


def unpack(a_ref, b_ref, row, half, place):
    below, above = beside(a_ref[row : row + half], b_ref[row : row + half], place)
    first = first_layer(below.shape)
    low = jnp.where(first, above, pltpu.roll(below, LAYER, 1))
    high = jnp.where(first, pltpu.roll(above, LAYER, 1), below)
    return jnp.concatenate([low, high], axis=0)


def blend(bottom, top):
    return jnp.where(first_layer(bottom.shape), bottom, top)


def end_rows():
    first = first_layer((8, 128))
    return [
        jnp.where(first, float(DERIV[c, 0]), float(DERIV[c, 7])).astype(f32)
        for c in range(8)
    ]


def inner_planes(next_ref, coef_ref, out_ref, row):
    first = first_layer((8, 128))
    ends = end_rows()
    for j in range(8):
        cols = [next_ref[k * 64 + j * 8 : k * 64 + j * 8 + 8] for k in range(8)]
        cols[0] = jnp.where(first, 0.0, cols[0])
        cols[7] = jnp.where(first, cols[7], 0.0)
        grad = deriv8(DERIV, cols)
        total = None
        for c in range(8):
            at = 1024 + c * 64 + j * 8
            term = grad[c] * coef_ref[at : at + 8] * ends[c]
            total = term if total is None else total + term
        out_ref[row + j * 8 : row + j * 8 + 8] = total


def send_planes(w_ref, next_ref, coef_ref, work_ref, a_ref, b_ref, even):
    work_ref[0:64] = blend(w_ref[0:64], w_ref[448:512])
    inner_planes(next_ref, coef_ref, work_ref, 64)
    both = work_ref[...]
    pack(both, both, a_ref, b_ref, 0, even)


def shift_x(src_ref, dst_ref, count):
    rows = count * NP
    col = iota((rows, 128), 1) % EX
    dst_ref[...] = jnp.zeros(dst_ref.shape, f32)
    low = pltpu.roll(src_ref[pl.ds(7, rows, stride=8), :], 1, 1)
    high = pltpu.roll(src_ref[pl.ds(0, rows, stride=8), :], 127, 1)
    dst_ref[pl.ds(0, rows, stride=8), :] = jnp.where(col > 0, low, 0.0)
    dst_ref[pl.ds(7, rows, stride=8), :] = jnp.where(col < EX - 1, high, 0.0)


def shift_y(src_ref, dst_ref, count):
    line = (iota((8, 128), 1) // EX) % EY
    dst_ref[...] = jnp.zeros(dst_ref.shape, f32)
    for k in range(count):
        low = pltpu.roll(src_ref[k * 64 + 56 : k * 64 + 64], EX, 1)
        high = pltpu.roll(src_ref[k * 64 : k * 64 + 8], 128 - EX, 1)
        dst_ref[k * 64 : k * 64 + 8] = jnp.where(line > 0, low, 0.0)
        dst_ref[k * 64 + 56 : k * 64 + 64] = jnp.where(line < EY - 1, high, 0.0)


def correction_shares(coef_ref, mass_ref, invd_ref, out_ref, next_ref, x_ref, y_ref, face_ref, side_ref):
    scaled = STEPS[0][1]
    next_ref[...] = mass_ref[...] * invd_ref[...] * scaled
    inner_planes(next_ref, coef_ref, out_ref, 0)
    shift_x(mass_ref, x_ref, NP)
    next_ref[...] = x_ref[...] * invd_ref[...] * scaled
    inner_planes(next_ref, coef_ref, out_ref, 64)
    shift_y(mass_ref, y_ref, NP)
    next_ref[...] = y_ref[...] * invd_ref[...] * scaled
    inner_planes(next_ref, coef_ref, out_ref, 128)
    shift_y(x_ref, y_ref, NP)
    next_ref[...] = y_ref[...] * invd_ref[...] * scaled
    inner_planes(next_ref, coef_ref, out_ref, 192)
    first = first_layer((8, 128))
    ends = end_rows()
    weights = [
        ends[c] * jnp.where(first, float(DERIV[c, 7]), float(DERIV[c, 0]))
        for c in range(8)
    ]
    for j in range(8):
        total = None
        for c in range(8):
            at = 1024 + c * 64 + j * 8
            term = coef_ref[at : at + 8] * weights[c]
            total = term if total is None else total + term
        at = slice(j * 8, j * 8 + 8)
        inv = blend(invd_ref[448 + j * 8 : 456 + j * 8], invd_ref[at])
        next_ref[at] = total * inv * scaled
    share = next_ref[0:64]
    face_ref[...] = pltpu.roll(blend(mass_ref[448:512], mass_ref[0:64]), LAYER, 1)
    out_ref[256:320] = share * face_ref[...]
    shift_x(face_ref, side_ref, 1)
    out_ref[320:384] = share * side_ref[...]
    shift_y(face_ref, next_ref.at[64:128], 1)
    out_ref[384:448] = share * next_ref[64:128]
    shift_y(side_ref, next_ref.at[64:128], 1)
    out_ref[448:512] = share * next_ref[64:128]


def correction_inner(shares, near, behind):
    node = iota((64, 128), 0)
    left, front = node % 8 == 0, node < 8
    total = None
    for base, row in ((0, near), (256, behind)):
        row = jnp.broadcast_to(row, (64, 128))

        def turn(count):
            return pltpu.roll(row, count % 128, 1)

        values = [
            row,
            jnp.where(left, turn(1), turn(-1)),
            jnp.where(front, turn(8), turn(-8)),
            jnp.where(
                front,
                jnp.where(left, turn(9), turn(7)),
                jnp.where(left, turn(-7), turn(-9)),
            ),
        ]
        for n, value in enumerate(values):
            at = base + n * 64
            term = shares[at : at + 64] * value
            total = term if total is None else total + term
    return total


def ghost_side(update_ref, inner, planes_ref, face_ref, side_ref):
    face_ref[...] = pltpu.roll(blend(update_ref[0:64], update_ref[448:512]), LAYER, 1)
    lines = [face_ref[pl.ds(i, 8, stride=8), :] for i in range(8)]
    res = apply_line(lines, lambda a: planes_ref[a * 8 : a * 8 + 8])
    for i in range(8):
        side_ref[pl.ds(i, 8, stride=8), :] = res[i]
    rows = [face_ref[j * 8 : j * 8 + 8] for j in range(8)]
    res = apply_line(rows, lambda b: planes_ref[64 + b * 8 : 72 + b * 8])
    for j in range(8):
        at = slice(j * 8, j * 8 + 8)
        side_ref[at] = (
            side_ref[at]
            + res[j]
            + planes_ref[128 + j * 8 : 136 + j * 8] * rows[j]
            + inner[at]
        )
    in_plane(side_ref, 1)


def plain8(table, v):
    out = []
    for i in range(8):
        total = None
        for a in range(8):
            if table[a, i] == 0.0:
                continue
            term = v[a] * float(table[a, i])
            total = term if total is None else total + term
        out.append(total)
    return out


def take_lanes(x, index):
    return jnp.take_along_axis(
        x, jnp.broadcast_to(index, x.shape), axis=1, mode="promise_in_bounds"
    )


def local_diagonal(coef_ref, mass_ref, diag_ref):
    squared = DERIV * DERIV

    def per_k(k, carry):
        base = pl.multiple_of(k * 64, 64)
        res = plain8(squared, [coef_ref[pl.ds(base + a * 8, 8), :] for a in range(8)])
        for i in range(8):
            diag_ref[pl.ds(base + i, 8, stride=8), :] = res[i]
        res = plain8(squared, [coef_ref[pl.ds(512 + base + b * 8, 8), :] for b in range(8)])
        for j in range(8):
            at = pl.ds(base + j * 8, 8)
            diag_ref[at, :] = diag_ref[at, :] + res[j] + mass_ref[at, :]
        return carry

    lax.fori_loop(0, 8, per_k, 0)

    def per_j(j, carry):
        base = pl.multiple_of(j * 8, 8)
        res = plain8(squared, [coef_ref[pl.ds(1024 + base + c * 64, 8), :] for c in range(8)])
        for k in range(8):
            at = pl.ds(base + k * 64, 8)
            diag_ref[at, :] = diag_ref[at, :] + res[k]
        return carry

    lax.fori_loop(0, 8, per_j, 0)


SHARE_ROW = 192
BASIS_ROW = SHARE_ROW + 256
GHOST_ROWS = BASIS_ROW + 512


def setup_kernel(
    order_ref,
    stiff_hbm,
    mass_hbm,
    field_hbm,
    load_hbm,
    basis_hbm,
    inverse_hbm,
    coef_ref,
    mass_ref,
    static_ref,
    faces_ref,
    invd_ref,
    inv_ref,
    basis_ref,
    solve_ref,
    order_out_ref,
    a_ref,
    b_ref,
    stiff_in,
    mass_in,
    field_in,
    load_in,
    basis_in,
    inverse_in,
    tmp_ref,
    start_ref,
    diag_ref,
    share_ref,
    x_ref,
    y_ref,
    face_ref,
    side_ref,
    sems,
):
    copies = [
        pltpu.make_async_copy(src, dst, sems.at[n])
        for n, (src, dst) in enumerate(
            [
                (stiff_hbm, stiff_in),
                (mass_hbm, mass_in),
                (field_hbm, field_in),
                (load_hbm, load_in),
                (basis_hbm, basis_in),
                (inverse_hbm, inverse_in),
            ]
        )
    ]
    for copy in copies:
        copy.start()
    order = order_ref[...]
    match = (iota((128, 128), 0) == order).astype(f32)
    inv = jnp.sum(match.T * iota((128, 128), 0).astype(f32), axis=0, keepdims=True)
    inv = inv.astype(jnp.int32)
    inv_ref[...] = inv
    order_out_ref[...] = order
    copies[0].wait()
    tmp_ref[...] = take_lanes(stiff_in[0:512, :], inv)
    for k in range(8):
        for i in range(8):
            coef_ref[k * 64 + i * 8 : k * 64 + i * 8 + 8, :] = tmp_ref[
                pl.ds(k * 64 + i, 8, stride=8), :
            ]
    coef_ref[512:1536, :] = take_lanes(stiff_in[512:1536, :], inv)
    for copy in copies[1:]:
        copy.wait()
    mass_ref[...] = take_lanes(mass_in[...], inv)
    start_ref[...] = take_lanes(field_in[...], inv)
    stiff_apply(start_ref, coef_ref, mass_ref, static_ref)
    static_ref[...] = take_lanes(load_in[...], inv) - static_ref[...]
    in_plane(static_ref)
    basis = dot_nn(match, basis_in[...], exact_mode)
    basis_ref[...] = basis
    solve_ref[...] = dot_nn(basis, inverse_in[...], exact_mode)
    local_diagonal(coef_ref, mass_ref, diag_ref)
    in_plane(diag_ref)
    zeros = jnp.zeros((64, 128), f32)
    invd_ref[...] = 1.0 / coupled(diag_ref, zeros, zeros)
    ends = end_rows()
    for j in range(8):
        total = None
        for c in range(8):
            at = 1024 + c * 64 + j * 8
            term = coef_ref[at : at + 8] * (ends[c] * ends[c])
            total = term if total is None else total + term
        tmp_ref[j * 8 : j * 8 + 8] = total
    planes = jnp.concatenate(
        [
            blend(coef_ref[0:64], coef_ref[448:512]),
            blend(coef_ref[512:576], coef_ref[960:1024]),
            blend(mass_ref[0:64], mass_ref[448:512]) + tmp_ref[0:64],
            blend(diag_ref[0:64], diag_ref[448:512]),
            blend(mass_ref[0:64], mass_ref[448:512]),
            zeros,
        ],
        axis=0,
    )
    faces_ref[0:64] = diag_ref[0:64]
    faces_ref[64:128] = diag_ref[448:512]
    even = where_am_i()[0]
    pack(planes, planes, a_ref, b_ref, 0, even)
    correction_shares(
        coef_ref, mass_ref, invd_ref, share_ref, tmp_ref, x_ref, y_ref, face_ref, side_ref
    )
    shares = share_ref[...]
    pack(shares, shares, a_ref, b_ref, SHARE_ROW, even)
    for c in range(NC // 128):
        at = BASIS_ROW + c * 128
        cols = basis[:, c * 128 : c * 128 + 128]
        a_ref[at : at + 128] = cols
        b_ref[at : at + 128] = cols


def send_first(y_ref, base, invd, coef_ref, next_ref, work_ref, a_ref, b_ref):
    zeros = jnp.zeros((64, 128), f32)
    inner = coupled(y_ref, zeros, zeros)
    if base is not None:
        inner = inner + base
    next_ref[...] = inner * invd * STEPS[0][1]
    send_planes(y_ref, next_ref, coef_ref, work_ref, a_ref, b_ref, where_am_i()[0])


def source_kernel(
    ret_ref,
    owner_ref,
    rank_ref,
    ids_ref,
    live_ref,
    inv_ref,
    static_ref,
    invd_ref,
    coef_ref,
    y_ref,
    a_ref,
    b_ref,
    next_ref,
    work_ref,
):
    rank = rank_ref[...].astype(jnp.int32)
    place = rank + jnp.where(rank >= HALF, 16 - HALF, 0)
    ids = ids_ref[...]
    live = iota((1, R_DEV), 1) < live_ref[0, 0]
    node = jnp.where(live, lax.shift_right_logical(ids, 7), -1)
    elem = jnp.bitwise_and(ids, 127)
    hits = (iota((OWNERS, R_DEV), 0) == owner_ref[...]).astype(f32)
    picked = dot_nn(ret_ref[...].T, hits, exact_mode)[0:32]
    value = jnp.sum(
        jnp.where(iota((32, R_DEV), 0) == place, picked, 0.0), axis=0, keepdims=True
    )
    at_node = (iota((NODES, R_DEV), 0) == node).astype(f32).astype(bf16)
    at_elem = (iota((128, R_DEV), 0) == elem).astype(f32).astype(bf16)
    spread = jnp.concatenate([at_elem * piece for piece in split3(value)], axis=0)
    landed = dot_nt(at_node, spread)
    landed = landed[:, 0:128] + landed[:, 128:256] + landed[:, 256:384]
    y_ref[...] = take_lanes(landed, inv_ref[...])
    in_plane(y_ref)
    y_ref[...] = y_ref[...] + static_ref[...]
    send_first(y_ref, None, invd_ref[...], coef_ref, next_ref, work_ref, a_ref, b_ref)


def opening_half(
    place,
    base_ref,
    y_ref,
    cur_in,
    raw,
    inner,
    invd_ref,
    planes_ref,
    coef_ref,
    mass_ref,
    res_ref,
    upd_ref,
    cur_ref,
    w_ref,
    a_out_ref,
    b_out_ref,
    next_ref,
    work_ref,
    face_ref,
    side_ref,
):
    residual = coupled(y_ref, raw, raw)
    if base_ref is not None:
        residual = residual + base_ref[...]
    update = residual * invd_ref[...] * STEPS[0][1]
    upd_ref[...] = update
    ghost_side(upd_ref, inner, planes_ref, face_ref, side_ref)
    stiff_apply(upd_ref, coef_ref, mass_ref, w_ref)
    in_plane(w_ref)
    residual = residual - coupled(w_ref, side_ref[...], side_ref[...])
    res_ref[...] = residual
    alpha, beta = STEPS[1]
    second = alpha * update + beta * invd_ref[...] * residual
    upd_ref[...] = second
    done = update + second
    cur_ref[...] = done if cur_in is None else cur_in + done
    stiff_apply(upd_ref, coef_ref, mass_ref, w_ref)
    in_plane(w_ref)
    alpha, beta = STEPS[2]
    zeros = jnp.zeros((64, 128), f32)
    next_ref[...] = alpha * upd_ref[...] + beta * invd_ref[...] * (
        res_ref[...] - coupled(w_ref, zeros, zeros)
    )
    send_planes(w_ref, next_ref, coef_ref, work_ref, a_out_ref, b_out_ref, place[0])


def start_kernel(
    y_ref,
    faces_ref,
    invd_in_ref,
    a_ref,
    b_ref,
    ga_ref,
    gb_ref,
    coef_ref,
    mass_ref,
    res_ref,
    upd_ref,
    cur_ref,
    w_ref,
    a_out_ref,
    b_out_ref,
    invd_ref,
    planes_ref,
    *scratch,
):
    place = where_am_i()
    planes = unpack(ga_ref, gb_ref, 0, SHARE_ROW, place)
    planes_ref[...] = planes[0:320]
    came = unpack(a_ref, b_ref, 0, 64, place)
    bottom, top = through(
        faces_ref[0:64], faces_ref[64:128], planes[192:256], planes[192:256]
    )
    invd_ref[...] = whole(1.0 / bottom, invd_in_ref, 1.0 / top)
    opening_half(
        place,
        None,
        y_ref,
        None,
        came[0:64],
        came[64:128],
        invd_ref,
        planes_ref,
        coef_ref,
        mass_ref,
        res_ref,
        upd_ref,
        cur_ref,
        w_ref,
        a_out_ref,
        b_out_ref,
        *scratch,
    )


def near_kernel(
    ga_ref, gb_ref, inverse_ref, after_ref, out_ref, shares_hbm, shares_ref, sems
):
    place = where_am_i()
    blocks = []
    for c in range(NC // 128):
        at = BASIS_ROW + c * 128
        below, above = beside(ga_ref[at : at + 128], gb_ref[at : at + 128], place)
        blocks.append(jnp.concatenate([above, below], axis=0))
    rows = jnp.concatenate(blocks, axis=1)
    shares_ref[...] = unpack(ga_ref, gb_ref, SHARE_ROW, 256, place)
    copy = pltpu.make_async_copy(shares_ref, shares_hbm, sems.at[0])
    copy.start()
    out_ref[...] = dot_nn(rows, inverse_ref[...], exact_mode)
    copy.wait()


def again_kernel(
    parts_ref,
    solve_ref,
    near_ref,
    shares_hbm,
    base_hbm,
    a_ref,
    b_ref,
    invd_ref,
    planes_ref,
    coef_ref,
    mass_ref,
    res_ref,
    upd_ref,
    cur_ref,
    w_ref,
    a_out_ref,
    b_out_ref,
    y_ref,
    next_ref,
    work_ref,
    face_ref,
    side_ref,
    shares_ref,
    base_ref,
    sems,
):
    copies = [
        pltpu.make_async_copy(shares_hbm, shares_ref, sems.at[0]),
        pltpu.make_async_copy(base_hbm, base_ref, sems.at[1]),
    ]
    for copy in copies:
        copy.start()
    place = where_am_i()
    total = parts_ref[0:8]
    for n in range(1, OWNERS * NC // 1024):
        total = total + parts_ref[n * 8 : n * 8 + 8]
    total = total + pltpu.roll(total, 4, 0)
    both = None
    for c in range(NC // 128):
        row = jnp.broadcast_to(total[c : c + 1], (8, 128))
        cols = slice(c * 128, c * 128 + 128)
        rows = jnp.concatenate([solve_ref[:, cols], near_ref[:, cols]], axis=0)
        term = dot_nt(row, rows, exact_mode)
        both = term if both is None else both + term
    correction = both[0:1, 0:128]
    above, below = both[0:1, 128:256], both[0:1, 256:384]
    first = first_layer((1, 128))
    near = jnp.where(first, above, below)
    behind = pltpu.roll(jnp.broadcast_to(jnp.where(first, below, above), (8, 128)), LAYER, 1)
    y_ref[...] = mass_ref[...] * (-correction)
    in_plane(y_ref)
    came = unpack(a_ref, b_ref, 0, 64, place)
    side_ref[...] = planes_ref[256:320] * near
    in_plane(side_ref, 1)
    raw = -(came[0:64] + side_ref[...])
    for copy in copies:
        copy.wait()
    inner = came[64:128] - correction_inner(shares_ref, near, behind[0:1])
    opening_half(
        place,
        base_ref,
        y_ref,
        correction,
        raw,
        inner,
        invd_ref,
        planes_ref,
        coef_ref,
        mass_ref,
        res_ref,
        upd_ref,
        cur_ref,
        w_ref,
        a_out_ref,
        b_out_ref,
        next_ref,
        work_ref,
        face_ref,
        side_ref,
    )


def closing_half(
    w_ref,
    res_ref,
    upd_ref,
    cur_ref,
    invd_ref,
    a_ref,
    b_ref,
    planes_ref,
    coef_ref,
    mass_ref,
    work_ref,
    vec_ref,
    face_ref,
    side_ref,
):
    came = unpack(a_ref, b_ref, 0, 64, where_am_i())
    residual = res_ref[...] - coupled(w_ref, came[0:64], came[0:64])
    alpha, beta = STEPS[2]
    third = alpha * upd_ref[...] + beta * invd_ref[...] * residual
    vec_ref[...] = third
    ghost_side(vec_ref, came[64:128], planes_ref, face_ref, side_ref)
    stiff_apply(vec_ref, coef_ref, mass_ref, work_ref)
    in_plane(work_ref)
    residual = residual - coupled(work_ref, side_ref[...], side_ref[...])
    alpha, beta = STEPS[3]
    fourth = alpha * third + beta * invd_ref[...] * residual
    vec_ref[...] = fourth
    return residual, cur_ref[...] + (third + fourth)


def middle_kernel(
    w_ref,
    res_in_ref,
    upd_ref,
    cur_in_ref,
    invd_ref,
    a_ref,
    b_ref,
    planes_ref,
    coef_ref,
    mass_ref,
    basis_ref,
    ga_ref,
    gb_ref,
    local_hbm,
    cur_hbm,
    part_ref,
    a_out_ref,
    b_out_ref,
    w_out_ref,
    vec_ref,
    cur_ref,
    local_ref,
    next_ref,
    work_ref,
    face_ref,
    side_ref,
    sems,
):
    residual, current = closing_half(
        w_ref,
        res_in_ref,
        upd_ref,
        cur_in_ref,
        invd_ref,
        a_ref,
        b_ref,
            planes_ref,
        coef_ref,
        mass_ref,
        w_out_ref,
        vec_ref,
        face_ref,
        side_ref,
    )
    local_ref[...] = residual
    cur_ref[...] = current
    copy = pltpu.make_async_copy(cur_ref, cur_hbm, sems.at[0])
    copy.start()
    stiff_apply(vec_ref, coef_ref, mass_ref, w_out_ref)
    in_plane(w_out_ref)
    zeros = jnp.zeros((64, 128), f32)
    local = local_ref[...] - coupled(w_out_ref, zeros, zeros)
    local_ref[...] = local
    second = pltpu.make_async_copy(local_ref, local_hbm, sems.at[1])
    second.start()
    next_ref[...] = local * invd_ref[...] * STEPS[0][1]
    place = where_am_i()
    send_planes(w_out_ref, next_ref, coef_ref, work_ref, a_out_ref, b_out_ref, place[0])
    sums = jnp.sum(local, axis=0, keepdims=True)
    bottom = -jnp.sum(w_out_ref[0:64], axis=0, keepdims=True)
    top = -jnp.sum(w_out_ref[448:512], axis=0, keepdims=True)
    outer = jnp.where(first_layer((1, 128)), bottom, top)
    left = jnp.broadcast_to(jnp.concatenate([sums, outer], axis=1), (8, 256))
    blocks = []
    for c in range(NC // 128):
        at = BASIS_ROW + c * 128
        below, above = beside(ga_ref[at : at + 128], gb_ref[at : at + 128], place)
        own = basis_ref[:, c * 128 : c * 128 + 128]
        right = jnp.concatenate([own, below[LAYER:], above[:LAYER]], axis=0)
        part = dot_nn(left, right, exact_mode)[0:1]
        blocks.append(part * (1.0 / math.sqrt(NODES)))
    eight = jnp.concatenate(blocks + blocks, axis=0)
    for n in range(OWNERS * NC // 1024):
        part_ref[n * 8 : n * 8 + 8] = eight
    copy.wait()
    second.wait()


def last_kernel(*refs):
    inputs, (order_ref, field_hbm, first_hbm, out_ref), rest = (
        refs[:10],
        refs[10:14],
        refs[14:],
    )
    scratch, (field_in, first_in, sems) = rest[:-3], rest[-3:]
    copies = [
        pltpu.make_async_copy(field_hbm, field_in, sems.at[0]),
        pltpu.make_async_copy(first_hbm, first_in, sems.at[1]),
    ]
    for copy in copies:
        copy.start()
    current = closing_half(*inputs, *scratch)[1]
    for copy in copies:
        copy.wait()
    moved = take_lanes(first_in[...] + current, order_ref[...])
    out_ref[...] = field_in[...] + moved


def call(kernel, outs, *args, scratch=(), smem=(), far=(), near=(), copies=0, away=()):
    def stay(x):
        return pltpu.with_memory_space_constraint(x, pltpu.HBM)

    def space(n):
        if n in smem:
            return pltpu.SMEM
        return pltpu.HBM if n in far else pltpu.VMEM

    scratches = [pltpu.VMEM(s, f32) for s in scratch]
    if copies:
        scratches.append(pltpu.SemaphoreType.DMA((copies,)))
    return pl.pallas_call(
        kernel,
        out_shape=[
            pltpu.HBM(s, d) if n in away else jax.ShapeDtypeStruct(s, d)
            for n, (s, d) in enumerate(outs)
        ],
        in_specs=[pl.BlockSpec(memory_space=space(n)) for n in range(len(args))],
        out_specs=[
            pl.BlockSpec(memory_space=pltpu.HBM if n in away else pltpu.VMEM)
            for n in range(len(outs))
        ],
        scratch_shapes=scratches,
        compiler_params=pltpu.CompilerParams(vmem_limit_bytes=20 << 20),
    )(*[stay(x) if n in far + near else x for n, x in enumerate(args)])


FIELD = ((NODES, 128), f32)
SIDE_MSG = ((64, 128), f32)
GHOST_MSG = ((GHOST_ROWS, 128), f32)
SIDE_WORK = [(64, 128), (64, 128)]
SEND_WORK = [(NODES, 128), (128, 128)]


def exchange(a, b):
    count = lax.axis_size("elem")
    pairs_a, pairs_b = [], []
    for d in range(2 * count):
        base, slab = d - d % count, d % count
        pairs_a.append((d, base + (slab ^ 1)))
        other = slab + (1 if slab % 2 else -1)
        inside = 0 <= other < count
        pairs_b.append((d, base + other if inside else (d + count) % (2 * count)))
    axes = ("sess", "elem")
    return lax.ppermute(a, axes, pairs_a), lax.ppermute(b, axes, pairs_b)


def one_device(
    pressure,
    load,
    stiffness,
    helm_mass,
    order_slots,
    recv_ids,
    donor_owner,
    donor_slot,
    interp_weights,
    live_count,
    coarse_basis,
    coarse_inverse,
):
    own_field = pressure.reshape(NODES, 128)
    order = order_slots.reshape(1, 128)
    owner = donor_owner.reshape(1, R_DEV)
    other_field = lax.ppermute(own_field, "sess", [(0, 1), (1, 0)])

    send, rank, owner, ids = call(
        request_kernel,
        [
            ((OWNERS * ASK, 128), f32),
            ((1, R_DEV), f32),
            ((1, R_DEV), jnp.int32),
            ((1, R_DEV), jnp.int32),
        ],
        owner,
        donor_slot,
        interp_weights.reshape(3 * NP, R_DEV),
        recv_ids,
        near=(0, 1, 2, 3),
    )
    received = lax.all_to_all(
        send.reshape(OWNERS, ASK, 128), "elem", split_axis=0, concat_axis=0, tiled=True
    )
    coef, mass, static, faces, invd, inv, basis, solve, order, ga, gb = call(
        setup_kernel,
        [
            ((3 * NODES, 128), f32),
            FIELD,
            FIELD,
            ((128, 128), f32),
            FIELD,
            ((1, 128), jnp.int32),
            ((128, NC), f32),
            ((128, NC), f32),
            ((1, 128), jnp.int32),
            GHOST_MSG,
            GHOST_MSG,
        ],
        order,
        stiffness.reshape(3 * NODES, 128),
        helm_mass.reshape(NODES, 128),
        own_field,
        load.reshape(NODES, 128),
        coarse_basis.reshape(128, NC),
        coarse_inverse.reshape(NC, NC),
        near=(0,),
        far=(1, 2, 3, 4, 5, 6),
        scratch=[
            (3 * NODES, 128),
            (NODES, 128),
            (NODES, 128),
            (NODES, 128),
            (128, NC),
            (NC, NC),
            (NODES, 128),
            (NODES, 128),
            (NODES, 128),
            (NODES, 128),
            (NODES, 128),
            (NODES, 128),
            (64, 128),
            (64, 128),
        ],
        copies=6,
    )
    answer, inv = call(
        owner_kernel,
        [((OWNERS, 128), f32), ((1, 128), jnp.int32)],
        received.reshape(OWNERS * ASK, 128),
        other_field,
        inv,
    )
    answered = lax.all_to_all(answer, "elem", split_axis=0, concat_axis=0, tiled=True)
    ga, gb = exchange(ga, gb)
    y, a, b = call(
        source_kernel,
        [FIELD, SIDE_MSG, SIDE_MSG],
        answered,
        owner,
        rank,
        ids,
        live_count,
        inv,
        static,
        invd,
        coef,
        smem=(4,),
        scratch=SEND_WORK,
    )
    a, b = exchange(a, b)
    half = [FIELD, FIELD, FIELD, FIELD, SIDE_MSG, SIDE_MSG]
    res, upd, cur, w, a, b, invd, planes = call(
        start_kernel,
        half + [FIELD, ((320, 128), f32)],
        y,
        faces,
        invd,
        a,
        b,
        ga,
        gb,
        coef,
        mass,
        scratch=SEND_WORK + SIDE_WORK,
    )
    a, b = exchange(a, b)
    res, total, part, a, b = call(
        middle_kernel,
        [FIELD, FIELD, ((OWNERS * NC // 128, 128), f32), SIDE_MSG, SIDE_MSG],
        w,
        res,
        upd,
        cur,
        invd,
        a,
        b,
        planes,
        coef,
        mass,
        basis,
        ga,
        gb,
        scratch=[(NODES, 128)] * 4 + SEND_WORK + SIDE_WORK,
        copies=2,
        away=(0, 1),
    )
    near, shares = call(
        near_kernel,
        [((256, NC), f32), FIELD],
        ga,
        gb,
        coarse_inverse.reshape(NC, NC),
        a,
        near=(2,),
        scratch=[(NODES, 128)],
        copies=1,
        away=(1,),
    )
    parts = lax.all_to_all(
        part.reshape(OWNERS, NC // 128, 128),
        "elem",
        split_axis=0,
        concat_axis=0,
        tiled=True,
    )
    a, b = exchange(a, b)
    res, upd, cur, w, a, b = call(
        again_kernel,
        half,
        parts.reshape(OWNERS * NC // 128, 128),
        solve,
        near,
        shares,
        res,
        a,
        b,
        invd,
        planes,
        coef,
        mass,
        far=(3, 4),
        scratch=[(NODES, 128)] + SEND_WORK + SIDE_WORK + [(NODES, 128)] * 2,
        copies=2,
    )
    a, b = exchange(a, b)
    (out,) = call(
        last_kernel,
        [FIELD],
        w,
        res,
        upd,
        cur,
        invd,
        a,
        b,
        planes,
        coef,
        mass,
        order,
        own_field,
        total,
        far=(11, 12),
        scratch=[(NODES, 128)] * 2 + SIDE_WORK + [(NODES, 128)] * 2,
        copies=2,
    )
    return out.reshape(1, NP, NP, NP, 128)


def solution(mesh):
    return jax.shard_map(
        one_device,
        mesh=mesh,
        in_specs=(
            P("sess", None, None, None, "elem"),
            P("sess", None, None, None, "elem"),
            P("sess", None, None, None, None, "elem"),
            P("sess", None, None, None, "elem"),
            P("sess", "elem", None),
            P("sess", "elem"),
            P("sess", "elem", None),
            P("sess", "elem"),
            P("sess", None, "elem"),
            P("sess", "elem"),
            P("sess", "elem", None),
            P("sess", None, None),
        ),
        out_specs=P("sess", None, None, None, "elem"),
        check_vma=False,
    )
```

```python
import math

import jax
import jax.numpy as jnp
import numpy as np
from jax import lax
from jax.experimental import pallas as pl
from jax.experimental.pallas import tpu as pltpu
from jax.sharding import PartitionSpec as P


NP = 8
EX = 8
EY = 8
LAYER = EX * EY
NODES = NP**3
R_DEV = 1024
NC = 512
CHEB = 4
OWNERS = 64
COMPS = 32
HALF = 12
ASK = 8

exact_mode = lax.Precision.HIGHEST
spectrum_high = 8.0
spectrum_low = 0.8
f32 = jnp.float32
bf16 = jnp.bfloat16


def gll_derivative():
    x = np.array(
        [
            -1.0,
            -0.8717401485096066,
            -0.5917001814331423,
            -0.2092992179024789,
            0.2092992179024789,
            0.5917001814331423,
            0.8717401485096066,
            1.0,
        ]
    )
    legendre = (429.0 * x**7 - 693.0 * x**5 + 315.0 * x**3 - 35.0 * x) / 16.0
    distance = x[:, None] - x[None, :]
    same = np.eye(8, dtype=bool)
    table = legendre[:, None] / (legendre[None, :] * np.where(same, 1.0, distance))
    corner = np.zeros((8, 8))
    corner[0, 0] = -14.0
    corner[7, 7] = 14.0
    return np.where(same, corner, table).astype(np.float32).astype(np.float64)


DERIV = gll_derivative()


def chebyshev():
    center = 0.5 * (spectrum_high + spectrum_low)
    half_width = 0.5 * (spectrum_high - spectrum_low)
    sigma_ratio = center / half_width
    rho = 1.0 / sigma_ratio
    steps = [(0.0, 1.0 / center)]
    for _ in range(CHEB - 1):
        rho_next = 1.0 / (2.0 * sigma_ratio - rho)
        steps.append((rho_next * rho, 2.0 * rho_next / half_width))
        rho = rho_next
    return steps


STEPS = chebyshev()


def split3(x):
    hi = x.astype(bf16)
    rest = x - hi.astype(f32)
    mid = rest.astype(bf16)
    low = (rest - mid.astype(f32)).astype(bf16)
    return hi, mid, low


def dot_nn(a, b, precision=None):
    return lax.dot_general(
        a, b, (((1,), (0,)), ((), ())), precision=precision, preferred_element_type=f32
    )


def dot_nt(a, b, precision=None):
    return lax.dot_general(
        a, b, (((1,), (1,)), ((), ())), precision=precision, preferred_element_type=f32
    )


def iota(shape, axis):
    return lax.broadcasted_iota(jnp.int32, shape, axis)


def request_kernel(
    owner_ref, slot_ref, weight_ref, ids_ref, send_ref, rank_ref, owner_out_ref, ids_out_ref
):
    owner = owner_ref[...]
    hits = iota((OWNERS, R_DEV), 0) == owner
    hits_f = hits.astype(f32)
    hits_b = hits_f.astype(bf16)
    upper = (iota((128, 128), 0) < iota((128, 128), 1)).astype(f32).astype(bf16)
    carry = jnp.zeros((OWNERS, 1), f32)
    ranks = []
    for b in range(R_DEV // 128):
        cols = slice(b * 128, b * 128 + 128)
        block = hits_f[:, cols]
        count = dot_nn(hits_b[:, cols], upper) + carry
        ranks.append(jnp.sum(block * count, axis=0, keepdims=True))
        carry = carry + jnp.sum(block, axis=1, keepdims=True)
    rank = jnp.concatenate(ranks, axis=1)
    rank_ref[...] = rank
    owner_out_ref[...] = owner
    ids_out_ref[...] = ids_ref[...]
    payload = jnp.concatenate(
        [
            weight_ref[...],
            jnp.broadcast_to(slot_ref[...].astype(f32), (COMPS - 3 * NP, R_DEV)),
        ],
        axis=0,
    )
    pieces = split3(payload)
    total = None
    for piece in pieces:
        rows = [
            piece * (rank == float(m)).astype(f32).astype(bf16) for m in range(2 * HALF)
        ]
        part = dot_nt(hits_b, jnp.concatenate(rows, axis=0))
        total = part if total is None else total + part
    for c in range(ASK):
        if c < 2 * HALF * COMPS // 128:
            block = total[:, c * 128 : c * 128 + 128]
        else:
            block = jnp.zeros((OWNERS, 128), f32)
        send_ref[pl.ds(c, OWNERS, stride=ASK), :] = block


def owner_kernel(recv_ref, field_ref, before_ref, ret_ref, after_ref):
    cols = [recv_ref[pl.ds(c, OWNERS, stride=ASK), :] for c in range(6)]
    packed = jnp.concatenate(
        [jnp.concatenate(cols[:3], axis=1), jnp.concatenate(cols[3:], axis=1)], axis=0
    )
    comps = packed.T
    pieces = jnp.concatenate(split3(field_ref[...]), axis=1)
    rows = []
    for pair in range(HALF // 2):
        a = comps[(2 * pair) * COMPS : (2 * pair + 1) * COMPS]
        b = comps[(2 * pair + 1) * COMPS : (2 * pair + 2) * COMPS]
        both = jnp.concatenate([a, b], axis=1)
        slot = both[3 * NP : 3 * NP + 1].astype(jnp.int32)
        pick = (iota((128, 256), 0) == slot).astype(f32).astype(bf16)
        gathered = dot_nn(pieces, jnp.concatenate([pick, pick, pick], axis=0))
        wx = both[0:NP]
        wy = both[NP : 2 * NP]
        wz = both[2 * NP : 3 * NP]
        acc = None
        for k in range(NP):
            line = None
            for j in range(NP):
                row = (k * NP + j) * NP
                term = gathered[row : row + NP] * wy[j : j + 1]
                line = term if line is None else line + term
            line = line * wz[k : k + 1]
            acc = line if acc is None else acc + line
        value = jnp.sum(acc * wx, axis=0, keepdims=True)
        rows.append(value[:, :128])
        rows.append(value[:, 128:])
    rows.append(jnp.zeros((128 - HALF, 128), f32))
    turned = jnp.concatenate(rows, axis=0).T
    ret_ref[...] = turned[:OWNERS] + pltpu.roll(turned[OWNERS:], 16, 1)
    after_ref[...] = before_ref[...]


def deriv8(table, v):
    plus = [v[m] + v[7 - m] for m in range(4)]
    minus = [v[m] - v[7 - m] for m in range(4)]
    out = [None] * 8
    for a in range(4):
        even = odd = None
        for m in range(4):
            ce = 0.5 * (table[a, m] + table[a, 7 - m])
            co = 0.5 * (table[a, m] - table[a, 7 - m])
            te = plus[m] * float(ce)
            to = minus[m] * float(co)
            even = te if even is None else even + te
            odd = to if odd is None else odd + to
        out[a] = odd + even
        out[7 - a] = odd - even
    return out


def apply_line(v, coef):
    grad = deriv8(DERIV, v)
    return deriv8(DERIV.T, [grad[a] * coef(a) for a in range(8)])


def stiff_apply(v_ref, coef_ref, mass_ref, out_ref):
    def per_k(k, carry):
        base = pl.multiple_of(k * 64, 64)
        lines = [v_ref[pl.ds(base + i, 8, stride=8), :] for i in range(8)]
        res = apply_line(lines, lambda a: coef_ref[pl.ds(base + a * 8, 8), :])
        for i in range(8):
            out_ref[pl.ds(base + i, 8, stride=8), :] = res[i]
        rows = [v_ref[pl.ds(base + j * 8, 8), :] for j in range(8)]
        res = apply_line(rows, lambda b: coef_ref[pl.ds(512 + base + b * 8, 8), :])
        for j in range(8):
            at = pl.ds(base + j * 8, 8)
            out_ref[at, :] = out_ref[at, :] + res[j] + mass_ref[at, :] * rows[j]
        return carry

    lax.fori_loop(0, 8, per_k, 0)

    def per_j(j, carry):
        base = pl.multiple_of(j * 8, 8)
        cols = [v_ref[pl.ds(base + k * 64, 8), :] for k in range(8)]
        res = apply_line(cols, lambda c: coef_ref[pl.ds(1024 + base + c * 64, 8), :])
        for k in range(8):
            at = pl.ds(base + k * 64, 8)
            out_ref[at, :] = out_ref[at, :] + res[k]
        return carry

    lax.fori_loop(0, 8, per_j, 0)


def couple(high, low, shift, pos, count):
    lanes = high.shape[-1]
    next_low = pltpu.roll(low, lanes - shift, high.ndim - 1)
    prev_high = pltpu.roll(high, shift, high.ndim - 1)
    new_high = high + jnp.where(pos < count - 1, next_low, 0.0)
    new_low = low + jnp.where(pos > 0, prev_high, 0.0)
    return new_high, new_low


def in_plane(ref, count=NP):
    rows = count * NP
    col = iota((rows, 128), 1) % EX
    high, low = couple(
        ref[pl.ds(7, rows, stride=8), :], ref[pl.ds(0, rows, stride=8), :], 1, col, EX
    )
    ref[pl.ds(7, rows, stride=8), :] = high
    ref[pl.ds(0, rows, stride=8), :] = low
    line = (iota((8, 128), 1) // EX) % EY
    for k in range(count):
        high, low = couple(
            ref[k * 64 + 56 : k * 64 + 64], ref[k * 64 : k * 64 + 8], EX, line, EY
        )
        ref[k * 64 + 56 : k * 64 + 64] = high
        ref[k * 64 : k * 64 + 8] = low


def through(bottom, top, below, above):
    first = iota(bottom.shape, 1) < LAYER
    new_bottom = bottom + pltpu.roll(jnp.where(first, top, below), LAYER, 1)
    new_top = top + pltpu.roll(jnp.where(first, above, bottom), LAYER, 1)
    return new_bottom, new_top


def whole(bottom, ref, top):
    return jnp.concatenate([bottom, ref[64:448], top], axis=0)


def coupled(w_ref, below, above):
    bottom, top = through(w_ref[0:64], w_ref[448:512], below, above)
    return whole(bottom, w_ref, top)


def where_am_i():
    me = lax.axis_index("elem")
    last = lax.axis_size("elem") - 1
    return jnp.bitwise_and(me, 1) == 0, me > 0, me < last


def first_layer(shape):
    return iota(shape, 1) < LAYER


def pack(up, down, a_ref, b_ref, row, even):
    half = up.shape[0] // 2
    first = first_layer((half, 128))
    up = jnp.where(first, pltpu.roll(up[:half], LAYER, 1), up[half:])
    down = jnp.where(first, down[:half], pltpu.roll(down[half:], LAYER, 1))
    a_ref[row : row + half] = jnp.where(even, up, down)
    b_ref[row : row + half] = jnp.where(even, down, up)


def beside(a, b, place):
    even, has_below, has_above = place
    below = jnp.where(has_below, jnp.where(even, b, a), 0.0)
    above = jnp.where(has_above, jnp.where(even, a, b), 0.0)
    return below, above


def unpack(a_ref, b_ref, row, half, place):
    below, above = beside(a_ref[row : row + half], b_ref[row : row + half], place)
    first = first_layer(below.shape)
    low = jnp.where(first, above, pltpu.roll(below, LAYER, 1))
    high = jnp.where(first, pltpu.roll(above, LAYER, 1), below)
    return jnp.concatenate([low, high], axis=0)


def blend(bottom, top):
    return jnp.where(first_layer(bottom.shape), bottom, top)


def end_rows():
    first = first_layer((8, 128))
    return [
        jnp.where(first, float(DERIV[c, 0]), float(DERIV[c, 7])).astype(f32)
        for c in range(8)
    ]


def inner_planes(next_ref, coef_ref, out_ref, row):
    first = first_layer((8, 128))
    ends = end_rows()
    for j in range(8):
        cols = [next_ref[k * 64 + j * 8 : k * 64 + j * 8 + 8] for k in range(8)]
        cols[0] = jnp.where(first, 0.0, cols[0])
        cols[7] = jnp.where(first, cols[7], 0.0)
        grad = deriv8(DERIV, cols)
        total = None
        for c in range(8):
            at = 1024 + c * 64 + j * 8
            term = grad[c] * coef_ref[at : at + 8] * ends[c]
            total = term if total is None else total + term
        out_ref[row + j * 8 : row + j * 8 + 8] = total


def send_planes(w_ref, next_ref, coef_ref, work_ref, a_ref, b_ref, even):
    work_ref[0:64] = blend(w_ref[0:64], w_ref[448:512])
    inner_planes(next_ref, coef_ref, work_ref, 64)
    both = work_ref[...]
    pack(both, both, a_ref, b_ref, 0, even)


def shift_x(src_ref, dst_ref, count):
    rows = count * NP
    col = iota((rows, 128), 1) % EX
    dst_ref[...] = jnp.zeros(dst_ref.shape, f32)
    low = pltpu.roll(src_ref[pl.ds(7, rows, stride=8), :], 1, 1)
    high = pltpu.roll(src_ref[pl.ds(0, rows, stride=8), :], 127, 1)
    dst_ref[pl.ds(0, rows, stride=8), :] = jnp.where(col > 0, low, 0.0)
    dst_ref[pl.ds(7, rows, stride=8), :] = jnp.where(col < EX - 1, high, 0.0)


def shift_y(src_ref, dst_ref, count):
    line = (iota((8, 128), 1) // EX) % EY
    dst_ref[...] = jnp.zeros(dst_ref.shape, f32)
    for k in range(count):
        low = pltpu.roll(src_ref[k * 64 + 56 : k * 64 + 64], EX, 1)
        high = pltpu.roll(src_ref[k * 64 : k * 64 + 8], 128 - EX, 1)
        dst_ref[k * 64 : k * 64 + 8] = jnp.where(line > 0, low, 0.0)
        dst_ref[k * 64 + 56 : k * 64 + 64] = jnp.where(line < EY - 1, high, 0.0)


def correction_shares(coef_ref, mass_ref, invd_ref, out_ref, next_ref, x_ref, y_ref, face_ref, side_ref):
    scaled = STEPS[0][1]
    next_ref[...] = mass_ref[...] * invd_ref[...] * scaled
    inner_planes(next_ref, coef_ref, out_ref, 0)
    shift_x(mass_ref, x_ref, NP)
    next_ref[...] = x_ref[...] * invd_ref[...] * scaled
    inner_planes(next_ref, coef_ref, out_ref, 64)
    shift_y(mass_ref, y_ref, NP)
    next_ref[...] = y_ref[...] * invd_ref[...] * scaled
    inner_planes(next_ref, coef_ref, out_ref, 128)
    shift_y(x_ref, y_ref, NP)
    next_ref[...] = y_ref[...] * invd_ref[...] * scaled
    inner_planes(next_ref, coef_ref, out_ref, 192)
    first = first_layer((8, 128))
    ends = end_rows()
    weights = [
        ends[c] * jnp.where(first, float(DERIV[c, 7]), float(DERIV[c, 0]))
        for c in range(8)
    ]
    for j in range(8):
        total = None
        for c in range(8):
            at = 1024 + c * 64 + j * 8
            term = coef_ref[at : at + 8] * weights[c]
            total = term if total is None else total + term
        at = slice(j * 8, j * 8 + 8)
        inv = blend(invd_ref[448 + j * 8 : 456 + j * 8], invd_ref[at])
        next_ref[at] = total * inv * scaled
    share = next_ref[0:64]
    face_ref[...] = pltpu.roll(blend(mass_ref[448:512], mass_ref[0:64]), LAYER, 1)
    out_ref[256:320] = share * face_ref[...]
    shift_x(face_ref, side_ref, 1)
    out_ref[320:384] = share * side_ref[...]
    shift_y(face_ref, next_ref.at[64:128], 1)
    out_ref[384:448] = share * next_ref[64:128]
    shift_y(side_ref, next_ref.at[64:128], 1)
    out_ref[448:512] = share * next_ref[64:128]


def correction_inner(shares, near, behind):
    node = iota((64, 128), 0)
    left, front = node % 8 == 0, node < 8
    total = None
    for base, row in ((0, near), (256, behind)):
        row = jnp.broadcast_to(row, (64, 128))

        def turn(count):
            return pltpu.roll(row, count % 128, 1)

        values = [
            row,
            jnp.where(left, turn(1), turn(-1)),
            jnp.where(front, turn(8), turn(-8)),
            jnp.where(
                front,
                jnp.where(left, turn(9), turn(7)),
                jnp.where(left, turn(-7), turn(-9)),
            ),
        ]
        for n, value in enumerate(values):
            at = base + n * 64
            term = shares[at : at + 64] * value
            total = term if total is None else total + term
    return total


def ghost_side(update_ref, inner, planes_ref, face_ref, side_ref):
    face_ref[...] = pltpu.roll(blend(update_ref[0:64], update_ref[448:512]), LAYER, 1)
    lines = [face_ref[pl.ds(i, 8, stride=8), :] for i in range(8)]
    res = apply_line(lines, lambda a: planes_ref[a * 8 : a * 8 + 8])
    for i in range(8):
        side_ref[pl.ds(i, 8, stride=8), :] = res[i]
    rows = [face_ref[j * 8 : j * 8 + 8] for j in range(8)]
    res = apply_line(rows, lambda b: planes_ref[64 + b * 8 : 72 + b * 8])
    for j in range(8):
        at = slice(j * 8, j * 8 + 8)
        side_ref[at] = (
            side_ref[at]
            + res[j]
            + planes_ref[128 + j * 8 : 136 + j * 8] * rows[j]
            + inner[at]
        )
    in_plane(side_ref, 1)


def plain8(table, v):
    out = []
    for i in range(8):
        total = None
        for a in range(8):
            if table[a, i] == 0.0:
                continue
            term = v[a] * float(table[a, i])
            total = term if total is None else total + term
        out.append(total)
    return out


def take_lanes(x, index):
    return jnp.take_along_axis(
        x, jnp.broadcast_to(index, x.shape), axis=1, mode="promise_in_bounds"
    )


def local_diagonal(coef_ref, mass_ref, diag_ref):
    squared = DERIV * DERIV

    def per_k(k, carry):
        base = pl.multiple_of(k * 64, 64)
        res = plain8(squared, [coef_ref[pl.ds(base + a * 8, 8), :] for a in range(8)])
        for i in range(8):
            diag_ref[pl.ds(base + i, 8, stride=8), :] = res[i]
        res = plain8(squared, [coef_ref[pl.ds(512 + base + b * 8, 8), :] for b in range(8)])
        for j in range(8):
            at = pl.ds(base + j * 8, 8)
            diag_ref[at, :] = diag_ref[at, :] + res[j] + mass_ref[at, :]
        return carry

    lax.fori_loop(0, 8, per_k, 0)

    def per_j(j, carry):
        base = pl.multiple_of(j * 8, 8)
        res = plain8(squared, [coef_ref[pl.ds(1024 + base + c * 64, 8), :] for c in range(8)])
        for k in range(8):
            at = pl.ds(base + k * 64, 8)
            diag_ref[at, :] = diag_ref[at, :] + res[k]
        return carry

    lax.fori_loop(0, 8, per_j, 0)


SHARE_ROW = 192
BASIS_ROW = SHARE_ROW + 256
GHOST_ROWS = BASIS_ROW + 512


def setup_kernel(
    order_ref,
    stiff_hbm,
    mass_hbm,
    field_hbm,
    load_hbm,
    basis_hbm,
    inverse_hbm,
    coef_ref,
    mass_ref,
    static_ref,
    faces_ref,
    invd_ref,
    inv_ref,
    basis_ref,
    solve_ref,
    order_out_ref,
    a_ref,
    b_ref,
    stiff_in,
    mass_in,
    field_in,
    load_in,
    basis_in,
    inverse_in,
    tmp_ref,
    start_ref,
    diag_ref,
    share_ref,
    x_ref,
    y_ref,
    face_ref,
    side_ref,
    sems,
):
    copies = [
        pltpu.make_async_copy(src, dst, sems.at[n])
        for n, (src, dst) in enumerate(
            [
                (stiff_hbm, stiff_in),
                (mass_hbm, mass_in),
                (field_hbm, field_in),
                (load_hbm, load_in),
                (basis_hbm, basis_in),
                (inverse_hbm, inverse_in),
            ]
        )
    ]
    for copy in copies:
        copy.start()
    order = order_ref[...]
    match = (iota((128, 128), 0) == order).astype(f32)
    inv = jnp.sum(match.T * iota((128, 128), 0).astype(f32), axis=0, keepdims=True)
    inv = inv.astype(jnp.int32)
    inv_ref[...] = inv
    order_out_ref[...] = order
    copies[0].wait()
    tmp_ref[...] = take_lanes(stiff_in[0:512, :], inv)
    for k in range(8):
        for i in range(8):
            coef_ref[k * 64 + i * 8 : k * 64 + i * 8 + 8, :] = tmp_ref[
                pl.ds(k * 64 + i, 8, stride=8), :
            ]
    coef_ref[512:1536, :] = take_lanes(stiff_in[512:1536, :], inv)
    for copy in copies[1:]:
        copy.wait()
    mass_ref[...] = take_lanes(mass_in[...], inv)
    start_ref[...] = take_lanes(field_in[...], inv)
    stiff_apply(start_ref, coef_ref, mass_ref, static_ref)
    static_ref[...] = take_lanes(load_in[...], inv) - static_ref[...]
    in_plane(static_ref)
    basis = dot_nn(match, basis_in[...], exact_mode)
    basis_ref[...] = basis
    solve_ref[...] = dot_nn(basis, inverse_in[...], exact_mode)
    local_diagonal(coef_ref, mass_ref, diag_ref)
    in_plane(diag_ref)
    zeros = jnp.zeros((64, 128), f32)
    invd_ref[...] = 1.0 / coupled(diag_ref, zeros, zeros)
    ends = end_rows()
    for j in range(8):
        total = None
        for c in range(8):
            at = 1024 + c * 64 + j * 8
            term = coef_ref[at : at + 8] * (ends[c] * ends[c])
            total = term if total is None else total + term
        tmp_ref[j * 8 : j * 8 + 8] = total
    planes = jnp.concatenate(
        [
            blend(coef_ref[0:64], coef_ref[448:512]),
            blend(coef_ref[512:576], coef_ref[960:1024]),
            blend(mass_ref[0:64], mass_ref[448:512]) + tmp_ref[0:64],
            blend(diag_ref[0:64], diag_ref[448:512]),
            blend(mass_ref[0:64], mass_ref[448:512]),
            zeros,
        ],
        axis=0,
    )
    faces_ref[0:64] = diag_ref[0:64]
    faces_ref[64:128] = diag_ref[448:512]
    even = where_am_i()[0]
    pack(planes, planes, a_ref, b_ref, 0, even)
    correction_shares(
        coef_ref, mass_ref, invd_ref, share_ref, tmp_ref, x_ref, y_ref, face_ref, side_ref
    )
    shares = share_ref[...]
    pack(shares, shares, a_ref, b_ref, SHARE_ROW, even)
    for c in range(NC // 128):
        at = BASIS_ROW + c * 128
        cols = basis[:, c * 128 : c * 128 + 128]
        a_ref[at : at + 128] = cols
        b_ref[at : at + 128] = cols


def send_first(y_ref, base, invd, coef_ref, next_ref, work_ref, a_ref, b_ref):
    zeros = jnp.zeros((64, 128), f32)
    inner = coupled(y_ref, zeros, zeros)
    if base is not None:
        inner = inner + base
    next_ref[...] = inner * invd * STEPS[0][1]
    send_planes(y_ref, next_ref, coef_ref, work_ref, a_ref, b_ref, where_am_i()[0])


def source_kernel(
    ret_ref,
    owner_ref,
    rank_ref,
    ids_ref,
    live_ref,
    inv_ref,
    static_ref,
    invd_ref,
    coef_ref,
    y_ref,
    a_ref,
    b_ref,
    next_ref,
    work_ref,
):
    rank = rank_ref[...].astype(jnp.int32)
    place = rank + jnp.where(rank >= HALF, 16 - HALF, 0)
    ids = ids_ref[...]
    live = iota((1, R_DEV), 1) < live_ref[0, 0]
    node = jnp.where(live, lax.shift_right_logical(ids, 7), -1)
    elem = jnp.bitwise_and(ids, 127)
    hits = (iota((OWNERS, R_DEV), 0) == owner_ref[...]).astype(f32)
    picked = dot_nn(ret_ref[...].T, hits, exact_mode)[0:32]
    value = jnp.sum(
        jnp.where(iota((32, R_DEV), 0) == place, picked, 0.0), axis=0, keepdims=True
    )
    at_node = (iota((NODES, R_DEV), 0) == node).astype(f32).astype(bf16)
    at_elem = (iota((128, R_DEV), 0) == elem).astype(f32).astype(bf16)
    spread = jnp.concatenate([at_elem * piece for piece in split3(value)], axis=0)
    landed = dot_nt(at_node, spread)
    landed = landed[:, 0:128] + landed[:, 128:256] + landed[:, 256:384]
    y_ref[...] = take_lanes(landed, inv_ref[...])
    in_plane(y_ref)
    y_ref[...] = y_ref[...] + static_ref[...]
    send_first(y_ref, None, invd_ref[...], coef_ref, next_ref, work_ref, a_ref, b_ref)


def opening_half(
    place,
    base_ref,
    y_ref,
    cur_in,
    raw,
    inner,
    invd_ref,
    planes_ref,
    coef_ref,
    mass_ref,
    res_ref,
    upd_ref,
    cur_ref,
    w_ref,
    a_out_ref,
    b_out_ref,
    next_ref,
    work_ref,
    face_ref,
    side_ref,
):
    residual = coupled(y_ref, raw, raw)
    if base_ref is not None:
        residual = residual + base_ref[...]
    update = residual * invd_ref[...] * STEPS[0][1]
    upd_ref[...] = update
    ghost_side(upd_ref, inner, planes_ref, face_ref, side_ref)
    stiff_apply(upd_ref, coef_ref, mass_ref, w_ref)
    in_plane(w_ref)
    residual = residual - coupled(w_ref, side_ref[...], side_ref[...])
    res_ref[...] = residual
    alpha, beta = STEPS[1]
    second = alpha * update + beta * invd_ref[...] * residual
    upd_ref[...] = second
    done = update + second
    cur_ref[...] = done if cur_in is None else cur_in + done
    stiff_apply(upd_ref, coef_ref, mass_ref, w_ref)
    in_plane(w_ref)
    alpha, beta = STEPS[2]
    zeros = jnp.zeros((64, 128), f32)
    next_ref[...] = alpha * upd_ref[...] + beta * invd_ref[...] * (
        res_ref[...] - coupled(w_ref, zeros, zeros)
    )
    send_planes(w_ref, next_ref, coef_ref, work_ref, a_out_ref, b_out_ref, place[0])


def start_kernel(
    y_ref,
    faces_ref,
    invd_in_ref,
    a_ref,
    b_ref,
    ga_ref,
    gb_ref,
    coef_ref,
    mass_ref,
    res_ref,
    upd_ref,
    cur_ref,
    w_ref,
    a_out_ref,
    b_out_ref,
    invd_ref,
    planes_ref,
    *scratch,
):
    place = where_am_i()
    planes = unpack(ga_ref, gb_ref, 0, SHARE_ROW, place)
    planes_ref[...] = planes[0:320]
    came = unpack(a_ref, b_ref, 0, 64, place)
    bottom, top = through(
        faces_ref[0:64], faces_ref[64:128], planes[192:256], planes[192:256]
    )
    invd_ref[...] = whole(1.0 / bottom, invd_in_ref, 1.0 / top)
    opening_half(
        place,
        None,
        y_ref,
        None,
        came[0:64],
        came[64:128],
        invd_ref,
        planes_ref,
        coef_ref,
        mass_ref,
        res_ref,
        upd_ref,
        cur_ref,
        w_ref,
        a_out_ref,
        b_out_ref,
        *scratch,
    )


def near_kernel(
    ga_ref, gb_ref, inverse_ref, after_ref, out_ref, shares_hbm, shares_ref, sems
):
    place = where_am_i()
    blocks = []
    for c in range(NC // 128):
        at = BASIS_ROW + c * 128
        below, above = beside(ga_ref[at : at + 128], gb_ref[at : at + 128], place)
        blocks.append(jnp.concatenate([above, below], axis=0))
    rows = jnp.concatenate(blocks, axis=1)
    shares_ref[...] = unpack(ga_ref, gb_ref, SHARE_ROW, 256, place)
    copy = pltpu.make_async_copy(shares_ref, shares_hbm, sems.at[0])
    copy.start()
    out_ref[...] = dot_nn(rows, inverse_ref[...], exact_mode)
    copy.wait()


def again_kernel(
    parts_ref,
    solve_ref,
    near_ref,
    shares_hbm,
    base_ref,
    a_ref,
    b_ref,
    invd_ref,
    planes_ref,
    coef_ref,
    mass_ref,
    res_ref,
    upd_ref,
    cur_ref,
    w_ref,
    a_out_ref,
    b_out_ref,
    y_ref,
    next_ref,
    work_ref,
    face_ref,
    side_ref,
    shares_ref,
    sems,
):
    copy = pltpu.make_async_copy(shares_hbm, shares_ref, sems.at[0])
    copy.start()
    place = where_am_i()
    total = parts_ref[0:8]
    for n in range(1, OWNERS * NC // 1024):
        total = total + parts_ref[n * 8 : n * 8 + 8]
    total = total + pltpu.roll(total, 4, 0)
    both = None
    for c in range(NC // 128):
        row = jnp.broadcast_to(total[c : c + 1], (8, 128))
        cols = slice(c * 128, c * 128 + 128)
        rows = jnp.concatenate([solve_ref[:, cols], near_ref[:, cols]], axis=0)
        term = dot_nt(row, rows, exact_mode)
        both = term if both is None else both + term
    correction = both[0:1, 0:128]
    above, below = both[0:1, 128:256], both[0:1, 256:384]
    first = first_layer((1, 128))
    near = jnp.where(first, above, below)
    behind = pltpu.roll(jnp.broadcast_to(jnp.where(first, below, above), (8, 128)), LAYER, 1)
    y_ref[...] = mass_ref[...] * (-correction)
    in_plane(y_ref)
    came = unpack(a_ref, b_ref, 0, 64, place)
    side_ref[...] = planes_ref[256:320] * near
    in_plane(side_ref, 1)
    raw = -(came[0:64] + side_ref[...])
    copy.wait()
    inner = came[64:128] - correction_inner(shares_ref, near, behind[0:1])
    opening_half(
        place,
        base_ref,
        y_ref,
        correction,
        raw,
        inner,
        invd_ref,
        planes_ref,
        coef_ref,
        mass_ref,
        res_ref,
        upd_ref,
        cur_ref,
        w_ref,
        a_out_ref,
        b_out_ref,
        next_ref,
        work_ref,
        face_ref,
        side_ref,
    )


def closing_half(
    w_ref,
    res_ref,
    upd_ref,
    cur_ref,
    invd_ref,
    a_ref,
    b_ref,
    planes_ref,
    coef_ref,
    mass_ref,
    work_ref,
    vec_ref,
    face_ref,
    side_ref,
):
    came = unpack(a_ref, b_ref, 0, 64, where_am_i())
    residual = res_ref[...] - coupled(w_ref, came[0:64], came[0:64])
    alpha, beta = STEPS[2]
    third = alpha * upd_ref[...] + beta * invd_ref[...] * residual
    vec_ref[...] = third
    ghost_side(vec_ref, came[64:128], planes_ref, face_ref, side_ref)
    stiff_apply(vec_ref, coef_ref, mass_ref, work_ref)
    in_plane(work_ref)
    residual = residual - coupled(work_ref, side_ref[...], side_ref[...])
    alpha, beta = STEPS[3]
    fourth = alpha * third + beta * invd_ref[...] * residual
    vec_ref[...] = fourth
    return residual, cur_ref[...] + (third + fourth)


def middle_kernel(
    w_ref,
    res_in_ref,
    upd_ref,
    cur_in_ref,
    invd_ref,
    a_ref,
    b_ref,
    planes_ref,
    coef_ref,
    mass_ref,
    basis_ref,
    ga_ref,
    gb_ref,
    local_ref,
    cur_hbm,
    part_ref,
    a_out_ref,
    b_out_ref,
    w_out_ref,
    vec_ref,
    cur_ref,
    next_ref,
    work_ref,
    face_ref,
    side_ref,
    sems,
):
    residual, current = closing_half(
        w_ref,
        res_in_ref,
        upd_ref,
        cur_in_ref,
        invd_ref,
        a_ref,
        b_ref,
            planes_ref,
        coef_ref,
        mass_ref,
        w_out_ref,
        vec_ref,
        face_ref,
        side_ref,
    )
    local_ref[...] = residual
    cur_ref[...] = current
    copy = pltpu.make_async_copy(cur_ref, cur_hbm, sems.at[0])
    copy.start()
    stiff_apply(vec_ref, coef_ref, mass_ref, w_out_ref)
    in_plane(w_out_ref)
    zeros = jnp.zeros((64, 128), f32)
    local = local_ref[...] - coupled(w_out_ref, zeros, zeros)
    local_ref[...] = local
    next_ref[...] = local * invd_ref[...] * STEPS[0][1]
    place = where_am_i()
    send_planes(w_out_ref, next_ref, coef_ref, work_ref, a_out_ref, b_out_ref, place[0])
    sums = jnp.sum(local, axis=0, keepdims=True)
    bottom = -jnp.sum(w_out_ref[0:64], axis=0, keepdims=True)
    top = -jnp.sum(w_out_ref[448:512], axis=0, keepdims=True)
    outer = jnp.where(first_layer((1, 128)), bottom, top)
    left = jnp.broadcast_to(jnp.concatenate([sums, outer], axis=1), (8, 256))
    blocks = []
    for c in range(NC // 128):
        at = BASIS_ROW + c * 128
        below, above = beside(ga_ref[at : at + 128], gb_ref[at : at + 128], place)
        own = basis_ref[:, c * 128 : c * 128 + 128]
        right = jnp.concatenate([own, below[LAYER:], above[:LAYER]], axis=0)
        part = dot_nn(left, right, exact_mode)[0:1]
        blocks.append(part * (1.0 / math.sqrt(NODES)))
    eight = jnp.concatenate(blocks + blocks, axis=0)
    for n in range(OWNERS * NC // 1024):
        part_ref[n * 8 : n * 8 + 8] = eight
    copy.wait()


def last_kernel(*refs):
    inputs, (order_ref, field_hbm, first_hbm, out_ref), rest = (
        refs[:10],
        refs[10:14],
        refs[14:],
    )
    scratch, (field_in, first_in, sems) = rest[:-3], rest[-3:]
    copies = [
        pltpu.make_async_copy(field_hbm, field_in, sems.at[0]),
        pltpu.make_async_copy(first_hbm, first_in, sems.at[1]),
    ]
    for copy in copies:
        copy.start()
    current = closing_half(*inputs, *scratch)[1]
    for copy in copies:
        copy.wait()
    moved = take_lanes(first_in[...] + current, order_ref[...])
    out_ref[...] = field_in[...] + moved


def call(kernel, outs, *args, scratch=(), smem=(), far=(), near=(), copies=0, away=()):
    def stay(x):
        return pltpu.with_memory_space_constraint(x, pltpu.HBM)

    def space(n):
        if n in smem:
            return pltpu.SMEM
        return pltpu.HBM if n in far else pltpu.VMEM

    scratches = [pltpu.VMEM(s, f32) for s in scratch]
    if copies:
        scratches.append(pltpu.SemaphoreType.DMA((copies,)))
    return pl.pallas_call(
        kernel,
        out_shape=[
            pltpu.HBM(s, d) if n in away else jax.ShapeDtypeStruct(s, d)
            for n, (s, d) in enumerate(outs)
        ],
        in_specs=[pl.BlockSpec(memory_space=space(n)) for n in range(len(args))],
        out_specs=[
            pl.BlockSpec(memory_space=pltpu.HBM if n in away else pltpu.VMEM)
            for n in range(len(outs))
        ],
        scratch_shapes=scratches,
        compiler_params=pltpu.CompilerParams(vmem_limit_bytes=20 << 20),
    )(*[stay(x) if n in far + near else x for n, x in enumerate(args)])


FIELD = ((NODES, 128), f32)
SIDE_MSG = ((64, 128), f32)
GHOST_MSG = ((GHOST_ROWS, 128), f32)
SIDE_WORK = [(64, 128), (64, 128)]
SEND_WORK = [(NODES, 128), (128, 128)]


def exchange(a, b):
    count = lax.axis_size("elem")
    pairs_a, pairs_b = [], []
    for d in range(2 * count):
        base, slab = d - d % count, d % count
        pairs_a.append((d, base + (slab ^ 1)))
        other = slab + (1 if slab % 2 else -1)
        inside = 0 <= other < count
        pairs_b.append((d, base + other if inside else (d + count) % (2 * count)))
    axes = ("sess", "elem")
    b = lax.ppermute(b, axes, pairs_b)
    a = lax.ppermute(a, axes, pairs_a)
    return a, b


def one_device(
    pressure,
    load,
    stiffness,
    helm_mass,
    order_slots,
    recv_ids,
    donor_owner,
    donor_slot,
    interp_weights,
    live_count,
    coarse_basis,
    coarse_inverse,
):
    own_field = pressure.reshape(NODES, 128)
    order = order_slots.reshape(1, 128)
    owner = donor_owner.reshape(1, R_DEV)
    other_field = lax.ppermute(own_field, "sess", [(0, 1), (1, 0)])

    send, rank, owner, ids = call(
        request_kernel,
        [
            ((OWNERS * ASK, 128), f32),
            ((1, R_DEV), f32),
            ((1, R_DEV), jnp.int32),
            ((1, R_DEV), jnp.int32),
        ],
        owner,
        donor_slot,
        interp_weights.reshape(3 * NP, R_DEV),
        recv_ids,
        near=(0, 1, 2, 3),
    )
    received = lax.all_to_all(
        send.reshape(OWNERS, ASK, 128), "elem", split_axis=0, concat_axis=0, tiled=True
    )
    coef, mass, static, faces, invd, inv, basis, solve, order, ga, gb = call(
        setup_kernel,
        [
            ((3 * NODES, 128), f32),
            FIELD,
            FIELD,
            ((128, 128), f32),
            FIELD,
            ((1, 128), jnp.int32),
            ((128, NC), f32),
            ((128, NC), f32),
            ((1, 128), jnp.int32),
            GHOST_MSG,
            GHOST_MSG,
        ],
        order,
        stiffness.reshape(3 * NODES, 128),
        helm_mass.reshape(NODES, 128),
        own_field,
        load.reshape(NODES, 128),
        coarse_basis.reshape(128, NC),
        coarse_inverse.reshape(NC, NC),
        near=(0,),
        far=(1, 2, 3, 4, 5, 6),
        scratch=[
            (3 * NODES, 128),
            (NODES, 128),
            (NODES, 128),
            (NODES, 128),
            (128, NC),
            (NC, NC),
            (NODES, 128),
            (NODES, 128),
            (NODES, 128),
            (NODES, 128),
            (NODES, 128),
            (NODES, 128),
            (64, 128),
            (64, 128),
        ],
        copies=6,
    )
    answer, inv = call(
        owner_kernel,
        [((OWNERS, 128), f32), ((1, 128), jnp.int32)],
        received.reshape(OWNERS * ASK, 128),
        other_field,
        inv,
    )
    answered = lax.all_to_all(answer, "elem", split_axis=0, concat_axis=0, tiled=True)
    ga, gb = exchange(ga, gb)
    y, a, b = call(
        source_kernel,
        [FIELD, SIDE_MSG, SIDE_MSG],
        answered,
        owner,
        rank,
        ids,
        live_count,
        inv,
        static,
        invd,
        coef,
        smem=(4,),
        scratch=SEND_WORK,
    )
    a, b = exchange(a, b)
    half = [FIELD, FIELD, FIELD, FIELD, SIDE_MSG, SIDE_MSG]
    res, upd, cur, w, a, b, invd, planes = call(
        start_kernel,
        half + [FIELD, ((320, 128), f32)],
        y,
        faces,
        invd,
        a,
        b,
        ga,
        gb,
        coef,
        mass,
        scratch=SEND_WORK + SIDE_WORK,
    )
    near, shares = call(
        near_kernel,
        [((256, NC), f32), FIELD],
        ga,
        gb,
        coarse_inverse.reshape(NC, NC),
        a,
        near=(2,),
        scratch=[(NODES, 128)],
        copies=1,
        away=(1,),
    )
    a, b = exchange(a, b)
    res, total, part, a, b = call(
        middle_kernel,
        [FIELD, FIELD, ((OWNERS * NC // 128, 128), f32), SIDE_MSG, SIDE_MSG],
        w,
        res,
        upd,
        cur,
        invd,
        a,
        b,
        planes,
        coef,
        mass,
        basis,
        ga,
        gb,
        scratch=[(NODES, 128)] * 3 + SEND_WORK + SIDE_WORK,
        copies=1,
        away=(1,),
    )
    parts = lax.all_to_all(
        part.reshape(OWNERS, NC // 128, 128),
        "elem",
        split_axis=0,
        concat_axis=0,
        tiled=True,
    )
    a, b = exchange(a, b)
    res, upd, cur, w, a, b = call(
        again_kernel,
        half,
        parts.reshape(OWNERS * NC // 128, 128),
        solve,
        near,
        shares,
        res,
        a,
        b,
        invd,
        planes,
        coef,
        mass,
        far=(3,),
        scratch=[(NODES, 128)] + SEND_WORK + SIDE_WORK + [(NODES, 128)],
        copies=1,
    )
    a, b = exchange(a, b)
    (out,) = call(
        last_kernel,
        [FIELD],
        w,
        res,
        upd,
        cur,
        invd,
        a,
        b,
        planes,
        coef,
        mass,
        order,
        own_field,
        total,
        far=(11, 12),
        scratch=[(NODES, 128)] * 2 + SIDE_WORK + [(NODES, 128)] * 2,
        copies=2,
    )
    return out.reshape(1, NP, NP, NP, 128)


def solution(mesh):
    return jax.shard_map(
        one_device,
        mesh=mesh,
        in_specs=(
            P("sess", None, None, None, "elem"),
            P("sess", None, None, None, "elem"),
            P("sess", None, None, None, None, "elem"),
            P("sess", None, None, None, "elem"),
            P("sess", "elem", None),
            P("sess", "elem"),
            P("sess", "elem", None),
            P("sess", "elem"),
            P("sess", None, "elem"),
            P("sess", "elem"),
            P("sess", "elem", None),
            P("sess", None, None),
        ),
        out_specs=P("sess", None, None, None, "elem"),
        check_vma=False,
    )
```

```python
import math

import jax
import jax.numpy as jnp
import numpy as np
from jax import lax
from jax.experimental import pallas as pl
from jax.experimental.pallas import tpu as pltpu
from jax.sharding import PartitionSpec as P


NP = 8
EX = 8
EY = 8
LAYER = EX * EY
NODES = NP**3
R_DEV = 1024
NC = 512
CHEB = 4
OWNERS = 64
COMPS = 32
HALF = 12
ASK = 6

exact_mode = lax.Precision.HIGHEST
spectrum_high = 8.0
spectrum_low = 0.8
f32 = jnp.float32
bf16 = jnp.bfloat16


def gll_derivative():
    x = np.array(
        [
            -1.0,
            -0.8717401485096066,
            -0.5917001814331423,
            -0.2092992179024789,
            0.2092992179024789,
            0.5917001814331423,
            0.8717401485096066,
            1.0,
        ]
    )
    legendre = (429.0 * x**7 - 693.0 * x**5 + 315.0 * x**3 - 35.0 * x) / 16.0
    distance = x[:, None] - x[None, :]
    same = np.eye(8, dtype=bool)
    table = legendre[:, None] / (legendre[None, :] * np.where(same, 1.0, distance))
    corner = np.zeros((8, 8))
    corner[0, 0] = -14.0
    corner[7, 7] = 14.0
    return np.where(same, corner, table).astype(np.float32).astype(np.float64)


DERIV = gll_derivative()


def chebyshev():
    center = 0.5 * (spectrum_high + spectrum_low)
    half_width = 0.5 * (spectrum_high - spectrum_low)
    sigma_ratio = center / half_width
    rho = 1.0 / sigma_ratio
    steps = [(0.0, 1.0 / center)]
    for _ in range(CHEB - 1):
        rho_next = 1.0 / (2.0 * sigma_ratio - rho)
        steps.append((rho_next * rho, 2.0 * rho_next / half_width))
        rho = rho_next
    return steps


STEPS = chebyshev()


def split3(x):
    hi = x.astype(bf16)
    rest = x - hi.astype(f32)
    mid = rest.astype(bf16)
    low = (rest - mid.astype(f32)).astype(bf16)
    return hi, mid, low


def dot_nn(a, b, precision=None):
    return lax.dot_general(
        a, b, (((1,), (0,)), ((), ())), precision=precision, preferred_element_type=f32
    )


def dot_nt(a, b, precision=None):
    return lax.dot_general(
        a, b, (((1,), (1,)), ((), ())), precision=precision, preferred_element_type=f32
    )


def iota(shape, axis):
    return lax.broadcasted_iota(jnp.int32, shape, axis)


def request_kernel(
    owner_ref, slot_ref, weight_ref, ids_ref, send_ref, rank_ref, owner_out_ref, ids_out_ref
):
    owner = owner_ref[...]
    hits = iota((OWNERS, R_DEV), 0) == owner
    hits_f = hits.astype(f32)
    hits_b = hits_f.astype(bf16)
    upper = (iota((128, 128), 0) < iota((128, 128), 1)).astype(f32).astype(bf16)
    carry = jnp.zeros((OWNERS, 1), f32)
    ranks = []
    for b in range(R_DEV // 128):
        cols = slice(b * 128, b * 128 + 128)
        block = hits_f[:, cols]
        count = dot_nn(hits_b[:, cols], upper) + carry
        ranks.append(jnp.sum(block * count, axis=0, keepdims=True))
        carry = carry + jnp.sum(block, axis=1, keepdims=True)
    rank = jnp.concatenate(ranks, axis=1)
    rank_ref[...] = rank
    owner_out_ref[...] = owner
    ids_out_ref[...] = ids_ref[...]
    payload = jnp.concatenate(
        [
            weight_ref[...],
            jnp.broadcast_to(slot_ref[...].astype(f32), (COMPS - 3 * NP, R_DEV)),
        ],
        axis=0,
    )
    pieces = split3(payload)
    total = None
    for piece in pieces:
        rows = [
            piece * (rank == float(m)).astype(f32).astype(bf16) for m in range(2 * HALF)
        ]
        part = dot_nt(hits_b, jnp.concatenate(rows, axis=0))
        total = part if total is None else total + part
    for c in range(ASK):
        if c < 2 * HALF * COMPS // 128:
            block = total[:, c * 128 : c * 128 + 128]
        else:
            block = jnp.zeros((OWNERS, 128), f32)
        send_ref[pl.ds(c, OWNERS, stride=ASK), :] = block


def owner_kernel(recv_ref, field_ref, before_ref, ret_ref, after_ref):
    cols = [recv_ref[pl.ds(c, OWNERS, stride=ASK), :] for c in range(6)]
    packed = jnp.concatenate(
        [jnp.concatenate(cols[:3], axis=1), jnp.concatenate(cols[3:], axis=1)], axis=0
    )
    comps = packed.T
    pieces = jnp.concatenate(split3(field_ref[...]), axis=1)
    rows = []
    for pair in range(HALF // 2):
        a = comps[(2 * pair) * COMPS : (2 * pair + 1) * COMPS]
        b = comps[(2 * pair + 1) * COMPS : (2 * pair + 2) * COMPS]
        both = jnp.concatenate([a, b], axis=1)
        slot = both[3 * NP : 3 * NP + 1].astype(jnp.int32)
        pick = (iota((128, 256), 0) == slot).astype(f32).astype(bf16)
        gathered = dot_nn(pieces, jnp.concatenate([pick, pick, pick], axis=0))
        wx = both[0:NP]
        wy = both[NP : 2 * NP]
        wz = both[2 * NP : 3 * NP]
        acc = None
        for k in range(NP):
            line = None
            for j in range(NP):
                row = (k * NP + j) * NP
                term = gathered[row : row + NP] * wy[j : j + 1]
                line = term if line is None else line + term
            line = line * wz[k : k + 1]
            acc = line if acc is None else acc + line
        value = jnp.sum(acc * wx, axis=0, keepdims=True)
        rows.append(value[:, :128])
        rows.append(value[:, 128:])
    rows.append(jnp.zeros((128 - HALF, 128), f32))
    turned = jnp.concatenate(rows, axis=0).T
    ret_ref[...] = turned[:OWNERS] + pltpu.roll(turned[OWNERS:], 16, 1)
    after_ref[...] = before_ref[...]


def deriv8(table, v):
    plus = [v[m] + v[7 - m] for m in range(4)]
    minus = [v[m] - v[7 - m] for m in range(4)]
    out = [None] * 8
    for a in range(4):
        even = odd = None
        for m in range(4):
            ce = 0.5 * (table[a, m] + table[a, 7 - m])
            co = 0.5 * (table[a, m] - table[a, 7 - m])
            te = plus[m] * float(ce)
            to = minus[m] * float(co)
            even = te if even is None else even + te
            odd = to if odd is None else odd + to
        out[a] = odd + even
        out[7 - a] = odd - even
    return out


def apply_line(v, coef):
    grad = deriv8(DERIV, v)
    return deriv8(DERIV.T, [grad[a] * coef(a) for a in range(8)])


def stiff_apply(v_ref, coef_ref, mass_ref, out_ref):
    def per_k(k, carry):
        base = pl.multiple_of(k * 64, 64)
        lines = [v_ref[pl.ds(base + i, 8, stride=8), :] for i in range(8)]
        res = apply_line(lines, lambda a: coef_ref[pl.ds(base + a * 8, 8), :])
        for i in range(8):
            out_ref[pl.ds(base + i, 8, stride=8), :] = res[i]
        rows = [v_ref[pl.ds(base + j * 8, 8), :] for j in range(8)]
        res = apply_line(rows, lambda b: coef_ref[pl.ds(512 + base + b * 8, 8), :])
        for j in range(8):
            at = pl.ds(base + j * 8, 8)
            out_ref[at, :] = out_ref[at, :] + res[j] + mass_ref[at, :] * rows[j]
        return carry

    lax.fori_loop(0, 8, per_k, 0)

    def per_j(j, carry):
        base = pl.multiple_of(j * 8, 8)
        cols = [v_ref[pl.ds(base + k * 64, 8), :] for k in range(8)]
        res = apply_line(cols, lambda c: coef_ref[pl.ds(1024 + base + c * 64, 8), :])
        for k in range(8):
            at = pl.ds(base + k * 64, 8)
            out_ref[at, :] = out_ref[at, :] + res[k]
        return carry

    lax.fori_loop(0, 8, per_j, 0)


def couple(high, low, shift, pos, count):
    lanes = high.shape[-1]
    next_low = pltpu.roll(low, lanes - shift, high.ndim - 1)
    prev_high = pltpu.roll(high, shift, high.ndim - 1)
    new_high = high + jnp.where(pos < count - 1, next_low, 0.0)
    new_low = low + jnp.where(pos > 0, prev_high, 0.0)
    return new_high, new_low


def in_plane(ref, count=NP):
    rows = count * NP
    col = iota((rows, 128), 1) % EX
    high, low = couple(
        ref[pl.ds(7, rows, stride=8), :], ref[pl.ds(0, rows, stride=8), :], 1, col, EX
    )
    ref[pl.ds(7, rows, stride=8), :] = high
    ref[pl.ds(0, rows, stride=8), :] = low
    line = (iota((8, 128), 1) // EX) % EY
    for k in range(count):
        high, low = couple(
            ref[k * 64 + 56 : k * 64 + 64], ref[k * 64 : k * 64 + 8], EX, line, EY
        )
        ref[k * 64 + 56 : k * 64 + 64] = high
        ref[k * 64 : k * 64 + 8] = low


def through(bottom, top, below, above):
    first = iota(bottom.shape, 1) < LAYER
    new_bottom = bottom + pltpu.roll(jnp.where(first, top, below), LAYER, 1)
    new_top = top + pltpu.roll(jnp.where(first, above, bottom), LAYER, 1)
    return new_bottom, new_top


def whole(bottom, ref, top):
    return jnp.concatenate([bottom, ref[64:448], top], axis=0)


def coupled(w_ref, below, above):
    bottom, top = through(w_ref[0:64], w_ref[448:512], below, above)
    return whole(bottom, w_ref, top)


def where_am_i():
    me = lax.axis_index("elem")
    last = lax.axis_size("elem") - 1
    return jnp.bitwise_and(me, 1) == 0, me > 0, me < last


def first_layer(shape):
    return iota(shape, 1) < LAYER


def pack(up, down, a_ref, b_ref, row, even):
    half = up.shape[0] // 2
    first = first_layer((half, 128))
    up = jnp.where(first, pltpu.roll(up[:half], LAYER, 1), up[half:])
    down = jnp.where(first, down[:half], pltpu.roll(down[half:], LAYER, 1))
    a_ref[row : row + half] = jnp.where(even, up, down)
    b_ref[row : row + half] = jnp.where(even, down, up)


def beside(a, b, place):
    even, has_below, has_above = place
    below = jnp.where(has_below, jnp.where(even, b, a), 0.0)
    above = jnp.where(has_above, jnp.where(even, a, b), 0.0)
    return below, above


def unpack(a_ref, b_ref, row, half, place):
    below, above = beside(a_ref[row : row + half], b_ref[row : row + half], place)
    first = first_layer(below.shape)
    low = jnp.where(first, above, pltpu.roll(below, LAYER, 1))
    high = jnp.where(first, pltpu.roll(above, LAYER, 1), below)
    return jnp.concatenate([low, high], axis=0)


def blend(bottom, top):
    return jnp.where(first_layer(bottom.shape), bottom, top)


def end_rows():
    first = first_layer((8, 128))
    return [
        jnp.where(first, float(DERIV[c, 0]), float(DERIV[c, 7])).astype(f32)
        for c in range(8)
    ]


def inner_planes(next_ref, coef_ref, out_ref, row):
    first = first_layer((8, 128))
    ends = end_rows()
    for j in range(8):
        cols = [next_ref[k * 64 + j * 8 : k * 64 + j * 8 + 8] for k in range(8)]
        cols[0] = jnp.where(first, 0.0, cols[0])
        cols[7] = jnp.where(first, cols[7], 0.0)
        grad = deriv8(DERIV, cols)
        total = None
        for c in range(8):
            at = 1024 + c * 64 + j * 8
            term = grad[c] * coef_ref[at : at + 8] * ends[c]
            total = term if total is None else total + term
        out_ref[row + j * 8 : row + j * 8 + 8] = total


def send_planes(w_ref, next_ref, coef_ref, work_ref, a_ref, b_ref, even):
    work_ref[0:64] = blend(w_ref[0:64], w_ref[448:512])
    inner_planes(next_ref, coef_ref, work_ref, 64)
    both = work_ref[...]
    pack(both, both, a_ref, b_ref, 0, even)


def shift_x(src_ref, dst_ref, count):
    rows = count * NP
    col = iota((rows, 128), 1) % EX
    dst_ref[...] = jnp.zeros(dst_ref.shape, f32)
    low = pltpu.roll(src_ref[pl.ds(7, rows, stride=8), :], 1, 1)
    high = pltpu.roll(src_ref[pl.ds(0, rows, stride=8), :], 127, 1)
    dst_ref[pl.ds(0, rows, stride=8), :] = jnp.where(col > 0, low, 0.0)
    dst_ref[pl.ds(7, rows, stride=8), :] = jnp.where(col < EX - 1, high, 0.0)


def shift_y(src_ref, dst_ref, count):
    line = (iota((8, 128), 1) // EX) % EY
    dst_ref[...] = jnp.zeros(dst_ref.shape, f32)
    for k in range(count):
        low = pltpu.roll(src_ref[k * 64 + 56 : k * 64 + 64], EX, 1)
        high = pltpu.roll(src_ref[k * 64 : k * 64 + 8], 128 - EX, 1)
        dst_ref[k * 64 : k * 64 + 8] = jnp.where(line > 0, low, 0.0)
        dst_ref[k * 64 + 56 : k * 64 + 64] = jnp.where(line < EY - 1, high, 0.0)


def correction_shares(coef_ref, mass_ref, invd_ref, out_ref, next_ref, x_ref, y_ref, face_ref, side_ref):
    scaled = STEPS[0][1]
    next_ref[...] = mass_ref[...] * invd_ref[...] * scaled
    inner_planes(next_ref, coef_ref, out_ref, 0)
    shift_x(mass_ref, x_ref, NP)
    next_ref[...] = x_ref[...] * invd_ref[...] * scaled
    inner_planes(next_ref, coef_ref, out_ref, 64)
    shift_y(mass_ref, y_ref, NP)
    next_ref[...] = y_ref[...] * invd_ref[...] * scaled
    inner_planes(next_ref, coef_ref, out_ref, 128)
    shift_y(x_ref, y_ref, NP)
    next_ref[...] = y_ref[...] * invd_ref[...] * scaled
    inner_planes(next_ref, coef_ref, out_ref, 192)
    first = first_layer((8, 128))
    ends = end_rows()
    weights = [
        ends[c] * jnp.where(first, float(DERIV[c, 7]), float(DERIV[c, 0]))
        for c in range(8)
    ]
    for j in range(8):
        total = None
        for c in range(8):
            at = 1024 + c * 64 + j * 8
            term = coef_ref[at : at + 8] * weights[c]
            total = term if total is None else total + term
        at = slice(j * 8, j * 8 + 8)
        inv = blend(invd_ref[448 + j * 8 : 456 + j * 8], invd_ref[at])
        next_ref[at] = total * inv * scaled
    share = next_ref[0:64]
    face_ref[...] = pltpu.roll(blend(mass_ref[448:512], mass_ref[0:64]), LAYER, 1)
    out_ref[256:320] = share * face_ref[...]
    shift_x(face_ref, side_ref, 1)
    out_ref[320:384] = share * side_ref[...]
    shift_y(face_ref, next_ref.at[64:128], 1)
    out_ref[384:448] = share * next_ref[64:128]
    shift_y(side_ref, next_ref.at[64:128], 1)
    out_ref[448:512] = share * next_ref[64:128]


def correction_inner(shares, near, behind):
    node = iota((64, 128), 0)
    left, front = node % 8 == 0, node < 8
    total = None
    for base, row in ((0, near), (256, behind)):
        row = jnp.broadcast_to(row, (64, 128))

        def turn(count):
            return pltpu.roll(row, count % 128, 1)

        values = [
            row,
            jnp.where(left, turn(1), turn(-1)),
            jnp.where(front, turn(8), turn(-8)),
            jnp.where(
                front,
                jnp.where(left, turn(9), turn(7)),
                jnp.where(left, turn(-7), turn(-9)),
            ),
        ]
        for n, value in enumerate(values):
            at = base + n * 64
            term = shares[at : at + 64] * value
            total = term if total is None else total + term
    return total


def ghost_side(update_ref, inner, planes_ref, face_ref, side_ref):
    face_ref[...] = pltpu.roll(blend(update_ref[0:64], update_ref[448:512]), LAYER, 1)
    lines = [face_ref[pl.ds(i, 8, stride=8), :] for i in range(8)]
    res = apply_line(lines, lambda a: planes_ref[a * 8 : a * 8 + 8])
    for i in range(8):
        side_ref[pl.ds(i, 8, stride=8), :] = res[i]
    rows = [face_ref[j * 8 : j * 8 + 8] for j in range(8)]
    res = apply_line(rows, lambda b: planes_ref[64 + b * 8 : 72 + b * 8])
    for j in range(8):
        at = slice(j * 8, j * 8 + 8)
        side_ref[at] = (
            side_ref[at]
            + res[j]
            + planes_ref[128 + j * 8 : 136 + j * 8] * rows[j]
            + inner[at]
        )
    in_plane(side_ref, 1)


def plain8(table, v):
    out = []
    for i in range(8):
        total = None
        for a in range(8):
            if table[a, i] == 0.0:
                continue
            term = v[a] * float(table[a, i])
            total = term if total is None else total + term
        out.append(total)
    return out


def take_lanes(x, index):
    return jnp.take_along_axis(
        x, jnp.broadcast_to(index, x.shape), axis=1, mode="promise_in_bounds"
    )


def local_diagonal(coef_ref, mass_ref, diag_ref):
    squared = DERIV * DERIV

    def per_k(k, carry):
        base = pl.multiple_of(k * 64, 64)
        res = plain8(squared, [coef_ref[pl.ds(base + a * 8, 8), :] for a in range(8)])
        for i in range(8):
            diag_ref[pl.ds(base + i, 8, stride=8), :] = res[i]
        res = plain8(squared, [coef_ref[pl.ds(512 + base + b * 8, 8), :] for b in range(8)])
        for j in range(8):
            at = pl.ds(base + j * 8, 8)
            diag_ref[at, :] = diag_ref[at, :] + res[j] + mass_ref[at, :]
        return carry

    lax.fori_loop(0, 8, per_k, 0)

    def per_j(j, carry):
        base = pl.multiple_of(j * 8, 8)
        res = plain8(squared, [coef_ref[pl.ds(1024 + base + c * 64, 8), :] for c in range(8)])
        for k in range(8):
            at = pl.ds(base + k * 64, 8)
            diag_ref[at, :] = diag_ref[at, :] + res[k]
        return carry

    lax.fori_loop(0, 8, per_j, 0)


SHARE_ROW = 192
BASIS_ROW = SHARE_ROW + 256
GHOST_ROWS = BASIS_ROW + 512


def setup_kernel(
    order_ref,
    stiff_hbm,
    mass_hbm,
    field_hbm,
    load_hbm,
    basis_hbm,
    coef_ref,
    mass_ref,
    static_ref,
    faces_ref,
    invd_ref,
    inv_ref,
    basis_ref,
    order_out_ref,
    a_ref,
    b_ref,
    stiff_in,
    mass_in,
    field_in,
    load_in,
    basis_in,
    tmp_ref,
    start_ref,
    diag_ref,
    share_ref,
    x_ref,
    y_ref,
    face_ref,
    side_ref,
    sems,
):
    copies = [
        pltpu.make_async_copy(src, dst, sems.at[n])
        for n, (src, dst) in enumerate(
            [
                (stiff_hbm, stiff_in),
                (mass_hbm, mass_in),
                (field_hbm, field_in),
                (load_hbm, load_in),
                (basis_hbm, basis_in),
            ]
        )
    ]
    for copy in copies:
        copy.start()
    order = order_ref[...]
    match = (iota((128, 128), 0) == order).astype(f32)
    inv = jnp.sum(match.T * iota((128, 128), 0).astype(f32), axis=0, keepdims=True)
    inv = inv.astype(jnp.int32)
    inv_ref[...] = inv
    order_out_ref[...] = order
    copies[0].wait()
    tmp_ref[...] = take_lanes(stiff_in[0:512, :], inv)
    for k in range(8):
        for i in range(8):
            coef_ref[k * 64 + i * 8 : k * 64 + i * 8 + 8, :] = tmp_ref[
                pl.ds(k * 64 + i, 8, stride=8), :
            ]
    coef_ref[512:1536, :] = take_lanes(stiff_in[512:1536, :], inv)
    for copy in copies[1:]:
        copy.wait()
    mass_ref[...] = take_lanes(mass_in[...], inv)
    start_ref[...] = take_lanes(field_in[...], inv)
    stiff_apply(start_ref, coef_ref, mass_ref, static_ref)
    static_ref[...] = take_lanes(load_in[...], inv) - static_ref[...]
    in_plane(static_ref)
    basis = dot_nn(match, basis_in[...], exact_mode)
    basis_ref[...] = basis
    local_diagonal(coef_ref, mass_ref, diag_ref)
    in_plane(diag_ref)
    zeros = jnp.zeros((64, 128), f32)
    invd_ref[...] = 1.0 / coupled(diag_ref, zeros, zeros)
    ends = end_rows()
    for j in range(8):
        total = None
        for c in range(8):
            at = 1024 + c * 64 + j * 8
            term = coef_ref[at : at + 8] * (ends[c] * ends[c])
            total = term if total is None else total + term
        tmp_ref[j * 8 : j * 8 + 8] = total
    planes = jnp.concatenate(
        [
            blend(coef_ref[0:64], coef_ref[448:512]),
            blend(coef_ref[512:576], coef_ref[960:1024]),
            blend(mass_ref[0:64], mass_ref[448:512]) + tmp_ref[0:64],
            blend(diag_ref[0:64], diag_ref[448:512]),
            blend(mass_ref[0:64], mass_ref[448:512]),
            zeros,
        ],
        axis=0,
    )
    faces_ref[0:64] = diag_ref[0:64]
    faces_ref[64:128] = diag_ref[448:512]
    even = where_am_i()[0]
    pack(planes, planes, a_ref, b_ref, 0, even)
    correction_shares(
        coef_ref, mass_ref, invd_ref, share_ref, tmp_ref, x_ref, y_ref, face_ref, side_ref
    )
    shares = share_ref[...]
    pack(shares, shares, a_ref, b_ref, SHARE_ROW, even)
    for c in range(NC // 128):
        at = BASIS_ROW + c * 128
        cols = basis[:, c * 128 : c * 128 + 128]
        a_ref[at : at + 128] = cols
        b_ref[at : at + 128] = cols


def send_first(y_ref, base, invd, coef_ref, next_ref, work_ref, a_ref, b_ref):
    zeros = jnp.zeros((64, 128), f32)
    inner = coupled(y_ref, zeros, zeros)
    if base is not None:
        inner = inner + base
    next_ref[...] = inner * invd * STEPS[0][1]
    send_planes(y_ref, next_ref, coef_ref, work_ref, a_ref, b_ref, where_am_i()[0])


def source_kernel(
    ret_ref,
    owner_ref,
    rank_ref,
    ids_ref,
    live_ref,
    inv_ref,
    static_ref,
    invd_ref,
    coef_ref,
    y_ref,
    a_ref,
    b_ref,
    next_ref,
    work_ref,
):
    rank = rank_ref[...].astype(jnp.int32)
    place = rank + jnp.where(rank >= HALF, 16 - HALF, 0)
    ids = ids_ref[...]
    live = iota((1, R_DEV), 1) < live_ref[0, 0]
    node = jnp.where(live, lax.shift_right_logical(ids, 7), -1)
    elem = jnp.bitwise_and(ids, 127)
    hits = (iota((OWNERS, R_DEV), 0) == owner_ref[...]).astype(f32).astype(bf16)
    answers = jnp.concatenate(split3(ret_ref[...].T[0:32]), axis=0)
    picked = dot_nn(answers, hits)
    picked = picked[0:32] + picked[32:64] + picked[64:96]
    value = jnp.sum(
        jnp.where(iota((32, R_DEV), 0) == place, picked, 0.0), axis=0, keepdims=True
    )
    at_node = (iota((NODES, R_DEV), 0) == node).astype(f32).astype(bf16)
    at_elem = (iota((128, R_DEV), 0) == elem).astype(f32).astype(bf16)
    spread = jnp.concatenate([at_elem * piece for piece in split3(value)], axis=0)
    landed = dot_nt(at_node, spread)
    landed = landed[:, 0:128] + landed[:, 128:256] + landed[:, 256:384]
    y_ref[...] = take_lanes(landed, inv_ref[...])
    in_plane(y_ref)
    y_ref[...] = y_ref[...] + static_ref[...]
    send_first(y_ref, None, invd_ref[...], coef_ref, next_ref, work_ref, a_ref, b_ref)


def opening_half(
    place,
    base_ref,
    y_ref,
    cur_in,
    raw,
    inner,
    invd_ref,
    planes_ref,
    coef_ref,
    mass_ref,
    res_ref,
    upd_ref,
    cur_ref,
    w_ref,
    a_out_ref,
    b_out_ref,
    next_ref,
    work_ref,
    face_ref,
    side_ref,
):
    residual = coupled(y_ref, raw, raw)
    if base_ref is not None:
        residual = residual + base_ref[...]
    update = residual * invd_ref[...] * STEPS[0][1]
    upd_ref[...] = update
    ghost_side(upd_ref, inner, planes_ref, face_ref, side_ref)
    stiff_apply(upd_ref, coef_ref, mass_ref, w_ref)
    in_plane(w_ref)
    residual = residual - coupled(w_ref, side_ref[...], side_ref[...])
    res_ref[...] = residual
    alpha, beta = STEPS[1]
    second = alpha * update + beta * invd_ref[...] * residual
    upd_ref[...] = second
    done = update + second
    cur_ref[...] = done if cur_in is None else cur_in + done
    stiff_apply(upd_ref, coef_ref, mass_ref, w_ref)
    in_plane(w_ref)
    alpha, beta = STEPS[2]
    zeros = jnp.zeros((64, 128), f32)
    next_ref[...] = alpha * upd_ref[...] + beta * invd_ref[...] * (
        res_ref[...] - coupled(w_ref, zeros, zeros)
    )
    send_planes(w_ref, next_ref, coef_ref, work_ref, a_out_ref, b_out_ref, place[0])


def start_kernel(
    y_ref,
    faces_ref,
    invd_in_ref,
    a_ref,
    b_ref,
    ga_ref,
    gb_ref,
    coef_ref,
    mass_ref,
    res_ref,
    upd_ref,
    cur_ref,
    w_ref,
    a_out_ref,
    b_out_ref,
    invd_ref,
    planes_ref,
    *scratch,
):
    place = where_am_i()
    planes = unpack(ga_ref, gb_ref, 0, SHARE_ROW, place)
    planes_ref[...] = planes[0:320]
    came = unpack(a_ref, b_ref, 0, 64, place)
    bottom, top = through(
        faces_ref[0:64], faces_ref[64:128], planes[192:256], planes[192:256]
    )
    invd_ref[...] = whole(1.0 / bottom, invd_in_ref, 1.0 / top)
    opening_half(
        place,
        None,
        y_ref,
        None,
        came[0:64],
        came[64:128],
        invd_ref,
        planes_ref,
        coef_ref,
        mass_ref,
        res_ref,
        upd_ref,
        cur_ref,
        w_ref,
        a_out_ref,
        b_out_ref,
        *scratch,
    )


def near_kernel(
    basis_ref, ga_ref, gb_ref, inverse_ref, after_ref,
    out_hbm, shares_hbm, out_ref, shares_ref, sems
):
    place = where_am_i()
    blocks = []
    for c in range(NC // 128):
        at = BASIS_ROW + c * 128
        below, above = beside(ga_ref[at : at + 128], gb_ref[at : at + 128], place)
        own = basis_ref[:, c * 128 : c * 128 + 128]
        blocks.append(jnp.concatenate([own, above, below], axis=0))
    rows = jnp.concatenate(blocks, axis=1)
    shares_ref[...] = unpack(ga_ref, gb_ref, SHARE_ROW, 256, place)
    copy = pltpu.make_async_copy(shares_ref, shares_hbm, sems.at[0])
    copy.start()
    out_ref[...] = dot_nn(rows, inverse_ref[...], exact_mode)
    second = pltpu.make_async_copy(out_ref, out_hbm, sems.at[1])
    second.start()
    copy.wait()
    second.wait()


def again_kernel(
    parts_ref,
    near_hbm,
    shares_hbm,
    base_ref,
    a_ref,
    b_ref,
    invd_ref,
    planes_ref,
    coef_ref,
    mass_ref,
    res_ref,
    upd_ref,
    cur_ref,
    w_ref,
    a_out_ref,
    b_out_ref,
    y_ref,
    next_ref,
    work_ref,
    face_ref,
    side_ref,
    shares_ref,
    near_ref,
    sems,
):
    mine, others = pl.ds(0, 128), pl.ds(128, 256)
    copies = [
        pltpu.make_async_copy(near_hbm.at[mine], near_ref.at[mine], sems.at[0]),
        pltpu.make_async_copy(near_hbm.at[others], near_ref.at[others], sems.at[1]),
        pltpu.make_async_copy(shares_hbm, shares_ref, sems.at[2]),
    ]
    for copy in copies:
        copy.start()
    place = where_am_i()
    total = parts_ref[0:8]
    for n in range(1, OWNERS * NC // 1024):
        total = total + parts_ref[n * 8 : n * 8 + 8]
    total = total + pltpu.roll(total, 4, 0)

    def solved(g):
        acc = None
        for c in range(NC // 128):
            cols = slice(c * 128, c * 128 + 128)
            term = near_ref[g * 128 : g * 128 + 128, cols] * total[c : c + 1]
            acc = term if acc is None else acc + term
        return jnp.sum(acc.T, axis=0, keepdims=True)

    copies[0].wait()
    correction = solved(0)
    y_ref[...] = mass_ref[...] * (-correction)
    in_plane(y_ref)
    copies[1].wait()
    above, below = solved(1), solved(2)
    first = first_layer((1, 128))
    near = jnp.where(first, above, below)
    behind = pltpu.roll(jnp.broadcast_to(jnp.where(first, below, above), (8, 128)), LAYER, 1)
    came = unpack(a_ref, b_ref, 0, 64, place)
    side_ref[...] = planes_ref[256:320] * near
    in_plane(side_ref, 1)
    raw = -(came[0:64] + side_ref[...])
    copies[2].wait()
    inner = came[64:128] - correction_inner(shares_ref, near, behind[0:1])
    opening_half(
        place,
        base_ref,
        y_ref,
        correction,
        raw,
        inner,
        invd_ref,
        planes_ref,
        coef_ref,
        mass_ref,
        res_ref,
        upd_ref,
        cur_ref,
        w_ref,
        a_out_ref,
        b_out_ref,
        next_ref,
        work_ref,
        face_ref,
        side_ref,
    )


def closing_half(
    w_ref,
    res_ref,
    upd_ref,
    cur_ref,
    invd_ref,
    a_ref,
    b_ref,
    planes_ref,
    coef_ref,
    mass_ref,
    work_ref,
    vec_ref,
    face_ref,
    side_ref,
):
    came = unpack(a_ref, b_ref, 0, 64, where_am_i())
    residual = res_ref[...] - coupled(w_ref, came[0:64], came[0:64])
    alpha, beta = STEPS[2]
    third = alpha * upd_ref[...] + beta * invd_ref[...] * residual
    vec_ref[...] = third
    ghost_side(vec_ref, came[64:128], planes_ref, face_ref, side_ref)
    stiff_apply(vec_ref, coef_ref, mass_ref, work_ref)
    in_plane(work_ref)
    residual = residual - coupled(work_ref, side_ref[...], side_ref[...])
    alpha, beta = STEPS[3]
    fourth = alpha * third + beta * invd_ref[...] * residual
    vec_ref[...] = fourth
    return residual, cur_ref[...] + (third + fourth)


def middle_kernel(
    w_ref,
    res_in_ref,
    upd_ref,
    cur_in_ref,
    invd_ref,
    a_ref,
    b_ref,
    planes_ref,
    coef_ref,
    mass_ref,
    basis_ref,
    ga_ref,
    gb_ref,
    local_ref,
    cur_hbm,
    part_ref,
    a_out_ref,
    b_out_ref,
    w_out_ref,
    vec_ref,
    cur_ref,
    next_ref,
    work_ref,
    face_ref,
    side_ref,
    sems,
):
    residual, current = closing_half(
        w_ref,
        res_in_ref,
        upd_ref,
        cur_in_ref,
        invd_ref,
        a_ref,
        b_ref,
            planes_ref,
        coef_ref,
        mass_ref,
        w_out_ref,
        vec_ref,
        face_ref,
        side_ref,
    )
    local_ref[...] = residual
    cur_ref[...] = current
    copy = pltpu.make_async_copy(cur_ref, cur_hbm, sems.at[0])
    copy.start()
    stiff_apply(vec_ref, coef_ref, mass_ref, w_out_ref)
    in_plane(w_out_ref)
    zeros = jnp.zeros((64, 128), f32)
    local = local_ref[...] - coupled(w_out_ref, zeros, zeros)
    local_ref[...] = local
    next_ref[...] = local * invd_ref[...] * STEPS[0][1]
    place = where_am_i()
    send_planes(w_out_ref, next_ref, coef_ref, work_ref, a_out_ref, b_out_ref, place[0])
    sums = jnp.sum(local, axis=0, keepdims=True)
    bottom = -jnp.sum(w_out_ref[0:64], axis=0, keepdims=True)
    top = -jnp.sum(w_out_ref[448:512], axis=0, keepdims=True)
    outer = jnp.where(first_layer((1, 128)), bottom, top)
    sums = jnp.broadcast_to(sums, (128, 128)).T
    outer = jnp.broadcast_to(outer, (128, 128)).T
    blocks = []
    for c in range(NC // 128):
        at = BASIS_ROW + c * 128
        below, above = beside(ga_ref[at : at + 128], gb_ref[at : at + 128], place)
        own = basis_ref[:, c * 128 : c * 128 + 128]
        other = jnp.concatenate([below[LAYER:], above[:LAYER]], axis=0)
        part = jnp.sum(own * sums + other * outer, axis=0, keepdims=True)
        blocks.append(part * (1.0 / math.sqrt(NODES)))
    eight = jnp.concatenate(blocks + blocks, axis=0)
    for n in range(OWNERS * NC // 1024):
        part_ref[n * 8 : n * 8 + 8] = eight
    copy.wait()


def last_kernel(*refs):
    inputs, (order_ref, field_hbm, first_hbm, out_ref), rest = (
        refs[:10],
        refs[10:14],
        refs[14:],
    )
    scratch, (field_in, first_in, sems) = rest[:-3], rest[-3:]
    copies = [
        pltpu.make_async_copy(field_hbm, field_in, sems.at[0]),
        pltpu.make_async_copy(first_hbm, first_in, sems.at[1]),
    ]
    for copy in copies:
        copy.start()
    current = closing_half(*inputs, *scratch)[1]
    for copy in copies:
        copy.wait()
    moved = take_lanes(first_in[...] + current, order_ref[...])
    out_ref[...] = field_in[...] + moved


def call(kernel, outs, *args, scratch=(), smem=(), far=(), near=(), copies=0, away=()):
    def stay(x):
        return pltpu.with_memory_space_constraint(x, pltpu.HBM)

    def space(n):
        if n in smem:
            return pltpu.SMEM
        return pltpu.HBM if n in far else pltpu.VMEM

    scratches = [pltpu.VMEM(s, f32) for s in scratch]
    if copies:
        scratches.append(pltpu.SemaphoreType.DMA((copies,)))
    return pl.pallas_call(
        kernel,
        out_shape=[
            pltpu.HBM(s, d) if n in away else jax.ShapeDtypeStruct(s, d)
            for n, (s, d) in enumerate(outs)
        ],
        in_specs=[pl.BlockSpec(memory_space=space(n)) for n in range(len(args))],
        out_specs=[
            pl.BlockSpec(memory_space=pltpu.HBM if n in away else pltpu.VMEM)
            for n in range(len(outs))
        ],
        scratch_shapes=scratches,
        compiler_params=pltpu.CompilerParams(vmem_limit_bytes=20 << 20),
    )(*[stay(x) if n in far + near else x for n, x in enumerate(args)])


FIELD = ((NODES, 128), f32)
SIDE_MSG = ((64, 128), f32)
GHOST_MSG = ((GHOST_ROWS, 128), f32)
SIDE_WORK = [(64, 128), (64, 128)]
SEND_WORK = [(NODES, 128), (128, 128)]


def exchange(a, b):
    count = lax.axis_size("elem")
    pairs_a, pairs_b = [], []
    for d in range(2 * count):
        base, slab = d - d % count, d % count
        pairs_a.append((d, base + (slab ^ 1)))
        other = slab + (1 if slab % 2 else -1)
        inside = 0 <= other < count
        pairs_b.append((d, base + other if inside else (d + count) % (2 * count)))
    axes = ("sess", "elem")
    b = lax.ppermute(b, axes, pairs_b)
    a = lax.ppermute(a, axes, pairs_a)
    return a, b


def one_device(
    pressure,
    load,
    stiffness,
    helm_mass,
    order_slots,
    recv_ids,
    donor_owner,
    donor_slot,
    interp_weights,
    live_count,
    coarse_basis,
    coarse_inverse,
):
    own_field = pressure.reshape(NODES, 128)
    order = order_slots.reshape(1, 128)
    owner = donor_owner.reshape(1, R_DEV)
    other_field = lax.ppermute(own_field, "sess", [(0, 1), (1, 0)])

    send, rank, owner, ids = call(
        request_kernel,
        [
            ((OWNERS * ASK, 128), f32),
            ((1, R_DEV), f32),
            ((1, R_DEV), jnp.int32),
            ((1, R_DEV), jnp.int32),
        ],
        owner,
        donor_slot,
        interp_weights.reshape(3 * NP, R_DEV),
        recv_ids,
        near=(0, 1, 2, 3),
    )
    received = lax.all_to_all(
        send.reshape(OWNERS, 1, ASK * 128), "elem", split_axis=0, concat_axis=0, tiled=True
    )
    coef, mass, static, faces, invd, inv, basis, order, ga, gb = call(
        setup_kernel,
        [
            ((3 * NODES, 128), f32),
            FIELD,
            FIELD,
            ((128, 128), f32),
            FIELD,
            ((1, 128), jnp.int32),
            ((128, NC), f32),
            ((1, 128), jnp.int32),
            GHOST_MSG,
            GHOST_MSG,
        ],
        order,
        stiffness.reshape(3 * NODES, 128),
        helm_mass.reshape(NODES, 128),
        own_field,
        load.reshape(NODES, 128),
        coarse_basis.reshape(128, NC),
        near=(0,),
        far=(1, 2, 3, 4, 5),
        scratch=[
            (3 * NODES, 128),
            (NODES, 128),
            (NODES, 128),
            (NODES, 128),
            (128, NC),
            (NODES, 128),
            (NODES, 128),
            (NODES, 128),
            (NODES, 128),
            (NODES, 128),
            (NODES, 128),
            (64, 128),
            (64, 128),
        ],
        copies=5,
    )
    answer, inv = call(
        owner_kernel,
        [((OWNERS, 128), f32), ((1, 128), jnp.int32)],
        received.reshape(OWNERS * ASK, 128),
        other_field,
        inv,
    )
    answered = lax.all_to_all(answer, "elem", split_axis=0, concat_axis=0, tiled=True)
    ga, gb = exchange(ga, gb)
    y, a, b = call(
        source_kernel,
        [FIELD, SIDE_MSG, SIDE_MSG],
        answered,
        owner,
        rank,
        ids,
        live_count,
        inv,
        static,
        invd,
        coef,
        smem=(4,),
        scratch=SEND_WORK,
    )
    a, b = exchange(a, b)
    half = [FIELD, FIELD, FIELD, FIELD, SIDE_MSG, SIDE_MSG]
    res, upd, cur, w, a, b, invd, planes = call(
        start_kernel,
        half + [FIELD, ((320, 128), f32)],
        y,
        faces,
        invd,
        a,
        b,
        ga,
        gb,
        coef,
        mass,
        scratch=SEND_WORK + SIDE_WORK,
    )
    near, shares = call(
        near_kernel,
        [((384, NC), f32), FIELD],
        basis,
        ga,
        gb,
        coarse_inverse.reshape(NC, NC),
        a,
        near=(3,),
        scratch=[(384, NC), (NODES, 128)],
        copies=2,
        away=(0, 1),
    )
    a, b = exchange(a, b)
    res, total, part, a, b = call(
        middle_kernel,
        [FIELD, FIELD, ((OWNERS * NC // 128, 128), f32), SIDE_MSG, SIDE_MSG],
        w,
        res,
        upd,
        cur,
        invd,
        a,
        b,
        planes,
        coef,
        mass,
        basis,
        ga,
        gb,
        scratch=[(NODES, 128)] * 3 + SEND_WORK + SIDE_WORK,
        copies=1,
        away=(1,),
    )
    parts = lax.all_to_all(
        part.reshape(OWNERS, NC // 128, 128),
        "elem",
        split_axis=0,
        concat_axis=0,
        tiled=True,
    )
    a, b = exchange(a, b)
    res, upd, cur, w, a, b = call(
        again_kernel,
        half,
        parts.reshape(OWNERS * NC // 128, 128),
        near,
        shares,
        res,
        a,
        b,
        invd,
        planes,
        coef,
        mass,
        far=(1, 2),
        scratch=[(NODES, 128)] + SEND_WORK + SIDE_WORK + [(NODES, 128), (384, NC)],
        copies=3,
    )
    a, b = exchange(a, b)
    (out,) = call(
        last_kernel,
        [FIELD],
        w,
        res,
        upd,
        cur,
        invd,
        a,
        b,
        planes,
        coef,
        mass,
        order,
        own_field,
        total,
        far=(11, 12),
        scratch=[(NODES, 128)] * 2 + SIDE_WORK + [(NODES, 128)] * 2,
        copies=2,
    )
    return out.reshape(1, NP, NP, NP, 128)


def solution(mesh):
    return jax.shard_map(
        one_device,
        mesh=mesh,
        in_specs=(
            P("sess", None, None, None, "elem"),
            P("sess", None, None, None, "elem"),
            P("sess", None, None, None, None, "elem"),
            P("sess", None, None, None, "elem"),
            P("sess", "elem", None),
            P("sess", "elem"),
            P("sess", "elem", None),
            P("sess", "elem"),
            P("sess", None, "elem"),
            P("sess", "elem"),
            P("sess", "elem", None),
            P("sess", None, None),
        ),
        out_specs=P("sess", None, None, None, "elem"),
        check_vma=False,
    )
```

```python
import math

import jax
import jax.numpy as jnp
import numpy as np
from jax import lax
from jax.experimental import pallas as pl
from jax.experimental.pallas import tpu as pltpu
from jax.sharding import PartitionSpec as P


NP = 8
EX = 8
EY = 8
LAYER = EX * EY
NODES = NP**3
R_DEV = 1024
NC = 512
CHEB = 4
OWNERS = 64
COMPS = 32
HALF = 12
ASK = 6

exact_mode = lax.Precision.HIGHEST
spectrum_high = 8.0
spectrum_low = 0.8
f32 = jnp.float32
bf16 = jnp.bfloat16


def gll_derivative():
    x = np.array(
        [
            -1.0,
            -0.8717401485096066,
            -0.5917001814331423,
            -0.2092992179024789,
            0.2092992179024789,
            0.5917001814331423,
            0.8717401485096066,
            1.0,
        ]
    )
    legendre = (429.0 * x**7 - 693.0 * x**5 + 315.0 * x**3 - 35.0 * x) / 16.0
    distance = x[:, None] - x[None, :]
    same = np.eye(8, dtype=bool)
    table = legendre[:, None] / (legendre[None, :] * np.where(same, 1.0, distance))
    corner = np.zeros((8, 8))
    corner[0, 0] = -14.0
    corner[7, 7] = 14.0
    return np.where(same, corner, table).astype(np.float32).astype(np.float64)


DERIV = gll_derivative()


def chebyshev():
    center = 0.5 * (spectrum_high + spectrum_low)
    half_width = 0.5 * (spectrum_high - spectrum_low)
    sigma_ratio = center / half_width
    rho = 1.0 / sigma_ratio
    steps = [(0.0, 1.0 / center)]
    for _ in range(CHEB - 1):
        rho_next = 1.0 / (2.0 * sigma_ratio - rho)
        steps.append((rho_next * rho, 2.0 * rho_next / half_width))
        rho = rho_next
    return steps


STEPS = chebyshev()


def split3(x):
    hi = x.astype(bf16)
    rest = x - hi.astype(f32)
    mid = rest.astype(bf16)
    low = (rest - mid.astype(f32)).astype(bf16)
    return hi, mid, low


def dot_nn(a, b, precision=None):
    return lax.dot_general(
        a, b, (((1,), (0,)), ((), ())), precision=precision, preferred_element_type=f32
    )


def dot_nt(a, b, precision=None):
    return lax.dot_general(
        a, b, (((1,), (1,)), ((), ())), precision=precision, preferred_element_type=f32
    )


def iota(shape, axis):
    return lax.broadcasted_iota(jnp.int32, shape, axis)


def request_kernel(
    owner_ref, slot_ref, weight_ref, ids_ref, send_ref, rank_ref, owner_out_ref, ids_out_ref
):
    owner = owner_ref[...]
    hits = iota((OWNERS, R_DEV), 0) == owner
    hits_f = hits.astype(f32)
    hits_b = hits_f.astype(bf16)
    upper = (iota((128, 128), 0) < iota((128, 128), 1)).astype(f32).astype(bf16)
    carry = jnp.zeros((OWNERS, 1), f32)
    ranks = []
    for b in range(R_DEV // 128):
        cols = slice(b * 128, b * 128 + 128)
        block = hits_f[:, cols]
        count = dot_nn(hits_b[:, cols], upper) + carry
        ranks.append(jnp.sum(block * count, axis=0, keepdims=True))
        carry = carry + jnp.sum(block, axis=1, keepdims=True)
    rank = jnp.concatenate(ranks, axis=1)
    rank_ref[...] = rank
    owner_out_ref[...] = owner
    ids_out_ref[...] = ids_ref[...]
    payload = jnp.concatenate(
        [
            weight_ref[...],
            jnp.broadcast_to(slot_ref[...].astype(f32), (COMPS - 3 * NP, R_DEV)),
        ],
        axis=0,
    )
    pieces = split3(payload)
    total = None
    for piece in pieces:
        rows = [
            piece * (rank == float(m)).astype(f32).astype(bf16) for m in range(2 * HALF)
        ]
        part = dot_nt(hits_b, jnp.concatenate(rows, axis=0))
        total = part if total is None else total + part
    for c in range(ASK):
        if c < 2 * HALF * COMPS // 128:
            block = total[:, c * 128 : c * 128 + 128]
        else:
            block = jnp.zeros((OWNERS, 128), f32)
        send_ref[pl.ds(c, OWNERS, stride=ASK), :] = block


def owner_kernel(recv_ref, field_ref, before_ref, ret_ref, after_ref):
    cols = [recv_ref[pl.ds(c, OWNERS, stride=ASK), :] for c in range(6)]
    packed = jnp.concatenate(
        [jnp.concatenate(cols[:3], axis=1), jnp.concatenate(cols[3:], axis=1)], axis=0
    )
    comps = packed.T
    pieces = jnp.concatenate(split3(field_ref[...]), axis=1)
    rows = []
    for pair in range(HALF // 2):
        a = comps[(2 * pair) * COMPS : (2 * pair + 1) * COMPS]
        b = comps[(2 * pair + 1) * COMPS : (2 * pair + 2) * COMPS]
        both = jnp.concatenate([a, b], axis=1)
        slot = both[3 * NP : 3 * NP + 1].astype(jnp.int32)
        pick = (iota((128, 256), 0) == slot).astype(f32).astype(bf16)
        gathered = dot_nn(pieces, jnp.concatenate([pick, pick, pick], axis=0))
        wx = both[0:NP]
        wy = both[NP : 2 * NP]
        wz = both[2 * NP : 3 * NP]
        acc = None
        for k in range(NP):
            line = None
            for j in range(NP):
                row = (k * NP + j) * NP
                term = gathered[row : row + NP] * wy[j : j + 1]
                line = term if line is None else line + term
            line = line * wz[k : k + 1]
            acc = line if acc is None else acc + line
        value = jnp.sum(acc * wx, axis=0, keepdims=True)
        rows.append(value[:, :128])
        rows.append(value[:, 128:])
    rows.append(jnp.zeros((128 - HALF, 128), f32))
    turned = jnp.concatenate(rows, axis=0).T
    ret_ref[...] = turned[:OWNERS] + pltpu.roll(turned[OWNERS:], 16, 1)
    after_ref[...] = before_ref[...]


def deriv8(table, v):
    plus = [v[m] + v[7 - m] for m in range(4)]
    minus = [v[m] - v[7 - m] for m in range(4)]
    out = [None] * 8
    for a in range(4):
        even = odd = None
        for m in range(4):
            ce = 0.5 * (table[a, m] + table[a, 7 - m])
            co = 0.5 * (table[a, m] - table[a, 7 - m])
            te = plus[m] * float(ce)
            to = minus[m] * float(co)
            even = te if even is None else even + te
            odd = to if odd is None else odd + to
        out[a] = odd + even
        out[7 - a] = odd - even
    return out


def apply_line(v, coef):
    grad = deriv8(DERIV, v)
    return deriv8(DERIV.T, [grad[a] * coef(a) for a in range(8)])


def stiff_apply(v_ref, coef_ref, mass_ref, out_ref):
    def per_k(k, carry):
        base = pl.multiple_of(k * 64, 64)
        lines = [v_ref[pl.ds(base + i, 8, stride=8), :] for i in range(8)]
        res = apply_line(lines, lambda a: coef_ref[pl.ds(base + a * 8, 8), :])
        for i in range(8):
            out_ref[pl.ds(base + i, 8, stride=8), :] = res[i]
        rows = [v_ref[pl.ds(base + j * 8, 8), :] for j in range(8)]
        res = apply_line(rows, lambda b: coef_ref[pl.ds(512 + base + b * 8, 8), :])
        for j in range(8):
            at = pl.ds(base + j * 8, 8)
            out_ref[at, :] = out_ref[at, :] + res[j] + mass_ref[at, :] * rows[j]
        return carry

    lax.fori_loop(0, 8, per_k, 0, unroll=2)

    def per_j(j, carry):
        base = pl.multiple_of(j * 8, 8)
        cols = [v_ref[pl.ds(base + k * 64, 8), :] for k in range(8)]
        res = apply_line(cols, lambda c: coef_ref[pl.ds(1024 + base + c * 64, 8), :])
        for k in range(8):
            at = pl.ds(base + k * 64, 8)
            out_ref[at, :] = out_ref[at, :] + res[k]
        return carry

    lax.fori_loop(0, 8, per_j, 0, unroll=2)


def couple(high, low, shift, pos, count):
    lanes = high.shape[-1]
    next_low = pltpu.roll(low, lanes - shift, high.ndim - 1)
    prev_high = pltpu.roll(high, shift, high.ndim - 1)
    new_high = high + jnp.where(pos < count - 1, next_low, 0.0)
    new_low = low + jnp.where(pos > 0, prev_high, 0.0)
    return new_high, new_low


def in_plane(ref, count=NP):
    rows = count * NP
    col = iota((rows, 128), 1) % EX
    high, low = couple(
        ref[pl.ds(7, rows, stride=8), :], ref[pl.ds(0, rows, stride=8), :], 1, col, EX
    )
    ref[pl.ds(7, rows, stride=8), :] = high
    ref[pl.ds(0, rows, stride=8), :] = low
    line = (iota((8, 128), 1) // EX) % EY
    for k in range(count):
        high, low = couple(
            ref[k * 64 + 56 : k * 64 + 64], ref[k * 64 : k * 64 + 8], EX, line, EY
        )
        ref[k * 64 + 56 : k * 64 + 64] = high
        ref[k * 64 : k * 64 + 8] = low


def through(bottom, top, below, above):
    first = iota(bottom.shape, 1) < LAYER
    new_bottom = bottom + pltpu.roll(jnp.where(first, top, below), LAYER, 1)
    new_top = top + pltpu.roll(jnp.where(first, above, bottom), LAYER, 1)
    return new_bottom, new_top


def whole(bottom, ref, top):
    return jnp.concatenate([bottom, ref[64:448], top], axis=0)


def coupled(w_ref, below, above):
    bottom, top = through(w_ref[0:64], w_ref[448:512], below, above)
    return whole(bottom, w_ref, top)


def where_am_i():
    me = lax.axis_index("elem")
    last = lax.axis_size("elem") - 1
    return jnp.bitwise_and(me, 1) == 0, me > 0, me < last


def first_layer(shape):
    return iota(shape, 1) < LAYER


def pack(up, down, a_ref, b_ref, row, even):
    half = up.shape[0] // 2
    first = first_layer((half, 128))
    up = jnp.where(first, pltpu.roll(up[:half], LAYER, 1), up[half:])
    down = jnp.where(first, down[:half], pltpu.roll(down[half:], LAYER, 1))
    a_ref[row : row + half] = jnp.where(even, up, down)
    b_ref[row : row + half] = jnp.where(even, down, up)


def beside(a, b, place):
    even, has_below, has_above = place
    below = jnp.where(has_below, jnp.where(even, b, a), 0.0)
    above = jnp.where(has_above, jnp.where(even, a, b), 0.0)
    return below, above


def unpack(a_ref, b_ref, row, half, place):
    below, above = beside(a_ref[row : row + half], b_ref[row : row + half], place)
    first = first_layer(below.shape)
    low = jnp.where(first, above, pltpu.roll(below, LAYER, 1))
    high = jnp.where(first, pltpu.roll(above, LAYER, 1), below)
    return jnp.concatenate([low, high], axis=0)


def blend(bottom, top):
    return jnp.where(first_layer(bottom.shape), bottom, top)


def end_rows():
    first = first_layer((8, 128))
    return [
        jnp.where(first, float(DERIV[c, 0]), float(DERIV[c, 7])).astype(f32)
        for c in range(8)
    ]


def inner_planes(next_ref, coef_ref, out_ref, row):
    first = first_layer((8, 128))
    ends = end_rows()
    for j in range(8):
        cols = [next_ref[k * 64 + j * 8 : k * 64 + j * 8 + 8] for k in range(8)]
        cols[0] = jnp.where(first, 0.0, cols[0])
        cols[7] = jnp.where(first, cols[7], 0.0)
        grad = deriv8(DERIV, cols)
        total = None
        for c in range(8):
            at = 1024 + c * 64 + j * 8
            term = grad[c] * coef_ref[at : at + 8] * ends[c]
            total = term if total is None else total + term
        out_ref[row + j * 8 : row + j * 8 + 8] = total


def send_planes(w_ref, next_ref, coef_ref, work_ref, a_ref, b_ref, even):
    work_ref[0:64] = blend(w_ref[0:64], w_ref[448:512])
    inner_planes(next_ref, coef_ref, work_ref, 64)
    both = work_ref[...]
    pack(both, both, a_ref, b_ref, 0, even)


def shift_x(src_ref, dst_ref, count):
    rows = count * NP
    col = iota((rows, 128), 1) % EX
    dst_ref[...] = jnp.zeros(dst_ref.shape, f32)
    low = pltpu.roll(src_ref[pl.ds(7, rows, stride=8), :], 1, 1)
    high = pltpu.roll(src_ref[pl.ds(0, rows, stride=8), :], 127, 1)
    dst_ref[pl.ds(0, rows, stride=8), :] = jnp.where(col > 0, low, 0.0)
    dst_ref[pl.ds(7, rows, stride=8), :] = jnp.where(col < EX - 1, high, 0.0)


def shift_y(src_ref, dst_ref, count):
    line = (iota((8, 128), 1) // EX) % EY
    dst_ref[...] = jnp.zeros(dst_ref.shape, f32)
    for k in range(count):
        low = pltpu.roll(src_ref[k * 64 + 56 : k * 64 + 64], EX, 1)
        high = pltpu.roll(src_ref[k * 64 : k * 64 + 8], 128 - EX, 1)
        dst_ref[k * 64 : k * 64 + 8] = jnp.where(line > 0, low, 0.0)
        dst_ref[k * 64 + 56 : k * 64 + 64] = jnp.where(line < EY - 1, high, 0.0)


def correction_shares(coef_ref, mass_ref, invd_ref, out_ref, next_ref, x_ref, y_ref, face_ref, side_ref):
    scaled = STEPS[0][1]
    next_ref[...] = mass_ref[...] * invd_ref[...] * scaled
    inner_planes(next_ref, coef_ref, out_ref, 0)
    shift_x(mass_ref, x_ref, NP)
    next_ref[...] = x_ref[...] * invd_ref[...] * scaled
    inner_planes(next_ref, coef_ref, out_ref, 64)
    shift_y(mass_ref, y_ref, NP)
    next_ref[...] = y_ref[...] * invd_ref[...] * scaled
    inner_planes(next_ref, coef_ref, out_ref, 128)
    shift_y(x_ref, y_ref, NP)
    next_ref[...] = y_ref[...] * invd_ref[...] * scaled
    inner_planes(next_ref, coef_ref, out_ref, 192)
    first = first_layer((8, 128))
    ends = end_rows()
    weights = [
        ends[c] * jnp.where(first, float(DERIV[c, 7]), float(DERIV[c, 0]))
        for c in range(8)
    ]
    for j in range(8):
        total = None
        for c in range(8):
            at = 1024 + c * 64 + j * 8
            term = coef_ref[at : at + 8] * weights[c]
            total = term if total is None else total + term
        at = slice(j * 8, j * 8 + 8)
        inv = blend(invd_ref[448 + j * 8 : 456 + j * 8], invd_ref[at])
        next_ref[at] = total * inv * scaled
    share = next_ref[0:64]
    face_ref[...] = pltpu.roll(blend(mass_ref[448:512], mass_ref[0:64]), LAYER, 1)
    out_ref[256:320] = share * face_ref[...]
    shift_x(face_ref, side_ref, 1)
    out_ref[320:384] = share * side_ref[...]
    shift_y(face_ref, next_ref.at[64:128], 1)
    out_ref[384:448] = share * next_ref[64:128]
    shift_y(side_ref, next_ref.at[64:128], 1)
    out_ref[448:512] = share * next_ref[64:128]


def correction_inner(shares, near, behind):
    node = iota((64, 128), 0)
    left, front = node % 8 == 0, node < 8
    total = None
    for base, row in ((0, near), (256, behind)):
        row = jnp.broadcast_to(row, (64, 128))

        def turn(count):
            return pltpu.roll(row, count % 128, 1)

        values = [
            row,
            jnp.where(left, turn(1), turn(-1)),
            jnp.where(front, turn(8), turn(-8)),
            jnp.where(
                front,
                jnp.where(left, turn(9), turn(7)),
                jnp.where(left, turn(-7), turn(-9)),
            ),
        ]
        for n, value in enumerate(values):
            at = base + n * 64
            term = shares[at : at + 64] * value
            total = term if total is None else total + term
    return total


def ghost_side(update_ref, inner, planes_ref, face_ref, side_ref):
    face_ref[...] = pltpu.roll(blend(update_ref[0:64], update_ref[448:512]), LAYER, 1)
    lines = [face_ref[pl.ds(i, 8, stride=8), :] for i in range(8)]
    res = apply_line(lines, lambda a: planes_ref[a * 8 : a * 8 + 8])
    for i in range(8):
        side_ref[pl.ds(i, 8, stride=8), :] = res[i]
    rows = [face_ref[j * 8 : j * 8 + 8] for j in range(8)]
    res = apply_line(rows, lambda b: planes_ref[64 + b * 8 : 72 + b * 8])
    for j in range(8):
        at = slice(j * 8, j * 8 + 8)
        side_ref[at] = (
            side_ref[at]
            + res[j]
            + planes_ref[128 + j * 8 : 136 + j * 8] * rows[j]
            + inner[at]
        )
    in_plane(side_ref, 1)


def plain8(table, v):
    out = []
    for i in range(8):
        total = None
        for a in range(8):
            if table[a, i] == 0.0:
                continue
            term = v[a] * float(table[a, i])
            total = term if total is None else total + term
        out.append(total)
    return out


def take_lanes(x, index):
    return jnp.take_along_axis(
        x, jnp.broadcast_to(index, x.shape), axis=1, mode="promise_in_bounds"
    )


def local_diagonal(coef_ref, mass_ref, diag_ref):
    squared = DERIV * DERIV

    def per_k(k, carry):
        base = pl.multiple_of(k * 64, 64)
        res = plain8(squared, [coef_ref[pl.ds(base + a * 8, 8), :] for a in range(8)])
        for i in range(8):
            diag_ref[pl.ds(base + i, 8, stride=8), :] = res[i]
        res = plain8(squared, [coef_ref[pl.ds(512 + base + b * 8, 8), :] for b in range(8)])
        for j in range(8):
            at = pl.ds(base + j * 8, 8)
            diag_ref[at, :] = diag_ref[at, :] + res[j] + mass_ref[at, :]
        return carry

    lax.fori_loop(0, 8, per_k, 0, unroll=2)

    def per_j(j, carry):
        base = pl.multiple_of(j * 8, 8)
        res = plain8(squared, [coef_ref[pl.ds(1024 + base + c * 64, 8), :] for c in range(8)])
        for k in range(8):
            at = pl.ds(base + k * 64, 8)
            diag_ref[at, :] = diag_ref[at, :] + res[k]
        return carry

    lax.fori_loop(0, 8, per_j, 0, unroll=2)


SHARE_ROW = 192
BASIS_ROW = SHARE_ROW + 256
GHOST_ROWS = BASIS_ROW + 512


def setup_kernel(
    order_ref,
    stiff_hbm,
    mass_hbm,
    field_hbm,
    load_hbm,
    basis_hbm,
    coef_ref,
    mass_ref,
    static_ref,
    faces_ref,
    invd_ref,
    inv_ref,
    basis_ref,
    order_out_ref,
    a_ref,
    b_ref,
    stiff_in,
    mass_in,
    field_in,
    load_in,
    basis_in,
    tmp_ref,
    start_ref,
    diag_ref,
    share_ref,
    x_ref,
    y_ref,
    face_ref,
    side_ref,
    sems,
):
    copies = [
        pltpu.make_async_copy(src, dst, sems.at[n])
        for n, (src, dst) in enumerate(
            [
                (stiff_hbm, stiff_in),
                (mass_hbm, mass_in),
                (field_hbm, field_in),
                (load_hbm, load_in),
                (basis_hbm, basis_in),
            ]
        )
    ]
    for copy in copies:
        copy.start()
    order = order_ref[...]
    match = (iota((128, 128), 0) == order).astype(f32)
    inv = jnp.sum(match.T * iota((128, 128), 0).astype(f32), axis=0, keepdims=True)
    inv = inv.astype(jnp.int32)
    inv_ref[...] = inv
    order_out_ref[...] = order
    copies[0].wait()
    tmp_ref[...] = take_lanes(stiff_in[0:512, :], inv)
    for k in range(8):
        for i in range(8):
            coef_ref[k * 64 + i * 8 : k * 64 + i * 8 + 8, :] = tmp_ref[
                pl.ds(k * 64 + i, 8, stride=8), :
            ]
    coef_ref[512:1536, :] = take_lanes(stiff_in[512:1536, :], inv)
    for copy in copies[1:]:
        copy.wait()
    mass_ref[...] = take_lanes(mass_in[...], inv)
    start_ref[...] = take_lanes(field_in[...], inv)
    stiff_apply(start_ref, coef_ref, mass_ref, static_ref)
    static_ref[...] = take_lanes(load_in[...], inv) - static_ref[...]
    in_plane(static_ref)
    basis = dot_nn(match, basis_in[...], exact_mode)
    basis_ref[...] = basis
    local_diagonal(coef_ref, mass_ref, diag_ref)
    in_plane(diag_ref)
    zeros = jnp.zeros((64, 128), f32)
    invd_ref[...] = 1.0 / coupled(diag_ref, zeros, zeros)
    ends = end_rows()
    for j in range(8):
        total = None
        for c in range(8):
            at = 1024 + c * 64 + j * 8
            term = coef_ref[at : at + 8] * (ends[c] * ends[c])
            total = term if total is None else total + term
        tmp_ref[j * 8 : j * 8 + 8] = total
    planes = jnp.concatenate(
        [
            blend(coef_ref[0:64], coef_ref[448:512]),
            blend(coef_ref[512:576], coef_ref[960:1024]),
            blend(mass_ref[0:64], mass_ref[448:512]) + tmp_ref[0:64],
            blend(diag_ref[0:64], diag_ref[448:512]),
            blend(mass_ref[0:64], mass_ref[448:512]),
            zeros,
        ],
        axis=0,
    )
    faces_ref[0:64] = diag_ref[0:64]
    faces_ref[64:128] = diag_ref[448:512]
    even = where_am_i()[0]
    pack(planes, planes, a_ref, b_ref, 0, even)
    correction_shares(
        coef_ref, mass_ref, invd_ref, share_ref, tmp_ref, x_ref, y_ref, face_ref, side_ref
    )
    shares = share_ref[...]
    pack(shares, shares, a_ref, b_ref, SHARE_ROW, even)
    for c in range(NC // 128):
        at = BASIS_ROW + c * 128
        cols = basis[:, c * 128 : c * 128 + 128]
        a_ref[at : at + 128] = cols
        b_ref[at : at + 128] = cols


def send_first(y_ref, base, invd, coef_ref, next_ref, work_ref, a_ref, b_ref):
    zeros = jnp.zeros((64, 128), f32)
    inner = coupled(y_ref, zeros, zeros)
    if base is not None:
        inner = inner + base
    next_ref[...] = inner * invd * STEPS[0][1]
    send_planes(y_ref, next_ref, coef_ref, work_ref, a_ref, b_ref, where_am_i()[0])


def source_kernel(
    ret_ref,
    owner_ref,
    rank_ref,
    ids_ref,
    live_ref,
    inv_ref,
    static_ref,
    invd_ref,
    coef_ref,
    y_ref,
    a_ref,
    b_ref,
    next_ref,
    work_ref,
):
    rank = rank_ref[...].astype(jnp.int32)
    place = rank + jnp.where(rank >= HALF, 16 - HALF, 0)
    ids = ids_ref[...]
    live = iota((1, R_DEV), 1) < live_ref[0, 0]
    node = jnp.where(live, lax.shift_right_logical(ids, 7), -1)
    elem = jnp.bitwise_and(ids, 127)
    hits = (iota((OWNERS, R_DEV), 0) == owner_ref[...]).astype(f32).astype(bf16)
    answers = jnp.concatenate(split3(ret_ref[...].T[0:32]), axis=0)
    picked = dot_nn(answers, hits)
    picked = picked[0:32] + picked[32:64] + picked[64:96]
    value = jnp.sum(
        jnp.where(iota((32, R_DEV), 0) == place, picked, 0.0), axis=0, keepdims=True
    )
    at_node = (iota((NODES, R_DEV), 0) == node).astype(f32).astype(bf16)
    at_elem = (iota((128, R_DEV), 0) == elem).astype(f32).astype(bf16)
    spread = jnp.concatenate([at_elem * piece for piece in split3(value)], axis=0)
    landed = dot_nt(at_node, spread)
    landed = landed[:, 0:128] + landed[:, 128:256] + landed[:, 256:384]
    y_ref[...] = take_lanes(landed, inv_ref[...])
    in_plane(y_ref)
    y_ref[...] = y_ref[...] + static_ref[...]
    send_first(y_ref, None, invd_ref[...], coef_ref, next_ref, work_ref, a_ref, b_ref)


def opening_half(
    place,
    base_ref,
    y_ref,
    cur_in,
    raw,
    inner,
    invd_ref,
    planes_ref,
    coef_ref,
    mass_ref,
    res_ref,
    upd_ref,
    cur_ref,
    w_ref,
    a_out_ref,
    b_out_ref,
    next_ref,
    work_ref,
    face_ref,
    side_ref,
):
    residual = coupled(y_ref, raw, raw)
    if base_ref is not None:
        residual = residual + base_ref[...]
    update = residual * invd_ref[...] * STEPS[0][1]
    upd_ref[...] = update
    ghost_side(upd_ref, inner, planes_ref, face_ref, side_ref)
    stiff_apply(upd_ref, coef_ref, mass_ref, w_ref)
    in_plane(w_ref)
    residual = residual - coupled(w_ref, side_ref[...], side_ref[...])
    res_ref[...] = residual
    alpha, beta = STEPS[1]
    second = alpha * update + beta * invd_ref[...] * residual
    upd_ref[...] = second
    done = update + second
    cur_ref[...] = done if cur_in is None else cur_in + done
    stiff_apply(upd_ref, coef_ref, mass_ref, w_ref)
    in_plane(w_ref)
    alpha, beta = STEPS[2]
    zeros = jnp.zeros((64, 128), f32)
    next_ref[...] = alpha * upd_ref[...] + beta * invd_ref[...] * (
        res_ref[...] - coupled(w_ref, zeros, zeros)
    )
    send_planes(w_ref, next_ref, coef_ref, work_ref, a_out_ref, b_out_ref, place[0])


def start_kernel(
    y_ref,
    faces_ref,
    invd_in_ref,
    a_ref,
    b_ref,
    ga_ref,
    gb_ref,
    coef_ref,
    mass_ref,
    res_ref,
    upd_ref,
    cur_ref,
    w_ref,
    a_out_ref,
    b_out_ref,
    invd_ref,
    planes_ref,
    *scratch,
):
    place = where_am_i()
    planes = unpack(ga_ref, gb_ref, 0, SHARE_ROW, place)
    planes_ref[...] = planes[0:320]
    came = unpack(a_ref, b_ref, 0, 64, place)
    bottom, top = through(
        faces_ref[0:64], faces_ref[64:128], planes[192:256], planes[192:256]
    )
    invd_ref[...] = whole(1.0 / bottom, invd_in_ref, 1.0 / top)
    opening_half(
        place,
        None,
        y_ref,
        None,
        came[0:64],
        came[64:128],
        invd_ref,
        planes_ref,
        coef_ref,
        mass_ref,
        res_ref,
        upd_ref,
        cur_ref,
        w_ref,
        a_out_ref,
        b_out_ref,
        *scratch,
    )


def near_kernel(
    basis_ref, ga_ref, gb_ref, inverse_ref, after_ref,
    out_hbm, shares_hbm, out_ref, shares_ref, sems
):
    place = where_am_i()
    blocks = []
    for c in range(NC // 128):
        at = BASIS_ROW + c * 128
        below, above = beside(ga_ref[at : at + 128], gb_ref[at : at + 128], place)
        own = basis_ref[:, c * 128 : c * 128 + 128]
        blocks.append(jnp.concatenate([own, above, below], axis=0))
    rows = jnp.concatenate(blocks, axis=1)
    shares_ref[...] = unpack(ga_ref, gb_ref, SHARE_ROW, 256, place)
    copy = pltpu.make_async_copy(shares_ref, shares_hbm, sems.at[0])
    copy.start()
    out_ref[...] = dot_nn(rows, inverse_ref[...], exact_mode)
    second = pltpu.make_async_copy(out_ref, out_hbm, sems.at[1])
    second.start()
    copy.wait()
    second.wait()


def again_kernel(
    parts_ref,
    near_hbm,
    shares_hbm,
    base_ref,
    a_ref,
    b_ref,
    invd_ref,
    planes_ref,
    coef_ref,
    mass_ref,
    res_ref,
    upd_ref,
    cur_ref,
    w_ref,
    a_out_ref,
    b_out_ref,
    y_ref,
    next_ref,
    work_ref,
    face_ref,
    side_ref,
    shares_ref,
    near_ref,
    sems,
):
    mine, others = pl.ds(0, 128), pl.ds(128, 256)
    copies = [
        pltpu.make_async_copy(near_hbm.at[mine], near_ref.at[mine], sems.at[0]),
        pltpu.make_async_copy(near_hbm.at[others], near_ref.at[others], sems.at[1]),
        pltpu.make_async_copy(shares_hbm, shares_ref, sems.at[2]),
    ]
    for copy in copies:
        copy.start()
    place = where_am_i()
    total = parts_ref[0:8]
    for n in range(1, OWNERS * NC // 1024):
        total = total + parts_ref[n * 8 : n * 8 + 8]
    total = total + pltpu.roll(total, 4, 0)

    def solved(g):
        acc = None
        for c in range(NC // 128):
            cols = slice(c * 128, c * 128 + 128)
            term = near_ref[g * 128 : g * 128 + 128, cols] * total[c : c + 1]
            acc = term if acc is None else acc + term
        return jnp.sum(acc.T, axis=0, keepdims=True)

    copies[0].wait()
    correction = solved(0)
    y_ref[...] = mass_ref[...] * (-correction)
    in_plane(y_ref)
    copies[1].wait()
    above, below = solved(1), solved(2)
    first = first_layer((1, 128))
    near = jnp.where(first, above, below)
    behind = pltpu.roll(jnp.broadcast_to(jnp.where(first, below, above), (8, 128)), LAYER, 1)
    came = unpack(a_ref, b_ref, 0, 64, place)
    side_ref[...] = planes_ref[256:320] * near
    in_plane(side_ref, 1)
    raw = -(came[0:64] + side_ref[...])
    copies[2].wait()
    inner = came[64:128] - correction_inner(shares_ref, near, behind[0:1])
    opening_half(
        place,
        base_ref,
        y_ref,
        correction,
        raw,
        inner,
        invd_ref,
        planes_ref,
        coef_ref,
        mass_ref,
        res_ref,
        upd_ref,
        cur_ref,
        w_ref,
        a_out_ref,
        b_out_ref,
        next_ref,
        work_ref,
        face_ref,
        side_ref,
    )


def closing_half(
    w_ref,
    res_ref,
    upd_ref,
    cur_ref,
    invd_ref,
    a_ref,
    b_ref,
    planes_ref,
    coef_ref,
    mass_ref,
    work_ref,
    vec_ref,
    face_ref,
    side_ref,
):
    came = unpack(a_ref, b_ref, 0, 64, where_am_i())
    residual = res_ref[...] - coupled(w_ref, came[0:64], came[0:64])
    alpha, beta = STEPS[2]
    third = alpha * upd_ref[...] + beta * invd_ref[...] * residual
    vec_ref[...] = third
    ghost_side(vec_ref, came[64:128], planes_ref, face_ref, side_ref)
    stiff_apply(vec_ref, coef_ref, mass_ref, work_ref)
    in_plane(work_ref)
    residual = residual - coupled(work_ref, side_ref[...], side_ref[...])
    alpha, beta = STEPS[3]
    fourth = alpha * third + beta * invd_ref[...] * residual
    vec_ref[...] = fourth
    return residual, cur_ref[...] + (third + fourth)


def middle_kernel(
    w_ref,
    res_in_ref,
    upd_ref,
    cur_in_ref,
    invd_ref,
    a_ref,
    b_ref,
    planes_ref,
    coef_ref,
    mass_ref,
    basis_ref,
    ga_ref,
    gb_ref,
    local_ref,
    cur_hbm,
    part_ref,
    a_out_ref,
    b_out_ref,
    w_out_ref,
    vec_ref,
    cur_ref,
    next_ref,
    work_ref,
    face_ref,
    side_ref,
    sems,
):
    residual, current = closing_half(
        w_ref,
        res_in_ref,
        upd_ref,
        cur_in_ref,
        invd_ref,
        a_ref,
        b_ref,
            planes_ref,
        coef_ref,
        mass_ref,
        w_out_ref,
        vec_ref,
        face_ref,
        side_ref,
    )
    local_ref[...] = residual
    cur_ref[...] = current
    copy = pltpu.make_async_copy(cur_ref, cur_hbm, sems.at[0])
    copy.start()
    stiff_apply(vec_ref, coef_ref, mass_ref, w_out_ref)
    in_plane(w_out_ref)
    zeros = jnp.zeros((64, 128), f32)
    local = local_ref[...] - coupled(w_out_ref, zeros, zeros)
    local_ref[...] = local
    next_ref[...] = local * invd_ref[...] * STEPS[0][1]
    place = where_am_i()
    send_planes(w_out_ref, next_ref, coef_ref, work_ref, a_out_ref, b_out_ref, place[0])
    sums = jnp.sum(local, axis=0, keepdims=True)
    bottom = -jnp.sum(w_out_ref[0:64], axis=0, keepdims=True)
    top = -jnp.sum(w_out_ref[448:512], axis=0, keepdims=True)
    outer = jnp.where(first_layer((1, 128)), bottom, top)
    sums = jnp.broadcast_to(sums, (128, 128)).T
    outer = jnp.broadcast_to(outer, (128, 128)).T
    blocks = []
    for c in range(NC // 128):
        at = BASIS_ROW + c * 128
        below, above = beside(ga_ref[at : at + 128], gb_ref[at : at + 128], place)
        own = basis_ref[:, c * 128 : c * 128 + 128]
        other = jnp.concatenate([below[LAYER:], above[:LAYER]], axis=0)
        part = jnp.sum(own * sums + other * outer, axis=0, keepdims=True)
        blocks.append(part * (1.0 / math.sqrt(NODES)))
    eight = jnp.concatenate(blocks + blocks, axis=0)
    for n in range(OWNERS * NC // 1024):
        part_ref[n * 8 : n * 8 + 8] = eight
    copy.wait()


def last_kernel(*refs):
    inputs, (order_ref, field_hbm, first_hbm, out_ref), rest = (
        refs[:10],
        refs[10:14],
        refs[14:],
    )
    scratch, (field_in, first_in, sems) = rest[:-3], rest[-3:]
    copies = [
        pltpu.make_async_copy(field_hbm, field_in, sems.at[0]),
        pltpu.make_async_copy(first_hbm, first_in, sems.at[1]),
    ]
    for copy in copies:
        copy.start()
    current = closing_half(*inputs, *scratch)[1]
    for copy in copies:
        copy.wait()
    moved = take_lanes(first_in[...] + current, order_ref[...])
    out_ref[...] = field_in[...] + moved


def call(kernel, outs, *args, scratch=(), smem=(), far=(), near=(), copies=0, away=()):
    def stay(x):
        return pltpu.with_memory_space_constraint(x, pltpu.HBM)

    def space(n):
        if n in smem:
            return pltpu.SMEM
        return pltpu.HBM if n in far else pltpu.VMEM

    scratches = [pltpu.VMEM(s, f32) for s in scratch]
    if copies:
        scratches.append(pltpu.SemaphoreType.DMA((copies,)))
    return pl.pallas_call(
        kernel,
        out_shape=[
            pltpu.HBM(s, d) if n in away else jax.ShapeDtypeStruct(s, d)
            for n, (s, d) in enumerate(outs)
        ],
        in_specs=[pl.BlockSpec(memory_space=space(n)) for n in range(len(args))],
        out_specs=[
            pl.BlockSpec(memory_space=pltpu.HBM if n in away else pltpu.VMEM)
            for n in range(len(outs))
        ],
        scratch_shapes=scratches,
        compiler_params=pltpu.CompilerParams(vmem_limit_bytes=20 << 20),
    )(*[stay(x) if n in far + near else x for n, x in enumerate(args)])


FIELD = ((NODES, 128), f32)
SIDE_MSG = ((64, 128), f32)
GHOST_MSG = ((GHOST_ROWS, 128), f32)
SIDE_WORK = [(64, 128), (64, 128)]
SEND_WORK = [(NODES, 128), (128, 128)]


def exchange(a, b):
    count = lax.axis_size("elem")
    pairs_a, pairs_b = [], []
    for d in range(2 * count):
        base, slab = d - d % count, d % count
        pairs_a.append((d, base + (slab ^ 1)))
        other = slab + (1 if slab % 2 else -1)
        inside = 0 <= other < count
        pairs_b.append((d, base + other if inside else (d + count) % (2 * count)))
    axes = ("sess", "elem")
    b = lax.ppermute(b, axes, pairs_b)
    a = lax.ppermute(a, axes, pairs_a)
    return a, b


def one_device(
    pressure,
    load,
    stiffness,
    helm_mass,
    order_slots,
    recv_ids,
    donor_owner,
    donor_slot,
    interp_weights,
    live_count,
    coarse_basis,
    coarse_inverse,
):
    own_field = pressure.reshape(NODES, 128)
    order = order_slots.reshape(1, 128)
    owner = donor_owner.reshape(1, R_DEV)
    other_field = lax.ppermute(own_field, "sess", [(0, 1), (1, 0)])

    send, rank, owner, ids = call(
        request_kernel,
        [
            ((OWNERS * ASK, 128), f32),
            ((1, R_DEV), f32),
            ((1, R_DEV), jnp.int32),
            ((1, R_DEV), jnp.int32),
        ],
        owner,
        donor_slot,
        interp_weights.reshape(3 * NP, R_DEV),
        recv_ids,
        near=(0, 1, 2, 3),
    )
    received = lax.all_to_all(
        send.reshape(OWNERS, 1, ASK * 128), "elem", split_axis=0, concat_axis=0, tiled=True
    )
    coef, mass, static, faces, invd, inv, basis, order, ga, gb = call(
        setup_kernel,
        [
            ((3 * NODES, 128), f32),
            FIELD,
            FIELD,
            ((128, 128), f32),
            FIELD,
            ((1, 128), jnp.int32),
            ((128, NC), f32),
            ((1, 128), jnp.int32),
            GHOST_MSG,
            GHOST_MSG,
        ],
        order,
        stiffness.reshape(3 * NODES, 128),
        helm_mass.reshape(NODES, 128),
        own_field,
        load.reshape(NODES, 128),
        coarse_basis.reshape(128, NC),
        near=(0,),
        far=(1, 2, 3, 4, 5),
        scratch=[
            (3 * NODES, 128),
            (NODES, 128),
            (NODES, 128),
            (NODES, 128),
            (128, NC),
            (NODES, 128),
            (NODES, 128),
            (NODES, 128),
            (NODES, 128),
            (NODES, 128),
            (NODES, 128),
            (64, 128),
            (64, 128),
        ],
        copies=5,
    )
    answer, inv = call(
        owner_kernel,
        [((OWNERS, 128), f32), ((1, 128), jnp.int32)],
        received.reshape(OWNERS * ASK, 128),
        other_field,
        inv,
    )
    answered = lax.all_to_all(answer, "elem", split_axis=0, concat_axis=0, tiled=True)
    ga, gb = exchange(ga, gb)
    y, a, b = call(
        source_kernel,
        [FIELD, SIDE_MSG, SIDE_MSG],
        answered,
        owner,
        rank,
        ids,
        live_count,
        inv,
        static,
        invd,
        coef,
        smem=(4,),
        scratch=SEND_WORK,
    )
    a, b = exchange(a, b)
    half = [FIELD, FIELD, FIELD, FIELD, SIDE_MSG, SIDE_MSG]
    res, upd, cur, w, a, b, invd, planes = call(
        start_kernel,
        half + [FIELD, ((320, 128), f32)],
        y,
        faces,
        invd,
        a,
        b,
        ga,
        gb,
        coef,
        mass,
        scratch=SEND_WORK + SIDE_WORK,
    )
    near, shares = call(
        near_kernel,
        [((384, NC), f32), FIELD],
        basis,
        ga,
        gb,
        coarse_inverse.reshape(NC, NC),
        a,
        near=(3,),
        scratch=[(384, NC), (NODES, 128)],
        copies=2,
        away=(0, 1),
    )
    a, b = exchange(a, b)
    res, total, part, a, b = call(
        middle_kernel,
        [FIELD, FIELD, ((OWNERS * NC // 128, 128), f32), SIDE_MSG, SIDE_MSG],
        w,
        res,
        upd,
        cur,
        invd,
        a,
        b,
        planes,
        coef,
        mass,
        basis,
        ga,
        gb,
        scratch=[(NODES, 128)] * 3 + SEND_WORK + SIDE_WORK,
        copies=1,
        away=(1,),
    )
    parts = lax.all_to_all(
        part.reshape(OWNERS, NC // 128, 128),
        "elem",
        split_axis=0,
        concat_axis=0,
        tiled=True,
    )
    a, b = exchange(a, b)
    res, upd, cur, w, a, b = call(
        again_kernel,
        half,
        parts.reshape(OWNERS * NC // 128, 128),
        near,
        shares,
        res,
        a,
        b,
        invd,
        planes,
        coef,
        mass,
        far=(1, 2),
        scratch=[(NODES, 128)] + SEND_WORK + SIDE_WORK + [(NODES, 128), (384, NC)],
        copies=3,
    )
    a, b = exchange(a, b)
    (out,) = call(
        last_kernel,
        [FIELD],
        w,
        res,
        upd,
        cur,
        invd,
        a,
        b,
        planes,
        coef,
        mass,
        order,
        own_field,
        total,
        far=(11, 12),
        scratch=[(NODES, 128)] * 2 + SIDE_WORK + [(NODES, 128)] * 2,
        copies=2,
    )
    return out.reshape(1, NP, NP, NP, 128)


def solution(mesh):
    return jax.shard_map(
        one_device,
        mesh=mesh,
        in_specs=(
            P("sess", None, None, None, "elem"),
            P("sess", None, None, None, "elem"),
            P("sess", None, None, None, None, "elem"),
            P("sess", None, None, None, "elem"),
            P("sess", "elem", None),
            P("sess", "elem"),
            P("sess", "elem", None),
            P("sess", "elem"),
            P("sess", None, "elem"),
            P("sess", "elem"),
            P("sess", "elem", None),
            P("sess", None, None),
        ),
        out_specs=P("sess", None, None, None, "elem"),
        check_vma=False,
    )
```
